256 devices in a mesh: blk: 64 (over y, z, core), req: 4 (over x).
Axes of the slice: x: 4, y: 4, z: 8, core: 2. Of those that a mesh axis runs over, the one named last changes fastest.
Arguments:
- tokens_in: bfloat16 [4, 8192, 1792], P('req', 'blk'), may hold values from -6 to 6
- query_weight: bfloat16 [1792, 256], replicated, may hold values from -0.125 to 0.125
- key_weight: bfloat16 [1792, 256], replicated, may hold values from -0.125 to 0.125
- value_weight: bfloat16 [1792, 1792], replicated, may hold values from -0.125 to 0.125
- conv_weight: float32 [3, 1792], replicated, may hold values from -3 to 3
- prompt_lengths: int32 [4], P('req'), may hold values from 4096 to 8192, as said below
- decode_map: int32 [4], P('req'), may hold values from 0 to 3, each once
Outputs:
- mixed: bfloat16 [4, 8192, 1792], P('req', 'blk')
- decode_state: float32 [4, 273, 1792], P('req', None, 'blk')
- decode_norm: float32 [4, 273, 16], P('req')
The draws below stay inside these ranges and needn't reach their ends.
Inputs may be any that keep to these rules, and one draw needn't show every extreme that they name: `prompt_lengths`: some prompt has exactly 8192 live tokens. `decode_map`: each decode slot receives exactly one prompt.
All inputs are finite; a program needn't handle non-finite values.
Results may differ from the reference program's by a relative error of at most 0.0057.
Values may be sent and summed in bfloat16 or wider, within the bound.
A program may use at most 384 MiB of HBM per device.

```python
import math
import jax
import jax.numpy as jnp
from jax import lax

D = 1792
HEADS = 16
FEAT = 16
CONV = 3
HV = 112
EXPAND = 273
LEN = 8192
PROMPTS = 4


def draw_prompt_lengths(key, part):
    lengths = jax.random.randint(key, (PROMPTS,), LEN // 2, LEN + 1)
    chosen = jax.random.randint(jax.random.fold_in(key, 1), (), 0, PROMPTS)
    return jnp.where(jnp.arange(PROMPTS) == chosen, LEN, lengths).astype(jnp.int32)


def block_scale(rng, shape, split, least, largest):
    loudness, own = 1.0, jax.random.fold_in(rng, 6)
    for position, blocks in split:
        steps = jnp.exp(jax.random.uniform(jax.random.fold_in(own, position), (blocks,), jnp.float32, least / len(split), largest / len(split)))
        loudness = loudness * jnp.repeat(steps, shape[position] // blocks).reshape([-1 if axis == position else 1 for axis in range(len(shape))])
    return loudness


def centred(own_key, shape, width, most, cuts=(), kind=jnp.bfloat16):
    array = jax.random.normal(own_key, shape, jnp.float32) * width
    if len(cuts) > 0:
        array = block_scale(own_key, shape, cuts, -0.22, 0.18) * array
    return jnp.clip(array, min=-most, max=most).astype(kind)


def setup_inputs(seed: int = 0) -> dict:
    seeds = jax.random.split(jax.random.key(seed), 8)
    tokens_in = centred(seeds[0], (PROMPTS, LEN, D), 1.0, 6.0, ((0, 4), (1, 64)))
    query_weight = centred(seeds[1], (D, HEADS * FEAT), D ** -0.5, 0.125)
    key_weight = centred(seeds[2], (D, HEADS * FEAT), D ** -0.5, 0.125)
    value_weight = centred(seeds[3], (D, D), D ** -0.5, 0.125)
    conv_weight = centred(seeds[4], (CONV, D), 0.6, 3.0, (), jnp.float32)
    prompt_lengths = draw_prompt_lengths(jax.random.fold_in(seeds[7], 71), 0)
    decode_map = jax.random.permutation(seeds[6], PROMPTS).astype(jnp.int32)
    return {"tokens_in": tokens_in, "query_weight": query_weight, "key_weight": key_weight, "value_weight": value_weight, "conv_weight": conv_weight, "prompt_lengths": prompt_lengths, "decode_map": decode_map}


def features(x):
    half = x * FEAT ** (-0.25)
    outer = half[..., :, None] * half[..., None, :]
    flat = outer.reshape(outer.shape[:-2] + (FEAT * FEAT,)) * math.sqrt(0.5)
    ones = jnp.ones(x.shape[:-1] + (1,), jnp.float32)
    return jnp.concatenate([ones, half, flat], -1)

def reference(tokens_in, query_weight, key_weight, value_weight, conv_weight, prompt_lengths, decode_map):
    block = math.gcd(LEN, 512)
    count = LEN // block
    hi = lax.Precision.HIGHEST
    outs = []
    state_out = jnp.zeros((PROMPTS, EXPAND, D), jnp.float32)
    norm_out = jnp.zeros((PROMPTS, EXPAND, HEADS), jnp.float32)
    causal = jnp.arange(block)[:, None] >= jnp.arange(block)[None, :]
    for prompt in range(PROMPTS):
        inputs = tokens_in[prompt]
        queries = jnp.dot(inputs, query_weight, preferred_element_type=jnp.float32).reshape(LEN, HEADS, FEAT)
        keys = jnp.dot(inputs, key_weight, preferred_element_type=jnp.float32).reshape(LEN, HEADS, FEAT)
        values = jnp.dot(inputs, value_weight, preferred_element_type=jnp.float32).astype(jnp.bfloat16)
        padded = jnp.concatenate([jnp.zeros((CONV - 1, D), jnp.float32), values.astype(jnp.float32)], 0)
        conv = jnp.zeros((LEN, D), jnp.float32)
        for tap in range(CONV):
            conv = conv + conv_weight[tap][None, :] * padded[CONV - 1 - tap:CONV - 1 - tap + LEN]
        conv_v = conv.astype(jnp.bfloat16).astype(jnp.float32).reshape(LEN, HEADS, HV)
        live = (jnp.arange(LEN, dtype=jnp.int32) < prompt_lengths[prompt]).astype(jnp.float32)

        def step(carry, pieces):
            state, norm = carry
            qb, kb, cb, lb = pieces
            pq = features(qb)
            pk = features(kb) * lb[:, None, None]
            scores = jnp.einsum('thf,shf->hts', pq, pk, precision=hi) * causal[None]
            num = jnp.einsum('hts,shc->thc', scores, cb, precision=hi) + jnp.einsum('thf,fhc->thc', pq, state, precision=hi)
            den = lax.optimization_barrier(jnp.sum(scores, -1)).T + jnp.einsum('thf,fh->th', pq, norm, precision=hi) + (1.0 - lb)[:, None]
            result = jnp.where(lb[:, None, None] > 0, num / den[..., None], 0.0)
            state = state + jnp.einsum('thf,thc->fhc', pk, cb, precision=hi)
            norm = norm + lax.optimization_barrier(jnp.sum(pk, 0)).T
            return ((state, norm), result)
        init = (jnp.zeros((EXPAND, HEADS, HV), jnp.float32), jnp.zeros((EXPAND, HEADS), jnp.float32))
        pieces = (queries.reshape(count, block, HEADS, FEAT), keys.reshape(count, block, HEADS, FEAT), conv_v.reshape(count, block, HEADS, HV), live.reshape(count, block))
        (state, norm), results = lax.scan(step, init, pieces)
        outs.append(results.reshape(LEN, D).astype(jnp.bfloat16))
        slot = decode_map[prompt]
        state_out = state_out.at[slot].set(state.reshape(EXPAND, D))
        norm_out = norm_out.at[slot].set(norm)
    return (jnp.stack(outs, 0), state_out, norm_out)
```

```python
import math

import jax
import jax.numpy as jnp
import numpy as np
from jax import lax
from jax.experimental import pallas as pl
from jax.experimental.pallas import tpu as pltpu
from jax.sharding import PartitionSpec as P

HEADS = 16
FEAT = 16
CONV = 3
D = 1792
HV = 112
EXPAND = 273
XS, YS, ZS = 4, 4, 8
HALF = HEADS // 2
COLS = HALF * HV
TOK = 128
CHIP = 2 * TOK
HALO = 16
ROWS = 160
LANES = 128
MESH = pl.DeviceIdType.MESH
VCHUNKS = ((0, 256), (256, 256), (512, 256), (768, 128))
F32 = jnp.float32
BF16 = jnp.bfloat16


def selection():
    sel = np.zeros((280, ROWS), np.float32)
    sel[0, 152] = 1.0
    for a in range(16):
        sel[1 + a, a] = 1.0
        for b in range(16):
            row = 17 + 16 * a + b
            r = (b - a) % 16
            if r == 0:
                sel[row, 16 + a] = 1.0
            elif r < 8:
                sel[row, 16 + 16 * r + a] = math.sqrt(0.5)
            elif r > 8:
                sel[row, 16 + 16 * (16 - r) + b] = math.sqrt(0.5)
            else:
                sel[row, 144 + min(a, b)] = math.sqrt(0.5)
    return sel


def pickers():
    pick = np.zeros((HALF, HALF, LANES), np.float32)
    for i in range(HALF):
        pick[i, i, HV + 1] = 1.0
        pick[i, i, HV + 2] = 1.0
    return pick


def features(heads_t, yy, extra):
    yy[:, 0:16, :] = heads_t
    yy[:, 16:32, :] = heads_t
    parts = [heads_t, heads_t * heads_t * math.sqrt(0.5)]
    for r in range(1, 8):
        parts.append(heads_t * yy[:, r : r + 16, :])
    parts.append(heads_t[:, 0:8] * heads_t[:, 8:16])
    row = lax.broadcasted_iota(jnp.int32, (HALF, 8, CHIP), 1)
    parts.append(jnp.where(row == 0, 1.0, 0.0).astype(F32))
    phi = jnp.concatenate(parts, 1)
    if extra is not None:
        phi = phi * extra
    return phi


def kernel(
    tok, wq, wk, wv, cw, plen, dmap, sel, pick,
    mixed, dstate, dnorm,
    xs, wqk_v, wv_v, cw_v, sel_v, pick_v,
    vbuf, cvb, vp, yy, phik, phiq, ktb, numb, gsend, gat, tsend, ty, psend, pbuf,
    dt, dsend, dbuf, nsend, nbuf, obuf,
    lsem, xsend, xrecv, gs, gr, ys, yr, ps, pr, dsm, dr, ns, nr, osm, orm,
):
    x = lax.axis_index("req")
    blk = lax.axis_index("blk")
    c = blk % 2
    chip = blk // 2
    z = chip % ZS
    y = chip // ZS
    mine = (z % 2) * 4 + z // 2

    def dev(x_, y_, z_, c_):
        return ((y_ * ZS + z_) * 2 + c_, x_)

    nxt = (chip + 1) % (YS * ZS)
    prv = (chip + YS * ZS - 1) % (YS * ZS)

    def remote(src, dst, send, recv, device):
        return pltpu.make_async_remote_copy(
            src_ref=src, dst_ref=dst, send_sem=send, recv_sem=recv, device_id=device, device_id_type=MESH
        )

    half = pl.multiple_of(COLS * c, 128)
    khalf = pl.multiple_of(128 * c, 128)
    own_rows = pl.multiple_of(HALO + TOK * c, 16)
    loads = [
        pltpu.make_async_copy(wk.at[:, pl.ds(khalf, 128)], wqk_v.at[:, 0:128], lsem.at[0]),
        pltpu.make_async_copy(wq.at[:, pl.ds(khalf, 128)], wqk_v.at[:, 128:256], lsem.at[1]),
        pltpu.make_async_copy(tok, xs.at[pl.ds(own_rows, TOK)], lsem.at[2]),
        pltpu.make_async_copy(cw.at[:, pl.ds(half, COLS)], cw_v, lsem.at[3]),
    ]
    for n, (at, size) in enumerate(VCHUNKS):
        loads.append(
            pltpu.make_async_copy(
                wv.at[:, pl.ds(pl.multiple_of(half + at, 128), size)], wv_v.at[:, at : at + size], lsem.at[4 + n]
            )
        )
    loads.append(pltpu.make_async_copy(sel, sel_v, lsem.at[8]))
    loads.append(pltpu.make_async_copy(pick, pick_v, lsem.at[9]))
    for copy in loads:
        copy.start()

    pair = z - z % 2
    barrier = pltpu.get_barrier_semaphore()
    partners = []
    for cc in range(2):
        partners.append((nxt * 2 + cc, x))
        partners.append((prv * 2 + cc, x))
    for d in range(1, ZS):
        partners.append(dev(x, y, (z + d) % ZS, c))
    for d in range(1, YS):
        partners.append(dev(x, (y + d) % YS, z, c))
    me4 = (z % 2) * 2 + c
    for dx in range(XS):
        for dm in range(4):
            if dx == 0 and dm == 0:
                continue
            member = (me4 + dm) % 4
            partners.append(dev((x + dx) % XS, y, pair + member // 2, member % 2))
    for device in partners:
        pl.semaphore_signal(barrier, inc=1, device_id=device, device_id_type=MESH)
    pl.semaphore_wait(barrier, len(partners))

    to_sib = remote(tok, xs.at[pl.ds(own_rows, TOK)], xsend.at[0], xrecv.at[0], dev(x, y, z, 1 - c))
    to_sib.start()
    tail = tok.at[TOK - HALO : TOK]
    halo0 = remote(tail, xs.at[0:HALO], xsend.at[1], xrecv.at[1], (nxt * 2, x))
    halo1 = remote(tail, xs.at[0:HALO], xsend.at[2], xrecv.at[1], (nxt * 2 + 1, x))

    @pl.when(c == 1)
    def _():
        halo0.start()
        halo1.start()

    slot = dmap[0].astype(F32)
    length = plen[0]
    lane_tok = lax.broadcasted_iota(jnp.int32, (1, CHIP), 1) + chip * CHIP
    live_row = jnp.where(lane_tok < length, 1.0, 0.0).astype(F32)
    sub_tok = lax.broadcasted_iota(jnp.int32, (CHIP, 1), 0) + chip * CHIP
    live_col = jnp.where(sub_tok < length, 1.0, 0.0).astype(F32)
    lane = lax.broadcasted_iota(jnp.int32, (1, LANES), 1)

    loads[0].wait()
    loads[1].wait()
    loads[2].wait()
    other_rows = pl.multiple_of(HALO + TOK * (1 - c), 16)
    remote(tok, xs.at[pl.ds(other_rows, TOK)], xsend.at[0], xrecv.at[0], dev(x, y, z, 1 - c)).wait_recv()
    remote(tail, xs.at[0:HALO], xsend.at[1], xrecv.at[1], (prv * 2 + 1, x)).wait_recv()

    qk = jnp.dot(xs[HALO:, :], wqk_v[...], preferred_element_type=F32)
    keys_t = qk[:, 0:128].T
    ktb[...] = keys_t.astype(BF16)
    phi = features(keys_t.reshape(HALF, FEAT, CHIP) * 0.5, yy, live_row[None])
    phik[...] = phi.astype(BF16)

    loads[3].wait()
    first = (chip > 0).astype(F32)
    for n, (at, size) in enumerate(VCHUNKS):
        loads[4 + n].wait()
        val = jnp.dot(xs[...], wv_v[:, at : at + size], preferred_element_type=F32)
        vbuf[:, at : at + size] = val.astype(BF16).astype(F32)
        vbuf[0:HALO, at : at + size] = vbuf[0:HALO, at : at + size] * first
        conv = jnp.zeros((CHIP, size), F32)
        for tap in range(CONV):
            conv = conv + cw_v[tap : tap + 1, at : at + size] * vbuf[HALO - tap : HALO - tap + CHIP, at : at + size]
        cvb[:, at : at + size] = conv
    for i in range(HALF):
        tile, off = (HV * i) // 128, (HV * i) % 128
        width = 128 if off + HV <= 128 else 256
        wide = cvb[:, 128 * tile : 128 * tile + width]
        if off:
            wide = pltpu.roll(wide, width - off, 1)
        head = jnp.where(lane < HV, wide[:, 0:128], jnp.where(lane == HV, 1.0, 0.0))
        vp[i] = head.astype(BF16)

    sends = []
    for d in range(1, ZS):
        zt = (z + d) % ZS
        i = (zt % 2) * 4 + zt // 2
        gsend[i] = jnp.dot(phik[i], vp[i], preferred_element_type=F32).astype(BF16)
        copy = remote(gsend.at[i], gat.at[z], gs.at[d], gr.at[z], dev(x, y, zt, c))
        copy.start()
        sends.append(copy)
    gat[z] = jnp.dot(phik[mine], vp[mine], preferred_element_type=F32).astype(BF16)

    queries = qk[:, 128:256]
    phi_q = features((queries.T).reshape(HALF, FEAT, CHIP) * 0.5, yy, None)
    for i in range(HALF):
        phiq[i] = phi_q[i].T.astype(BF16)
    row_t = lax.broadcasted_iota(jnp.int32, (CHIP, CHIP), 0)
    col_s = lax.broadcasted_iota(jnp.int32, (CHIP, CHIP), 1)
    causal = jnp.where(row_t >= col_s, 1.0, 0.0).astype(F32) * live_row
    for i in range(HALF):
        one_head = jnp.where(lane // FEAT == i, queries, 0.0).astype(BF16)
        dots = jnp.dot(one_head, ktb[...], preferred_element_type=F32) * 0.25
        weights = (1.0 + dots + 0.5 * dots * dots) * causal
        numb[i] = jnp.dot(weights.astype(BF16), vp[i], preferred_element_type=F32)

    for d in range(1, ZS):
        zf = (z + ZS - d) % ZS
        remote(gat.at[zf], gat.at[zf], gs.at[0], gr.at[zf], dev(x, y, zf, c)).wait_recv()
    total = gat[0].astype(F32)
    for zz in range(1, ZS):
        total = total + gat[zz].astype(F32)
    tsend[...] = total.astype(BF16)
    for d in range(1, YS):
        copy = remote(tsend, ty.at[y], ys.at[d], yr.at[y], dev(x, (y + d) % YS, z, c))
        copy.start()
        sends.append(copy)
    ty[y] = total.astype(BF16)
    for d in range(1, YS):
        yf = (y + YS - d) % YS
        remote(tsend, ty.at[yf], ys.at[0], yr.at[yf], dev(x, yf, z, c)).wait_recv()
    before = jnp.zeros((ROWS, LANES), F32)
    whole = jnp.zeros((ROWS, LANES), F32)
    for yy_ in range(YS):
        piece = ty[yy_].astype(F32)
        whole = whole + piece
        before = before + piece * (yy_ < y).astype(F32)
    norm_next = pltpu.roll(whole, 1, 1)
    norm_hi = norm_next.astype(BF16).astype(F32)
    norm_lo = pltpu.roll(norm_next - norm_hi, 1, 1)
    for zz in range(ZS):
        tile = jnp.where(lane == HV + 1, norm_hi, jnp.where(lane == HV + 2, norm_lo, before))
        psend[zz] = tile.astype(BF16)
        before = before + gat[zz].astype(F32)
    for d in range(1, ZS):
        zt = (z + d) % ZS
        copy = remote(psend.at[zt], pbuf.at[mine], ps.at[d], pr.at[mine], dev(x, y, zt, c))
        copy.start()
        sends.append(copy)
    pbuf[mine] = psend[z]

    sender = (z % 2 == y % 2) & (c == y // 2)
    flagged = jnp.concatenate([whole, jnp.zeros((256 - ROWS, LANES), F32) + slot], 0)
    dt[...] = flagged.T
    for sub in range(4):
        dsend[sub] = dt[28 * sub : 28 * sub + 32, :]
    dcopies = []
    for dx in range(XS):
        for dm in range(4):
            if dx == 0 and dm == 0:
                continue
            member = (me4 + dm) % 4
            dcopies.append(
                remote(
                    dsend.at[member], dbuf.at[x], dsm.at[dx * 4 + dm], dr.at[x],
                    dev((x + dx) % XS, y, pair + member // 2, member % 2),
                )
            )

    @pl.when(sender)
    def _():
        for copy in dcopies:
            copy.start()
        dbuf[x] = dsend[me4]

    for d in range(1, ZS):
        zf = (z + ZS - d) % ZS
        i = (zf % 2) * 4 + zf // 2
        remote(pbuf.at[i], pbuf.at[i], ps.at[0], pr.at[i], dev(x, y, zf, c)).wait_recv()
    loads[8].wait()
    loads[9].wait()
    norm_t = jnp.zeros((HALF, ROWS), F32)
    for i in range(HALF):
        norm_t = norm_t + lax.dot_general(
            pick_v[i], pbuf[i], (((1,), (1,)), ((), ())), preferred_element_type=F32
        )
    nsend[0] = norm_t
    nsend[1] = jnp.zeros((HALF, ROWS), F32) + slot
    nbuf[x * 2 + c, 0] = norm_t
    nbuf[x * 2 + c, 1] = jnp.zeros((HALF, ROWS), F32) + slot
    for dx in range(XS):
        for dc in range(2):
            if dx == 0 and dc == 0:
                continue
            k = dx * 2 + dc
            copy = remote(
                nsend, nbuf.at[x * 2 + c], ns.at[k], nr.at[x * 2 + c],
                dev((x + dx) % XS, y, z, (c + dc) % 2),
            )
            copy.start()
            sends.append(copy)

    for i in range(HALF):
        num = numb[i] + jnp.dot(phiq[i], pbuf[i], preferred_element_type=F32)
        den = num[:, HV : HV + 1] + (1.0 - live_col)
        numb[i] = jnp.where(live_col > 0, num / den, 0.0)
    for j in range(7):
        left = numb[j]
        if j:
            left = pltpu.roll(left, 128 - 16 * j, 1)
        right = pltpu.roll(numb[j + 1], HV - 16 * j, 1)
        obuf[:, 128 * j : 128 * j + 128] = jnp.where(lane < HV - 16 * j, left, right).astype(BF16)
    theirs = pl.multiple_of(TOK * (1 - c), 128)
    ours = pl.multiple_of(TOK * c, 128)
    other_half = pl.multiple_of(COLS * (1 - c), 128)
    out_send = remote(
        obuf.at[pl.ds(theirs, TOK)], mixed.at[:, pl.ds(half, COLS)], osm.at[0], orm.at[0], dev(x, y, z, 1 - c)
    )
    out_send.start()
    out_own = pltpu.make_async_copy(obuf.at[pl.ds(ours, TOK)], mixed.at[:, pl.ds(half, COLS)], lsem.at[10])
    out_own.start()

    here = x.astype(F32)
    for xf in range(XS):

        @pl.when(jnp.logical_not(sender & (x == xf)))
        def _():
            remote(dsend.at[0], dbuf.at[xf], dsm.at[0], dr.at[xf], dev(x, y, z, 1 - c)).wait_recv()

    state_t = jnp.zeros((32, ROWS), F32)
    for xf in range(XS):
        got = dbuf[xf]
        state_t = state_t + jnp.where(got[:, 255:256] == here, got[:, 0:ROWS], 0.0)
    full = lax.dot_general(
        sel_v[...], state_t, (((1,), (1,)), ((), ())), precision=lax.Precision.HIGHEST, preferred_element_type=F32
    )
    dstate[...] = full[0:EXPAND, 0:28]

    for dx in range(XS):
        for dc in range(2):
            if dx == 0 and dc == 0:
                continue
            src = ((x + dx) % XS) * 2 + (c + dc) % 2
            remote(nsend, nbuf.at[src], ns.at[0], nr.at[src], dev((x + dx) % XS, y, z, (c + dc) % 2)).wait_recv()
    halves = []
    for cc in range(2):
        norm = jnp.zeros((HALF, ROWS), F32)
        for xf in range(XS):
            norm = norm + jnp.where(nbuf[xf * 2 + cc, 1] == here, nbuf[xf * 2 + cc, 0], 0.0)
        halves.append(norm)
    norms = jnp.concatenate(halves, 0)
    full = lax.dot_general(
        sel_v[...], norms, (((1,), (1,)), ((), ())), precision=lax.Precision.HIGHEST, preferred_element_type=F32
    )
    dnorm[...] = full[0:EXPAND, :]

    out_own.wait()
    out_send.wait_send()
    remote(
        obuf.at[pl.ds(theirs, TOK)], mixed.at[:, pl.ds(other_half, COLS)], osm.at[0], orm.at[0], dev(x, y, z, 1 - c)
    ).wait_recv()
    to_sib.wait_send()

    @pl.when(c == 1)
    def _():
        halo0.wait_send()
        halo1.wait_send()

    for copy in sends:
        copy.wait_send()

    @pl.when(sender)
    def _():
        for copy in dcopies:
            copy.wait_send()


def on_device(tokens_in, query_weight, key_weight, value_weight, conv_weight, prompt_lengths, decode_map):
    sel = jnp.asarray(selection())
    pick = jnp.asarray(pickers(), BF16)
    any_space = pl.BlockSpec(memory_space=pl.ANY)
    vmem = pl.BlockSpec(memory_space=pltpu.VMEM)
    smem = pl.BlockSpec(memory_space=pltpu.SMEM)
    dma = pltpu.SemaphoreType.DMA
    mixed, dstate, dnorm = pl.pallas_call(
        kernel,
        out_shape=(
            jax.ShapeDtypeStruct((TOK, D), BF16),
            jax.ShapeDtypeStruct((EXPAND, 28), F32),
            jax.ShapeDtypeStruct((EXPAND, HEADS), F32),
        ),
        in_specs=[any_space] * 5 + [smem] * 2 + [any_space] * 2,
        out_specs=(any_space, vmem, vmem),
        scratch_shapes=[
            pltpu.VMEM((HALO + CHIP, D), BF16),
            pltpu.VMEM((D, 256), BF16),
            pltpu.VMEM((D, COLS), BF16),
            pltpu.VMEM((CONV, COLS), F32),
            pltpu.VMEM((280, ROWS), F32),
            pltpu.VMEM((HALF, HALF, LANES), BF16),
            pltpu.VMEM((HALO + CHIP, COLS), F32),
            pltpu.VMEM((CHIP, COLS), F32),
            pltpu.VMEM((HALF, CHIP, LANES), BF16),
            pltpu.VMEM((HALF, 32, CHIP), F32),
            pltpu.VMEM((HALF, ROWS, CHIP), BF16),
            pltpu.VMEM((HALF, CHIP, ROWS), BF16),
            pltpu.VMEM((LANES, CHIP), BF16),
            pltpu.VMEM((HALF, CHIP, LANES), F32),
            pltpu.VMEM((HALF, ROWS, LANES), BF16),
            pltpu.VMEM((ZS, ROWS, LANES), BF16),
            pltpu.VMEM((ROWS, LANES), BF16),
            pltpu.VMEM((YS, ROWS, LANES), BF16),
            pltpu.VMEM((ZS, ROWS, LANES), BF16),
            pltpu.VMEM((HALF, ROWS, LANES), BF16),
            pltpu.VMEM((LANES, 256), F32),
            pltpu.VMEM((4, 32, 256), F32),
            pltpu.VMEM((XS, 32, 256), F32),
            pltpu.VMEM((2, HALF, ROWS), F32),
            pltpu.VMEM((2 * XS, 2, HALF, ROWS), F32),
            pltpu.VMEM((CHIP, COLS), BF16),
            dma((11,)),
            dma((3,)),
            dma((2,)),
            dma((8,)),
            dma((8,)),
            dma((4,)),
            dma((4,)),
            dma((8,)),
            dma((8,)),
            dma((16,)),
            dma((4,)),
            dma((8,)),
            dma((8,)),
            dma((1,)),
            dma((1,)),
        ],
        compiler_params=pltpu.CompilerParams(
            collective_id=0, has_side_effects=True, vmem_limit_bytes=48 * 1024 * 1024
        ),
        cost_estimate=pl.CostEstimate(flops=2_000_000_000, bytes_accessed=8_000_000, transcendentals=0),
        name="taylor_attention",
    )(
        tokens_in[0], query_weight, key_weight, value_weight, conv_weight, prompt_lengths, decode_map, sel, pick
    )
    return (mixed[None], dstate[None], dnorm[None])


def solution(mesh):
    return jax.shard_map(
        on_device,
        mesh=mesh,
        in_specs=(P("req", "blk", None), P(), P(), P(), P(), P("req"), P("req")),
        out_specs=(P("req", "blk", None), P("req", None, "blk"), P("req", None, None)),
        check_vma=False,
    )
```

```python
import math

import jax
import jax.numpy as jnp
import numpy as np
from jax import lax
from jax.experimental import pallas as pl
from jax.experimental.pallas import tpu as pltpu
from jax.sharding import PartitionSpec as P

HEADS = 16
FEAT = 16
CONV = 3
D = 1792
HV = 112
EXPAND = 273
XS, YS, ZS = 4, 4, 8
HALF = HEADS // 2
COLS = HALF * HV
TOK = 128
CHIP = 2 * TOK
HALO = 16
ROWS = 160
LANES = 128
MESH = pl.DeviceIdType.MESH
VCHUNKS = ((0, 256), (256, 256), (512, 256), (768, 128))
FAR_FIRST = (4, 3, 5, 2, 6, 1, 7)
PARTS = 2
PART = ROWS // PARTS
F32 = jnp.float32
BF16 = jnp.bfloat16


def selection():
    sel = np.zeros((384, ROWS), np.float32)
    sel[0, 152] = 1.0
    for a in range(16):
        sel[1 + a, a] = 1.0
        for b in range(16):
            row = 17 + 16 * a + b
            r = (b - a) % 16
            if r == 0:
                sel[row, 16 + a] = 1.0
            elif r < 8:
                sel[row, 16 + 16 * r + a] = math.sqrt(0.5)
            elif r > 8:
                sel[row, 16 + 16 * (16 - r) + b] = math.sqrt(0.5)
            else:
                sel[row, 144 + min(a, b)] = math.sqrt(0.5)
    return sel.T.copy()


def features(heads_t, yy, extra):
    yy[:, 0:16, :] = heads_t
    yy[:, 16:32, :] = heads_t
    parts = [heads_t, heads_t * heads_t * math.sqrt(0.5)]
    for r in range(1, 8):
        parts.append(heads_t * yy[:, r : r + 16, :])
    parts.append(heads_t[:, 0:8] * heads_t[:, 8:16])
    row = lax.broadcasted_iota(jnp.int32, (HALF, 8, CHIP), 1)
    parts.append(jnp.where(row == 0, 1.0, 0.0).astype(F32))
    phi = jnp.concatenate(parts, 1)
    if extra is not None:
        phi = phi * extra
    return phi


def kernel(
    tok, wq, wk, wv, cw, plen, dmap, sel,
    mixed, dstate, dnorm,
    xs, wqk_v, wv_v, cw_v, sel_v,
    qkb, vbuf, cvb, vp, yy, phik, phiq, ktb, numb, gsend, gat, tsend, ty, psend, pbuf,
    wholeb, dt, dsend, dbuf, drt, dfin, nsend, nxb, nzs, nzb, nss, nfull, obuf,
    lsem, xsend, xrecv, gs, gr, ys, yr, ps, pr, dsm, dr, des, der, ns, nr, nzsm, nzr, nps, npr, osm, orm,
):
    x = lax.axis_index("req")
    blk = lax.axis_index("blk")
    c = blk % 2
    chip = blk // 2
    z = chip % ZS
    y = chip // ZS

    def head_of(z_):
        return (z_ % 2) * 4 + z_ // 2

    mine = head_of(z)

    def dev(x_, y_, z_, c_):
        return ((y_ * ZS + z_) * 2 + c_, x_)

    nxt = (chip + 1) % (YS * ZS)
    prv = (chip + YS * ZS - 1) % (YS * ZS)
    sibling = dev(x, y, z, 1 - c)
    pair = z - z % 2
    lead = dev(x, y, pair + y % 2, y // 2)
    leads = (z % 2 == y % 2) & (c == y // 2)
    leads_int = leads.astype(jnp.int32)
    me4 = (z % 2) * 2 + c

    def remote(src, dst, send, recv, device):
        return pltpu.make_async_remote_copy(
            src_ref=src, dst_ref=dst, send_sem=send, recv_sem=recv, device_id=device, device_id_type=MESH
        )

    half = pl.multiple_of(COLS * c, 128)
    khalf = pl.multiple_of(128 * c, 128)
    loads = [
        pltpu.make_async_copy(tok, xs.at[0:TOK], lsem.at[0]),
        pltpu.make_async_copy(wk.at[:, pl.ds(khalf, 128)], wqk_v.at[:, 0:128], lsem.at[1]),
        pltpu.make_async_copy(wq.at[:, pl.ds(khalf, 128)], wqk_v.at[:, 128:256], lsem.at[2]),
        pltpu.make_async_copy(cw.at[:, pl.ds(half, COLS)], cw_v, lsem.at[3]),
    ]
    for n, (at, size) in enumerate(VCHUNKS):
        loads.append(
            pltpu.make_async_copy(
                wv.at[:, pl.ds(pl.multiple_of(half + at, 128), size)], wv_v.at[:, at : at + size], lsem.at[4 + n]
            )
        )
    loads.append(pltpu.make_async_copy(sel, sel_v, lsem.at[8]))
    for copy in loads:
        copy.start()

    barrier = pltpu.get_barrier_semaphore()

    def here_i_am(device):
        pl.semaphore_signal(barrier, inc=1, device_id=device, device_id_type=MESH)

    here_i_am(sibling)
    here_i_am((prv * 2 + 1, x))
    for d in FAR_FIRST:
        here_i_am(dev(x, y, (z + d) % ZS, c))
    for d in range(1, YS):
        here_i_am(dev(x, (y + d) % YS, z, c))
    for d in range(1, XS):
        here_i_am(dev((x + d) % XS, y, z, c))

    @pl.when(jnp.logical_not(leads))
    def _():
        here_i_am(lead)

    pl.semaphore_wait(barrier, 1 + (ZS - 1) + (YS - 1) + (XS - 1) + 2 * c + 3 * leads_int)

    to_sib = remote(tok, xs.at[TOK:CHIP], xsend.at[0], xrecv.at[0], sibling)
    to_sib.start()
    tail = tok.at[TOK - HALO : TOK]
    halo0 = remote(tail, xs.at[CHIP : CHIP + HALO], xsend.at[1], xrecv.at[1], (nxt * 2, x))
    halo1 = remote(tail, xs.at[CHIP : CHIP + HALO], xsend.at[2], xrecv.at[1], (nxt * 2 + 1, x))

    @pl.when(c == 1)
    def _():
        halo0.start()
        halo1.start()

    slot = dmap[0].astype(F32)
    length = plen[0]
    lane_tok = lax.broadcasted_iota(jnp.int32, (1, CHIP), 1) + chip * CHIP
    live_row = jnp.where(lane_tok < length, 1.0, 0.0).astype(F32)
    sub_tok = lax.broadcasted_iota(jnp.int32, (CHIP, 1), 0) + chip * CHIP
    live_col = jnp.where(sub_tok < length, 1.0, 0.0).astype(F32)
    lane = lax.broadcasted_iota(jnp.int32, (1, LANES), 1)

    ours = pl.multiple_of(TOK * c, TOK)
    theirs = pl.multiple_of(TOK * (1 - c), TOK)
    v_ours = pl.multiple_of(HALO + TOK * c, HALO)
    v_theirs = pl.multiple_of(HALO + TOK * (1 - c), HALO)
    for n in range(3):
        loads[n].wait()
    qkb[pl.ds(ours, TOK), :] = jnp.dot(xs[0:TOK, :], wqk_v[...], preferred_element_type=F32)
    for n, (at, size) in enumerate(VCHUNKS):
        loads[4 + n].wait()
        val = jnp.dot(xs[0:TOK, :], wv_v[:, at : at + size], preferred_element_type=F32)
        vbuf[pl.ds(v_ours, TOK), at : at + size] = val.astype(BF16).astype(F32)
    to_sib.wait_recv()
    qkb[pl.ds(theirs, TOK), :] = jnp.dot(xs[TOK:CHIP, :], wqk_v[...], preferred_element_type=F32)
    halo1.wait_recv()

    keys_t = qkb[:, 0:128].T
    ktb[...] = keys_t.astype(BF16)
    phi = features(keys_t.reshape(HALF, FEAT, CHIP) * 0.5, yy, live_row[None])
    phik[...] = phi.astype(BF16)

    loads[3].wait()
    first = (chip > 0).astype(F32)
    for n, (at, size) in enumerate(VCHUNKS):
        val = jnp.dot(xs[TOK:, :], wv_v[:, at : at + size], preferred_element_type=F32)
        val = val.astype(BF16).astype(F32)
        vbuf[pl.ds(v_theirs, TOK), at : at + size] = val[0:TOK]
        vbuf[0:HALO, at : at + size] = val[TOK:] * first
    for n, (at, size) in enumerate(VCHUNKS):
        conv = jnp.zeros((CHIP, size), F32)
        for tap in range(CONV):
            conv = conv + cw_v[tap : tap + 1, at : at + size] * vbuf[HALO - tap : HALO - tap + CHIP, at : at + size]
        cvb[:, at : at + size] = conv
    for i in range(HALF):
        tile, off = (HV * i) // 128, (HV * i) % 128
        width = 128 if off + HV <= 128 else 256
        wide = cvb[:, 128 * tile : 128 * tile + width]
        if off:
            wide = pltpu.roll(wide, width - off, 1)
        head = jnp.where(lane < HV, wide[:, 0:128], jnp.where(lane == HV, 1.0, 0.0))
        vp[i] = head.astype(BF16)

    sends = [to_sib]
    for n in range(PARTS):
        part = slice(n * PART, (n + 1) * PART)
        for d in FAR_FIRST:
            zt = (z + d) % ZS
            i = head_of(zt)
            gsend[i, part] = jnp.dot(phik[i, part], vp[i], preferred_element_type=F32).astype(BF16)
            copy = remote(gsend.at[i, part], gat.at[z, part], gs.at[n, d], gr.at[n, z], dev(x, y, zt, c))
            copy.start()
            sends.append(copy)
        gat[z, part] = jnp.dot(phik[mine, part], vp[mine], preferred_element_type=F32).astype(BF16)

    queries = qkb[:, 128:256]
    phi_q = features((queries.T).reshape(HALF, FEAT, CHIP) * 0.5, yy, None)
    for i in range(HALF):
        phiq[i] = phi_q[i].T.astype(BF16)
    row_t = lax.broadcasted_iota(jnp.int32, (CHIP, CHIP), 0)
    col_s = lax.broadcasted_iota(jnp.int32, (CHIP, CHIP), 1)
    causal = jnp.where(row_t >= col_s, 1.0, 0.0).astype(F32) * live_row
    for i in range(HALF):
        one_head = jnp.where(lane // FEAT == i, queries, 0.0).astype(BF16)
        dots = jnp.dot(one_head, ktb[...], preferred_element_type=F32) * 0.25
        weights = (1.0 + dots + 0.5 * dots * dots) * causal
        numb[i] = jnp.dot(weights.astype(BF16), vp[i], preferred_element_type=F32)

    for n in range(PARTS):
        part = slice(n * PART, (n + 1) * PART)
        for d in FAR_FIRST:
            zf = (z + ZS - d) % ZS
            remote(gat.at[zf, part], gat.at[zf, part], gs.at[n, d], gr.at[n, zf], sibling).wait_recv()
        total = gat[0, part].astype(F32)
        for zz in range(1, ZS):
            total = total + gat[zz, part].astype(F32)
        tsend[part] = total.astype(BF16)
        for d in (2, 1, 3):
            copy = remote(
                tsend.at[part], ty.at[y, part], ys.at[n, d], yr.at[n, y], dev(x, (y + d) % YS, z, c)
            )
            copy.start()
            sends.append(copy)
        ty[y, part] = total.astype(BF16)

    for n in range(PARTS):
        part = slice(n * PART, (n + 1) * PART)
        for d in (2, 1, 3):
            yf = (y + YS - d) % YS
            remote(tsend.at[part], ty.at[yf, part], ys.at[n, d], yr.at[n, yf], sibling).wait_recv()
        before = jnp.zeros((PART, LANES), F32)
        whole = jnp.zeros((PART, LANES), F32)
        for yf in range(YS):
            piece = ty[yf, part].astype(F32)
            whole = whole + piece
            before = before + piece * (yf < y).astype(F32)
        wholeb[part] = whole
        for zz in range(ZS):
            psend[zz, part] = before.astype(BF16)
            before = before + gat[zz, part].astype(F32)
        for d in FAR_FIRST:
            zt = (z + d) % ZS
            copy = remote(psend.at[zt, part], pbuf.at[mine, part], ps.at[n, d], pr.at[n, mine], dev(x, y, zt, c))
            copy.start()
            sends.append(copy)
        pbuf[mine, part] = psend[z, part]

    here = x.astype(F32)
    wholeb[ROWS:] = jnp.zeros((256 - ROWS, LANES), F32) + slot
    dt[...] = wholeb[...].T
    for sub in range(4):
        dsend[sub] = dt[28 * sub : 28 * sub + 32, :]
    nsend[...] = dt[HV : HV + 8, :]
    nxb[x] = nsend[...]
    d_copies, e_copies = [], []
    for d in range(1, XS):
        copy = remote(nsend, nxb.at[x], ns.at[d], nr.at[x], dev((x + d) % XS, y, z, c))
        copy.start()
        sends.append(copy)
        d_copies.append(remote(dsend, dbuf.at[x], dsm.at[d], dr.at[x], dev((x + d) % XS, y, z, c)))

    @pl.when(leads)
    def _():
        for copy in d_copies:
            copy.start()
        dbuf[x] = dsend[...]

    for d in range(1, XS):
        xf = (x + d) % XS
        remote(nsend, nxb.at[xf], ns.at[d], nr.at[xf], sibling).wait_recv()
    routed = jnp.zeros((8, 256), F32)
    for xf in range(XS):
        routed = routed + jnp.where(nxb[xf, :, 255:256] == here, nxb[xf], 0.0)
    nzs[...] = routed
    nzb[mine] = routed
    for d in FAR_FIRST:
        copy = remote(nzs, nzb.at[mine], nzsm.at[d], nzr.at[mine], dev(x, y, (z + d) % ZS, c))
        copy.start()
        sends.append(copy)

    for d in range(1, 4):
        member = (me4 + d) % 4
        e_copies.append(
            remote(drt.at[member], dfin, des.at[d], der.at[0], dev(x, y, pair + member // 2, member % 2))
        )

    @pl.when(leads)
    def _():
        for d in range(1, XS):
            xf = (x + d) % XS
            remote(dsend, dbuf.at[xf], dsm.at[d], dr.at[xf], sibling).wait_recv()
        state = jnp.zeros((4, 32, 256), F32)
        for xf in range(XS):
            state = state + jnp.where(dbuf[xf, :, :, 255:256] == here, dbuf[xf], 0.0)
        drt[...] = state
        for copy in e_copies:
            copy.start()
        dfin[...] = drt[me4]

    def finish(i):
        num = numb[i] + jnp.dot(phiq[i], pbuf[i], preferred_element_type=F32)
        den = num[:, HV : HV + 1] + (1.0 - live_col)
        numb[i] = num * (live_col / den)

    finish(mine)
    for d in FAR_FIRST:
        zf = (z + ZS - d) % ZS
        i = head_of(zf)
        for n in range(PARTS):
            part = slice(n * PART, (n + 1) * PART)
            remote(pbuf.at[i, part], pbuf.at[i, part], ps.at[n, d], pr.at[n, i], sibling).wait_recv()
        finish(i)

    for d in FAR_FIRST:
        i = head_of((z + ZS - d) % ZS)
        remote(nzs, nzb.at[i], nzsm.at[d], nzr.at[i], sibling).wait_recv()
    nss[...] = jnp.concatenate([nzb[i, 0:1, :] for i in range(HALF)], 0)
    nfull[c] = nss[...]
    to_sib_n = remote(nss, nfull.at[c], nps.at[0], npr.at[0], sibling)
    to_sib_n.start()
    sends.append(to_sib_n)

    for j in range(7):
        left = numb[j]
        if j:
            left = pltpu.roll(left, 128 - 16 * j, 1)
        right = pltpu.roll(numb[j + 1], HV - 16 * j, 1)
        obuf[:, 128 * j : 128 * j + 128] = jnp.where(lane < HV - 16 * j, left, right).astype(BF16)
    other_half = pl.multiple_of(COLS * (1 - c), 128)
    out_send = remote(obuf.at[pl.ds(theirs, TOK)], mixed.at[:, pl.ds(half, COLS)], osm.at[0], orm.at[0], sibling)
    out_send.start()
    sends.append(out_send)
    out_own = pltpu.make_async_copy(obuf.at[pl.ds(ours, TOK)], mixed.at[:, pl.ds(half, COLS)], lsem.at[9])
    out_own.start()

    loads[8].wait()

    @pl.when(jnp.logical_not(leads))
    def _():
        remote(dfin, dfin, des.at[0], der.at[0], sibling).wait_recv()

    full = jnp.dot(dfin[:, 0:ROWS], sel_v[...], precision=lax.Precision.HIGHEST, preferred_element_type=F32)
    dstate[...] = full[0:28, None, 0:EXPAND]
    to_sib_n.wait_recv()
    norms = nfull[...].reshape(HEADS, 256)[:, 0:ROWS]
    full = jnp.dot(norms, sel_v[...], precision=lax.Precision.HIGHEST, preferred_element_type=F32)
    dnorm[...] = full[:, 0:EXPAND]

    out_own.wait()
    remote(
        obuf.at[pl.ds(theirs, TOK)], mixed.at[:, pl.ds(other_half, COLS)], osm.at[0], orm.at[0], sibling
    ).wait_recv()
    for copy in sends:
        copy.wait_send()

    @pl.when(c == 1)
    def _():
        halo0.wait_send()
        halo1.wait_send()

    @pl.when(leads)
    def _():
        for copy in d_copies + e_copies:
            copy.wait_send()


def on_device(tokens_in, query_weight, key_weight, value_weight, conv_weight, prompt_lengths, decode_map):
    sel = jnp.asarray(selection())
    hbm = pl.BlockSpec(memory_space=pltpu.HBM)
    any_space = pl.BlockSpec(memory_space=pl.ANY)
    vmem = pl.BlockSpec(memory_space=pltpu.VMEM)
    smem = pl.BlockSpec(memory_space=pltpu.SMEM)
    dma = pltpu.SemaphoreType.DMA
    mixed, dstate, dnorm = pl.pallas_call(
        kernel,
        out_shape=(
            jax.ShapeDtypeStruct((TOK, D), BF16),
            jax.ShapeDtypeStruct((28, 1, EXPAND), F32),
            jax.ShapeDtypeStruct((HEADS, EXPAND), F32),
        ),
        in_specs=[hbm] * 5 + [smem] * 2 + [hbm],
        out_specs=(any_space, vmem, vmem),
        scratch_shapes=[
            pltpu.VMEM((CHIP + HALO, D), BF16),
            pltpu.VMEM((D, 256), BF16),
            pltpu.VMEM((D, COLS), BF16),
            pltpu.VMEM((CONV, COLS), F32),
            pltpu.VMEM((ROWS, 384), F32),
            pltpu.VMEM((CHIP, 256), F32),
            pltpu.VMEM((HALO + CHIP, COLS), F32),
            pltpu.VMEM((CHIP, COLS), F32),
            pltpu.VMEM((HALF, CHIP, LANES), BF16),
            pltpu.VMEM((HALF, 32, CHIP), F32),
            pltpu.VMEM((HALF, ROWS, CHIP), BF16),
            pltpu.VMEM((HALF, CHIP, ROWS), BF16),
            pltpu.VMEM((LANES, CHIP), BF16),
            pltpu.VMEM((HALF, CHIP, LANES), F32),
            pltpu.VMEM((HALF, ROWS, LANES), BF16),
            pltpu.VMEM((ZS, ROWS, LANES), BF16),
            pltpu.VMEM((ROWS, LANES), BF16),
            pltpu.VMEM((YS, ROWS, LANES), BF16),
            pltpu.VMEM((ZS, ROWS, LANES), BF16),
            pltpu.VMEM((HALF, ROWS, LANES), BF16),
            pltpu.VMEM((256, LANES), F32),
            pltpu.VMEM((LANES, 256), F32),
            pltpu.VMEM((4, 32, 256), F32),
            pltpu.VMEM((XS, 4, 32, 256), F32),
            pltpu.VMEM((4, 32, 256), F32),
            pltpu.VMEM((32, 256), F32),
            pltpu.VMEM((8, 256), F32),
            pltpu.VMEM((XS, 8, 256), F32),
            pltpu.VMEM((8, 256), F32),
            pltpu.VMEM((HALF, 8, 256), F32),
            pltpu.VMEM((HALF, 256), F32),
            pltpu.VMEM((2, HALF, 256), F32),
            pltpu.VMEM((CHIP, COLS), BF16),
            dma((10,)),
            dma((3,)),
            dma((2,)),
            dma((PARTS, ZS)),
            dma((PARTS, ZS)),
            dma((PARTS, YS)),
            dma((PARTS, YS)),
            dma((PARTS, ZS)),
            dma((PARTS, ZS)),
            dma((XS,)),
            dma((XS,)),
            dma((4,)),
            dma((1,)),
            dma((XS,)),
            dma((XS,)),
            dma((ZS,)),
            dma((ZS,)),
            dma((1,)),
            dma((1,)),
            dma((1,)),
            dma((1,)),
        ],
        compiler_params=pltpu.CompilerParams(
            collective_id=0, has_side_effects=True, vmem_limit_bytes=40 * 1024 * 1024
        ),
        cost_estimate=pl.CostEstimate(flops=2_000_000_000, bytes_accessed=8_000_000, transcendentals=0),
        name="taylor_attention",
    )(*[pltpu.with_memory_space_constraint(a, pltpu.HBM) for a in (tokens_in[0], query_weight, key_weight, value_weight, conv_weight)], prompt_lengths, decode_map, pltpu.with_memory_space_constraint(sel, pltpu.HBM))
    return (mixed[None], jnp.transpose(dstate, (1, 2, 0)), jnp.transpose(dnorm)[None])


def solution(mesh):
    return jax.shard_map(
        on_device,
        mesh=mesh,
        in_specs=(P("req", "blk", None), P(), P(), P(), P(), P("req"), P("req")),
        out_specs=(P("req", "blk", None), P("req", None, "blk"), P("req", None, None)),
        check_vma=False,
    )
```

```python
import math

import jax
import jax.numpy as jnp
import numpy as np
from jax import lax
from jax.experimental import pallas as pl
from jax.experimental.pallas import tpu as pltpu
from jax.sharding import PartitionSpec as P

HEADS = 16
FEAT = 16
CONV = 3
D = 1792
HV = 112
EXPAND = 273
XS, YS, ZS = 4, 4, 8
HALF = HEADS // 2
COLS = HALF * HV
TOK = 128
CHIP = 2 * TOK
HALO = 16
ROWS = 160
LANES = 128
MESH = pl.DeviceIdType.MESH
VCHUNKS = ((0, 256), (256, 256), (512, 256), (768, 128))
FAR_FIRST = (4, 3, 5, 2, 6, 1, 7)
PARTS = 2
PART = ROWS // PARTS
F32 = jnp.float32
BF16 = jnp.bfloat16


def selection():
    sel = np.zeros((384, ROWS), np.float32)
    sel[0, 152] = 1.0
    for a in range(16):
        sel[1 + a, a] = 1.0
        for b in range(16):
            row = 17 + 16 * a + b
            r = (b - a) % 16
            if r == 0:
                sel[row, 16 + a] = 1.0
            elif r < 8:
                sel[row, 16 + 16 * r + a] = math.sqrt(0.5)
            elif r > 8:
                sel[row, 16 + 16 * (16 - r) + b] = math.sqrt(0.5)
            else:
                sel[row, 144 + min(a, b)] = math.sqrt(0.5)
    return sel.T.copy()


def features(heads_t, yy, extra):
    yy[:, 0:16, :] = heads_t
    yy[:, 16:32, :] = heads_t
    parts = [heads_t, heads_t * heads_t * math.sqrt(0.5)]
    for r in range(1, 8):
        parts.append(heads_t * yy[:, r : r + 16, :])
    parts.append(heads_t[:, 0:8] * heads_t[:, 8:16])
    row = lax.broadcasted_iota(jnp.int32, (HALF, 8, CHIP), 1)
    parts.append(jnp.where(row == 0, 1.0, 0.0).astype(F32))
    phi = jnp.concatenate(parts, 1)
    if extra is not None:
        phi = phi * extra
    return phi


def kernel(
    tok, wq, wk, wv, cw, plen, dmap, sel,
    mixed, dstate, dnorm,
    xs, wqk_v, wv_v, cw_v, sel_v,
    qkb, vbuf, cvb, vp, yy, phik, phiq, ktb, numb, gsend, gat, tsend, ty, psend, pbuf,
    wholeb, dt, dbuf, drt, dfin, nsend, nxb, nzs, nzb, nss, nfull, osend, orecv,
    lsem, xsend, xrecv, gs, gr, ys, yr, ps, pr, dsm, dr, des, der, ns, nr, nzsm, nzr, nps, npr, osm, orm,
):
    x = lax.axis_index("req")
    blk = lax.axis_index("blk")
    c = blk % 2
    chip = blk // 2
    z = chip % ZS
    y = chip // ZS

    def head_of(z_):
        return (z_ % 2) * 4 + z_ // 2

    mine = head_of(z)

    def dev(x_, y_, z_, c_):
        return ((y_ * ZS + z_) * 2 + c_, x_)

    nxt = (chip + 1) % (YS * ZS)
    prv = (chip + YS * ZS - 1) % (YS * ZS)
    sibling = dev(x, y, z, 1 - c)
    pair = z - z % 2
    lead = dev(x, y, pair + y % 2, y // 2)
    leads = (z % 2 == y % 2) & (c == y // 2)
    leads_int = leads.astype(jnp.int32)
    me4 = (z % 2) * 2 + c

    def remote(src, dst, send, recv, device):
        return pltpu.make_async_remote_copy(
            src_ref=src, dst_ref=dst, send_sem=send, recv_sem=recv, device_id=device, device_id_type=MESH
        )

    half = pl.multiple_of(COLS * c, 128)
    khalf = pl.multiple_of(128 * c, 128)
    loads = [
        pltpu.make_async_copy(tok, xs.at[0:TOK], lsem.at[0]),
        pltpu.make_async_copy(wk.at[:, pl.ds(khalf, 128)], wqk_v.at[:, 0:128], lsem.at[1]),
        pltpu.make_async_copy(wq.at[:, pl.ds(khalf, 128)], wqk_v.at[:, 128:256], lsem.at[2]),
        pltpu.make_async_copy(cw.at[:, pl.ds(half, COLS)], cw_v, lsem.at[3]),
    ]
    for n, (at, size) in enumerate(VCHUNKS):
        loads.append(
            pltpu.make_async_copy(
                wv.at[:, pl.ds(pl.multiple_of(half + at, 128), size)], wv_v.at[:, at : at + size], lsem.at[4 + n]
            )
        )
    loads.append(pltpu.make_async_copy(sel, sel_v, lsem.at[8]))
    for copy in loads:
        copy.start()

    barrier = pltpu.get_barrier_semaphore()

    def here_i_am(device):
        pl.semaphore_signal(barrier, inc=1, device_id=device, device_id_type=MESH)

    here_i_am(sibling)
    here_i_am((prv * 2 + 1, x))
    for d in FAR_FIRST:
        here_i_am(dev(x, y, (z + d) % ZS, c))
    for d in range(1, YS):
        here_i_am(dev(x, (y + d) % YS, z, c))
    for d in range(1, XS):
        here_i_am(dev((x + d) % XS, y, z, c))

    @pl.when(jnp.logical_not(leads))
    def _():
        here_i_am(lead)

    pl.semaphore_wait(barrier, 1 + (ZS - 1) + (YS - 1) + (XS - 1) + 2 * c + 3 * leads_int)

    to_sib = remote(tok, xs.at[TOK:CHIP], xsend.at[0], xrecv.at[0], sibling)
    to_sib.start()
    tail = tok.at[TOK - HALO : TOK]
    halo0 = remote(tail, xs.at[CHIP : CHIP + HALO], xsend.at[1], xrecv.at[1], (nxt * 2, x))
    halo1 = remote(tail, xs.at[CHIP : CHIP + HALO], xsend.at[2], xrecv.at[1], (nxt * 2 + 1, x))

    @pl.when(c == 1)
    def _():
        halo0.start()
        halo1.start()

    slot = dmap[0].astype(F32)
    length = plen[0]
    lane_tok = lax.broadcasted_iota(jnp.int32, (1, CHIP), 1) + chip * CHIP
    live_row = jnp.where(lane_tok < length, 1.0, 0.0).astype(F32)
    sub_tok = lax.broadcasted_iota(jnp.int32, (CHIP, 1), 0) + chip * CHIP
    live_col = jnp.where(sub_tok < length, 1.0, 0.0).astype(F32)
    lane = lax.broadcasted_iota(jnp.int32, (1, LANES), 1)

    ours = pl.multiple_of(TOK * c, TOK)
    theirs = pl.multiple_of(TOK * (1 - c), TOK)
    v_ours = pl.multiple_of(HALO + TOK * c, HALO)
    v_theirs = pl.multiple_of(HALO + TOK * (1 - c), HALO)
    for n in range(3):
        loads[n].wait()
    qkb[pl.ds(ours, TOK), :] = jnp.dot(xs[0:TOK, :], wqk_v[...], preferred_element_type=F32)
    for n, (at, size) in enumerate(VCHUNKS):
        loads[4 + n].wait()
        val = jnp.dot(xs[0:TOK, :], wv_v[:, at : at + size], preferred_element_type=F32)
        vbuf[pl.ds(v_ours, TOK), at : at + size] = val.astype(BF16).astype(F32)
    to_sib.wait_recv()
    qkb[pl.ds(theirs, TOK), :] = jnp.dot(xs[TOK:CHIP, :], wqk_v[...], preferred_element_type=F32)
    halo1.wait_recv()

    keys_t = qkb[:, 0:128].T
    ktb[...] = keys_t.astype(BF16)
    phi = features(keys_t.reshape(HALF, FEAT, CHIP) * 0.5, yy, live_row[None])
    phik[...] = phi.astype(BF16)

    loads[3].wait()
    first = (chip > 0).astype(F32)
    for n, (at, size) in enumerate(VCHUNKS):
        val = jnp.dot(xs[TOK:, :], wv_v[:, at : at + size], preferred_element_type=F32)
        val = val.astype(BF16).astype(F32)
        vbuf[pl.ds(v_theirs, TOK), at : at + size] = val[0:TOK]
        vbuf[0:HALO, at : at + size] = val[TOK:] * first
    for n, (at, size) in enumerate(VCHUNKS):
        conv = jnp.zeros((CHIP, size), F32)
        for tap in range(CONV):
            conv = conv + cw_v[tap : tap + 1, at : at + size] * vbuf[HALO - tap : HALO - tap + CHIP, at : at + size]
        cvb[:, at : at + size] = conv
    for i in range(HALF):
        tile, off = (HV * i) // 128, (HV * i) % 128
        width = 128 if off + HV <= 128 else 256
        wide = cvb[:, 128 * tile : 128 * tile + width]
        if off:
            wide = pltpu.roll(wide, width - off, 1)
        head = jnp.where(lane < HV, wide[:, 0:128], jnp.where(lane == HV, 1.0, 0.0))
        vp[i] = head.astype(BF16)

    sends = [to_sib]
    for n in range(PARTS):
        part = slice(n * PART, (n + 1) * PART)
        for d in FAR_FIRST:
            zt = (z + d) % ZS
            i = head_of(zt)
            gsend[i, part] = jnp.dot(phik[i, part], vp[i], preferred_element_type=F32).astype(BF16)
            copy = remote(gsend.at[i, part], gat.at[z, part], gs.at[n, d], gr.at[n, z], dev(x, y, zt, c))
            copy.start()
            sends.append(copy)
        gat[z, part] = jnp.dot(phik[mine, part], vp[mine], preferred_element_type=F32).astype(BF16)

    queries = qkb[:, 128:256]
    phi_q = features((queries.T).reshape(HALF, FEAT, CHIP) * 0.5, yy, None)
    for i in range(HALF):
        for n in range(PARTS):
            phiq[n, i] = phi_q[i, n * PART : (n + 1) * PART].T.astype(BF16)
    row_t = lax.broadcasted_iota(jnp.int32, (CHIP, CHIP), 0)
    col_s = lax.broadcasted_iota(jnp.int32, (CHIP, CHIP), 1)
    causal = jnp.where(row_t >= col_s, 1.0, 0.0).astype(F32) * live_row
    for i in range(HALF):
        one_head = jnp.where(lane // FEAT == i, queries, 0.0).astype(BF16)
        dots = jnp.dot(one_head, ktb[...], preferred_element_type=F32) * 0.25
        weights = (1.0 + dots + 0.5 * dots * dots) * causal
        numb[i] = jnp.dot(weights.astype(BF16), vp[i], preferred_element_type=F32)

    for n in range(PARTS):
        part = slice(n * PART, (n + 1) * PART)
        for d in FAR_FIRST:
            zf = (z + ZS - d) % ZS
            remote(gat.at[zf, part], gat.at[zf, part], gs.at[n, d], gr.at[n, zf], sibling).wait_recv()
        total = gat[0, part].astype(F32)
        for zz in range(1, ZS):
            total = total + gat[zz, part].astype(F32)
        tsend[part] = total.astype(BF16)
        for d in (2, 1, 3):
            copy = remote(
                tsend.at[part], ty.at[y, part], ys.at[n, d], yr.at[n, y], dev(x, (y + d) % YS, z, c)
            )
            copy.start()
            sends.append(copy)
        ty[y, part] = total.astype(BF16)

    for n in range(PARTS):
        part = slice(n * PART, (n + 1) * PART)
        for d in (2, 1, 3):
            yf = (y + YS - d) % YS
            remote(tsend.at[part], ty.at[yf, part], ys.at[n, d], yr.at[n, yf], sibling).wait_recv()
        before = jnp.zeros((PART, LANES), F32)
        whole = jnp.zeros((PART, LANES), F32)
        for yf in range(YS):
            piece = ty[yf, part].astype(F32)
            whole = whole + piece
            before = before + piece * (yf < y).astype(F32)
        wholeb[part] = jnp.where(lane == LANES - 1, slot, whole)
        for zz in range(ZS):
            psend[zz, part] = before.astype(BF16)
            before = before + gat[zz, part].astype(F32)
        for d in FAR_FIRST:
            zt = (z + d) % ZS
            copy = remote(psend.at[zt, part], pbuf.at[mine, part], ps.at[n, d], pr.at[n, mine], dev(x, y, zt, c))
            copy.start()
            sends.append(copy)
        pbuf[mine, part] = psend[z, part]

    here = x.astype(F32)
    d_copies, e_copies = [], []
    for d in (2, 1, 3):
        d_copies.append(remote(wholeb, dbuf.at[x], dsm.at[d], dr.at[x], dev((x + d) % XS, y, z, c)))

    @pl.when(leads)
    def _():
        for copy in d_copies:
            copy.start()
        dbuf[x] = wholeb[...]

    row8 = lax.broadcasted_iota(jnp.int32, (8, LANES), 0)
    pick = jnp.where((lane == HV) & (row8 == 0) | (lane == LANES - 1) & (row8 == 1), 1.0, 0.0)
    nsend[...] = lax.dot_general(
        pick, wholeb[...], (((1,), (1,)), ((), ())), precision=lax.Precision.HIGHEST, preferred_element_type=F32
    )
    nxb[x] = nsend[...]
    for d in (2, 1, 3):
        copy = remote(nsend, nxb.at[x], ns.at[d], nr.at[x], dev((x + d) % XS, y, z, c))
        copy.start()
        sends.append(copy)
    for d in range(1, XS):
        xf = (x + d) % XS
        remote(nsend, nxb.at[xf], ns.at[d], nr.at[xf], sibling).wait_recv()
    routed = jnp.zeros((1, ROWS), F32)
    for xf in range(XS):
        routed = routed + jnp.where(nxb[xf, 1:2] == here, nxb[xf, 0:1], 0.0)
    nzs[0] = routed
    nzb[mine] = routed
    for d in FAR_FIRST:
        copy = remote(nzs.at[0], nzb.at[mine], nzsm.at[d], nzr.at[mine], dev(x, y, (z + d) % ZS, c))
        copy.start()
        sends.append(copy)

    for n in range(PARTS - 1):
        part = slice(n * PART, (n + 1) * PART)
        numb[mine] = numb[mine] + jnp.dot(phiq[n, mine], pbuf[mine, part], preferred_element_type=F32)
        for d in FAR_FIRST:
            i = head_of((z + ZS - d) % ZS)
            remote(pbuf.at[i, part], pbuf.at[i, part], ps.at[n, d], pr.at[n, i], sibling).wait_recv()
            numb[i] = numb[i] + jnp.dot(phiq[n, i], pbuf[i, part], preferred_element_type=F32)

    for d in range(1, 4):
        member = (me4 + d) % 4
        e_copies.append(
            remote(drt.at[member], dfin, des.at[d], der.at[0], dev(x, y, pair + member // 2, member % 2))
        )

    @pl.when(leads)
    def _():
        for d in range(1, XS):
            xf = (x + d) % XS
            remote(wholeb, dbuf.at[xf], dsm.at[d], dr.at[xf], sibling).wait_recv()
        state = jnp.zeros((ROWS, LANES), F32)
        for xf in range(XS):
            state = state + jnp.where(dbuf[xf, :, LANES - 1 :] == here, dbuf[xf], 0.0)
        dt[...] = jnp.concatenate([state, jnp.zeros((256 - ROWS, LANES), F32)], 0).T
        for sub in range(4):
            drt[sub] = dt[28 * sub : 28 * sub + 32, :]
        for copy in e_copies:
            copy.start()
        dfin[...] = drt[me4]

    last = slice((PARTS - 1) * PART, ROWS)

    def finish(k, i):
        num = numb[i] + jnp.dot(phiq[PARTS - 1, i], pbuf[i, last], preferred_element_type=F32)
        den = num[:, HV : HV + 1] + (1.0 - live_col)
        numb[i] = num * (live_col / den)
        osend[i] = numb[i, pl.ds(theirs, TOK), :].astype(BF16)
        copy = remote(osend.at[i], orecv.at[i], osm.at[k], orm.at[i], sibling)
        copy.start()
        sends.append(copy)

    finish(0, mine)
    for d in FAR_FIRST:
        i = head_of((z + ZS - d) % ZS)
        remote(pbuf.at[i, last], pbuf.at[i, last], ps.at[PARTS - 1, d], pr.at[PARTS - 1, i], sibling).wait_recv()
        finish(d, i)

    for d in FAR_FIRST:
        i = head_of((z + ZS - d) % ZS)
        remote(nzs.at[0], nzb.at[i], nzsm.at[d], nzr.at[i], sibling).wait_recv()
    nss[...] = jnp.concatenate([nzb[i] for i in range(HALF)], 0)
    nfull[c] = nss[...]
    to_sib_n = remote(nss, nfull.at[c], nps.at[0], npr.at[0], sibling)
    to_sib_n.start()
    sends.append(to_sib_n)

    def side_by_side(get, at):
        for j in range(7):
            left = get(j)
            if j:
                left = pltpu.roll(left, 128 - 16 * j, 1)
            right = pltpu.roll(get(j + 1), HV - 16 * j, 1)
            tile = jnp.where(lane < HV - 16 * j, left, right).astype(BF16)
            mixed[:, pl.ds(pl.multiple_of(at + 128 * j, 128), 128)] = tile

    side_by_side(lambda i: numb[i, pl.ds(ours, TOK), :], half)

    loads[8].wait()

    @pl.when(jnp.logical_not(leads))
    def _():
        remote(dfin, dfin, des.at[0], der.at[0], sibling).wait_recv()

    full = jnp.dot(dfin[:, 0:ROWS], sel_v[...], precision=lax.Precision.HIGHEST, preferred_element_type=F32)
    dstate[...] = full[0:28, None, 0:EXPAND]
    to_sib_n.wait_recv()
    norms = nfull[...].reshape(HEADS, ROWS)
    full = jnp.dot(norms, sel_v[...], precision=lax.Precision.HIGHEST, preferred_element_type=F32)
    dnorm[...] = full[:, 0:EXPAND]

    for i in range(HALF):
        remote(osend.at[i], orecv.at[i], osm.at[0], orm.at[i], sibling).wait_recv()
    side_by_side(lambda i: orecv[i].astype(F32), pl.multiple_of(COLS * (1 - c), 128))

    for copy in sends:
        copy.wait_send()

    @pl.when(c == 1)
    def _():
        halo0.wait_send()
        halo1.wait_send()

    @pl.when(leads)
    def _():
        for copy in d_copies + e_copies:
            copy.wait_send()


def on_device(tokens_in, query_weight, key_weight, value_weight, conv_weight, prompt_lengths, decode_map):
    sel = jnp.asarray(selection())
    hbm = pl.BlockSpec(memory_space=pltpu.HBM)
    vmem = pl.BlockSpec(memory_space=pltpu.VMEM)
    smem = pl.BlockSpec(memory_space=pltpu.SMEM)
    dma = pltpu.SemaphoreType.DMA
    mixed, dstate, dnorm = pl.pallas_call(
        kernel,
        out_shape=(
            jax.ShapeDtypeStruct((TOK, D), BF16),
            jax.ShapeDtypeStruct((28, 1, EXPAND), F32),
            jax.ShapeDtypeStruct((HEADS, EXPAND), F32),
        ),
        in_specs=[hbm] * 5 + [smem] * 2 + [hbm],
        out_specs=(vmem, vmem, vmem),
        scratch_shapes=[
            pltpu.VMEM((CHIP + HALO, D), BF16),
            pltpu.VMEM((D, 256), BF16),
            pltpu.VMEM((D, COLS), BF16),
            pltpu.VMEM((CONV, COLS), F32),
            pltpu.VMEM((ROWS, 384), F32),
            pltpu.VMEM((CHIP, 256), F32),
            pltpu.VMEM((HALO + CHIP, COLS), F32),
            pltpu.VMEM((CHIP, COLS), F32),
            pltpu.VMEM((HALF, CHIP, LANES), BF16),
            pltpu.VMEM((HALF, 32, CHIP), F32),
            pltpu.VMEM((HALF, ROWS, CHIP), BF16),
            pltpu.VMEM((PARTS, HALF, CHIP, PART), BF16),
            pltpu.VMEM((LANES, CHIP), BF16),
            pltpu.VMEM((HALF, CHIP, LANES), F32),
            pltpu.VMEM((HALF, ROWS, LANES), BF16),
            pltpu.VMEM((ZS, ROWS, LANES), BF16),
            pltpu.VMEM((ROWS, LANES), BF16),
            pltpu.VMEM((YS, ROWS, LANES), BF16),
            pltpu.VMEM((ZS, ROWS, LANES), BF16),
            pltpu.VMEM((HALF, ROWS, LANES), BF16),
            pltpu.VMEM((ROWS, LANES), F32),
            pltpu.VMEM((LANES, 256), F32),
            pltpu.VMEM((XS, ROWS, LANES), F32),
            pltpu.VMEM((4, 32, 256), F32),
            pltpu.VMEM((32, 256), F32),
            pltpu.VMEM((8, ROWS), F32),
            pltpu.VMEM((XS, 8, ROWS), F32),
            pltpu.VMEM((1, 1, ROWS), F32),
            pltpu.VMEM((HALF, 1, ROWS), F32),
            pltpu.VMEM((HALF, ROWS), F32),
            pltpu.VMEM((2, HALF, ROWS), F32),
            pltpu.VMEM((HALF, TOK, LANES), BF16),
            pltpu.VMEM((HALF, TOK, LANES), BF16),
            dma((10,)),
            dma((3,)),
            dma((2,)),
            dma((PARTS, ZS)),
            dma((PARTS, ZS)),
            dma((PARTS, YS)),
            dma((PARTS, YS)),
            dma((PARTS, ZS)),
            dma((PARTS, ZS)),
            dma((XS,)),
            dma((XS,)),
            dma((4,)),
            dma((1,)),
            dma((XS,)),
            dma((XS,)),
            dma((ZS,)),
            dma((ZS,)),
            dma((1,)),
            dma((1,)),
            dma((8,)),
            dma((8,)),
        ],
        compiler_params=pltpu.CompilerParams(
            collective_id=0, has_side_effects=True, vmem_limit_bytes=40 * 1024 * 1024
        ),
        cost_estimate=pl.CostEstimate(flops=2_000_000_000, bytes_accessed=8_000_000, transcendentals=0),
        name="taylor_attention",
    )(*[pltpu.with_memory_space_constraint(a, pltpu.HBM) for a in (tokens_in[0], query_weight, key_weight, value_weight, conv_weight)], prompt_lengths, decode_map, pltpu.with_memory_space_constraint(sel, pltpu.HBM))
    return (mixed[None], jnp.transpose(dstate, (1, 2, 0)), jnp.transpose(dnorm)[None])


def solution(mesh):
    return jax.shard_map(
        on_device,
        mesh=mesh,
        in_specs=(P("req", "blk", None), P(), P(), P(), P(), P("req"), P("req")),
        out_specs=(P("req", "blk", None), P("req", None, "blk"), P("req", None, None)),
        check_vma=False,
    )
```

```python
import math

import jax
import jax.numpy as jnp
import numpy as np
from jax import lax
from jax.experimental import pallas as pl
from jax.experimental.pallas import tpu as pltpu
from jax.sharding import PartitionSpec as P

HEADS = 16
FEAT = 16
CONV = 3
D = 1792
HV = 112
EXPAND = 273
XS, YS, ZS = 4, 4, 8
HALF = HEADS // 2
COLS = HALF * HV
TOK = 128
CHIP = 2 * TOK
HALO = 16
ROWS = 160
LANES = 128
MESH = pl.DeviceIdType.MESH
VCHUNKS = ((0, 256), (256, 256), (512, 256), (768, 128))
FAR_FIRST = (4, 3, 5, 2, 6, 1, 7)
PARTS = 2
PART = ROWS // PARTS
F32 = jnp.float32
BF16 = jnp.bfloat16


def selection():
    sel = np.zeros((384, ROWS), np.float32)
    sel[0, 152] = 1.0
    for a in range(16):
        sel[1 + a, a] = 1.0
        for b in range(16):
            row = 17 + 16 * a + b
            r = (b - a) % 16
            if r == 0:
                sel[row, 16 + a] = 1.0
            elif r < 8:
                sel[row, 16 + 16 * r + a] = math.sqrt(0.5)
            elif r > 8:
                sel[row, 16 + 16 * (16 - r) + b] = math.sqrt(0.5)
            else:
                sel[row, 144 + min(a, b)] = math.sqrt(0.5)
    return sel.T.copy()


def features(heads_t, yy, extra):
    yy[:, 0:16, :] = heads_t
    yy[:, 16:32, :] = heads_t
    parts = [heads_t, heads_t * heads_t * math.sqrt(0.5)]
    for r in range(1, 8):
        parts.append(heads_t * yy[:, r : r + 16, :])
    parts.append(heads_t[:, 0:8] * heads_t[:, 8:16])
    row = lax.broadcasted_iota(jnp.int32, (HALF, 8, CHIP), 1)
    parts.append(jnp.where(row == 0, 1.0, 0.0).astype(F32))
    phi = jnp.concatenate(parts, 1)
    if extra is not None:
        phi = phi * extra
    return phi


def kernel(
    tok, wq, wk, wv, cw, plen, dmap, sel,
    mixed, dstate, dnorm,
    xs, wqk_v, wv_v, cw_v, sel_v,
    qkb, vbuf, cvb, vp, yy, phik, phiq, ktb, numb, gsend, gat, tsend, ty, psend, pbuf,
    wholeb, dt, dbuf, drt, dfin, nys, nyb, nxs, nxb, nzs, nzr_b, nzo, nzb, nss, nfull, osend, orecv,
    lsem, xsend, xrecv, gs, gr, ys, yr, ps, pr, dsm, dr, des, der,
    nysm, nyr, nxsm, nxr, nzsm, nzr, nbs, nbr, nps, npr, osm, orm,
):
    x = lax.axis_index("req")
    blk = lax.axis_index("blk")
    c = blk % 2
    chip = blk // 2
    z = chip % ZS
    y = chip // ZS

    def head_of(z_):
        return (z_ % 2) * 4 + z_ // 2

    mine = head_of(z)

    def dev(x_, y_, z_, c_):
        return ((y_ * ZS + z_) * 2 + c_, x_)

    nxt = (chip + 1) % (YS * ZS)
    prv = (chip + YS * ZS - 1) % (YS * ZS)
    sibling = dev(x, y, z, 1 - c)
    pair = z - z % 2
    lead = dev(x, y, pair + y % 2, y // 2)
    leads = (z % 2 == y % 2) & (c == y // 2)
    leads_int = leads.astype(jnp.int32)
    me4 = (z % 2) * 2 + c

    def remote(src, dst, send, recv, device):
        return pltpu.make_async_remote_copy(
            src_ref=src, dst_ref=dst, send_sem=send, recv_sem=recv, device_id=device, device_id_type=MESH
        )

    half = pl.multiple_of(COLS * c, 128)
    khalf = pl.multiple_of(128 * c, 128)
    loads = [
        pltpu.make_async_copy(tok, xs.at[0:TOK], lsem.at[0]),
        pltpu.make_async_copy(wk.at[:, pl.ds(khalf, 128)], wqk_v.at[:, 0:128], lsem.at[1]),
        pltpu.make_async_copy(wq.at[:, pl.ds(khalf, 128)], wqk_v.at[:, 128:256], lsem.at[2]),
        pltpu.make_async_copy(cw.at[:, pl.ds(half, COLS)], cw_v, lsem.at[3]),
    ]
    for n, (at, size) in enumerate(VCHUNKS):
        loads.append(
            pltpu.make_async_copy(
                wv.at[:, pl.ds(pl.multiple_of(half + at, 128), size)], wv_v.at[:, at : at + size], lsem.at[4 + n]
            )
        )
    loads.append(pltpu.make_async_copy(sel, sel_v, lsem.at[8]))
    for copy in loads:
        copy.start()

    barrier = pltpu.get_barrier_semaphore()

    def here_i_am(device):
        pl.semaphore_signal(barrier, inc=1, device_id=device, device_id_type=MESH)

    here_i_am(sibling)

    @pl.when(chip > 0)
    def _():
        here_i_am((prv * 2 + 1, x))

    for d in FAR_FIRST:
        here_i_am(dev(x, y, (z + d) % ZS, c))
    for d in range(1, YS):
        here_i_am(dev(x, (y + d) % YS, z, c))
    for d in range(1, XS):
        here_i_am(dev((x + d) % XS, y, z, c))

    @pl.when(jnp.logical_not(leads))
    def _():
        here_i_am(lead)

    last_not = (chip < YS * ZS - 1).astype(jnp.int32)
    pl.semaphore_wait(barrier, 1 + (ZS - 1) + (YS - 1) + (XS - 1) + 2 * c * last_not + 3 * leads_int)

    to_sib = remote(tok, xs.at[TOK:CHIP], xsend.at[0], xrecv.at[0], sibling)
    tail = tok.at[TOK - HALO : TOK]
    halo0 = remote(tail, xs.at[CHIP : CHIP + HALO], xsend.at[1], xrecv.at[1], (nxt * 2, x))
    halo1 = remote(tail, xs.at[CHIP : CHIP + HALO], xsend.at[2], xrecv.at[1], (nxt * 2 + 1, x))

    sends_halo = (c == 1) & (chip < YS * ZS - 1)

    @pl.when(sends_halo)
    def _():
        halo0.start()
        halo1.start()

    to_sib.start()

    @pl.when(chip == 0)
    def _():
        xs[CHIP:, :] = jnp.zeros((HALO, D), BF16)

    slot = dmap[0].astype(F32)
    length = plen[0]
    lane_tok = lax.broadcasted_iota(jnp.int32, (1, CHIP), 1) + chip * CHIP
    live_row = jnp.where(lane_tok < length, 1.0, 0.0).astype(F32)
    sub_tok = lax.broadcasted_iota(jnp.int32, (CHIP, 1), 0) + chip * CHIP
    live_col = jnp.where(sub_tok < length, 1.0, 0.0).astype(F32)
    lane = lax.broadcasted_iota(jnp.int32, (1, LANES), 1)

    ours = pl.multiple_of(TOK * c, TOK)
    theirs = pl.multiple_of(TOK * (1 - c), TOK)
    v_ours = pl.multiple_of(HALO + TOK * c, HALO)
    v_theirs = pl.multiple_of(HALO + TOK * (1 - c), HALO)
    for n in range(3):
        loads[n].wait()
    qkb[pl.ds(ours, TOK), :] = jnp.dot(xs[0:TOK, :], wqk_v[...], preferred_element_type=F32)
    for n, (at, size) in enumerate(VCHUNKS):
        loads[4 + n].wait()
        val = jnp.dot(xs[0:TOK, :], wv_v[:, at : at + size], preferred_element_type=F32)
        vbuf[pl.ds(v_ours, TOK), at : at + size] = val.astype(BF16).astype(F32)
    to_sib.wait_recv()
    qkb[pl.ds(theirs, TOK), :] = jnp.dot(xs[TOK:CHIP, :], wqk_v[...], preferred_element_type=F32)

    @pl.when(chip > 0)
    def _():
        halo1.wait_recv()


    keys_t = qkb[:, 0:128].T
    ktb[...] = keys_t.astype(BF16)
    phi = features(keys_t.reshape(HALF, FEAT, CHIP) * 0.5, yy, live_row[None])
    phik[...] = phi.astype(BF16)

    loads[3].wait()
    for n, (at, size) in enumerate(VCHUNKS):
        val = jnp.dot(xs[TOK:, :], wv_v[:, at : at + size], preferred_element_type=F32)
        val = val.astype(BF16).astype(F32)
        vbuf[pl.ds(v_theirs, TOK), at : at + size] = val[0:TOK]
        vbuf[0:HALO, at : at + size] = val[TOK:]
    for n, (at, size) in enumerate(VCHUNKS):
        conv = jnp.zeros((CHIP, size), F32)
        for tap in range(CONV):
            conv = conv + cw_v[tap : tap + 1, at : at + size] * vbuf[HALO - tap : HALO - tap + CHIP, at : at + size]
        cvb[:, at : at + size] = conv
    for i in range(HALF):
        tile, off = (HV * i) // 128, (HV * i) % 128
        width = 128 if off + HV <= 128 else 256
        wide = cvb[:, 128 * tile : 128 * tile + width]
        if off:
            wide = pltpu.roll(wide, width - off, 1)
        head = jnp.where(lane < HV, wide[:, 0:128], jnp.where(lane == HV, 1.0, 0.0))
        vp[i] = head.astype(BF16)

    sends = [to_sib]
    for n in range(PARTS):
        part = slice(n * PART, (n + 1) * PART)
        for d in FAR_FIRST:
            zt = (z + d) % ZS
            i = head_of(zt)
            gsend[i, part] = jnp.dot(phik[i, part], vp[i], preferred_element_type=F32).astype(BF16)
            copy = remote(gsend.at[i, part], gat.at[z, part], gs.at[n, d], gr.at[n, z], dev(x, y, zt, c))
            copy.start()
            sends.append(copy)
        gat[z, part] = jnp.dot(phik[mine, part], vp[mine], preferred_element_type=F32).astype(BF16)

    here = x.astype(F32)
    wide = lax.broadcasted_iota(jnp.int32, (1, 256), 1)
    row8 = lax.broadcasted_iota(jnp.int32, (HALF, 1), 0)
    ones = jnp.ones((HALF, CHIP), BF16)
    sums = jnp.zeros((HALF, ROWS), F32)
    for i in range(HALF):
        head_sum = lax.dot_general(ones, phik[i], (((1,), (1,)), ((), ())), preferred_element_type=F32)
        sums = jnp.where(row8 == i, head_sum, sums)
    nys[...] = sums
    nyb[y] = sums
    for d in (2, 1, 3):
        copy = remote(nys, nyb.at[y], nysm.at[d], nyr.at[y], dev(x, (y + d) % YS, z, c))
        copy.start()
        sends.append(copy)

    queries = qkb[:, 128:256]
    phi_q = features((queries.T).reshape(HALF, FEAT, CHIP) * 0.5, yy, None)
    for i in range(HALF):
        for n in range(PARTS):
            phiq[n, i] = phi_q[i, n * PART : (n + 1) * PART].T.astype(BF16)
    row_t = lax.broadcasted_iota(jnp.int32, (CHIP, CHIP), 0)
    col_s = lax.broadcasted_iota(jnp.int32, (CHIP, CHIP), 1)
    causal = jnp.where(row_t >= col_s, 1.0, 0.0).astype(F32) * live_row
    for i in range(HALF):
        one_head = jnp.where(lane // FEAT == i, queries, 0.0).astype(BF16)
        dots = jnp.dot(one_head, ktb[...], preferred_element_type=F32) * 0.25
        weights = (1.0 + dots + 0.5 * dots * dots) * causal
        numb[i] = jnp.dot(weights.astype(BF16), vp[i], preferred_element_type=F32)

    for d in range(1, YS):
        yf = (y + d) % YS
        remote(nys, nyb.at[yf], nysm.at[d], nyr.at[yf], sibling).wait_recv()
    nxs[:, 0:ROWS] = nyb[0] + nyb[1] + nyb[2] + nyb[3]
    nxs[:, ROWS:] = jnp.zeros((HALF, 256 - ROWS), F32) + slot
    nxb[x] = nxs[...]
    for d in (2, 1, 3):
        copy = remote(nxs, nxb.at[x], nxsm.at[d], nxr.at[x], dev((x + d) % XS, y, z, c))
        copy.start()
        sends.append(copy)

    for n in range(PARTS):
        part = slice(n * PART, (n + 1) * PART)
        for d in FAR_FIRST:
            zf = (z + ZS - d) % ZS
            remote(gat.at[zf, part], gat.at[zf, part], gs.at[n, d], gr.at[n, zf], sibling).wait_recv()
        total = gat[0, part].astype(F32)
        for zz in range(1, ZS):
            total = total + gat[zz, part].astype(F32)
        tsend[part] = total.astype(BF16)
        for d in (2, 1, 3):
            copy = remote(
                tsend.at[part], ty.at[y, part], ys.at[n, d], yr.at[n, y], dev(x, (y + d) % YS, z, c)
            )
            copy.start()
            sends.append(copy)
        ty[y, part] = total.astype(BF16)

    for d in range(1, XS):
        xf = (x + d) % XS
        remote(nxs, nxb.at[xf], nxsm.at[d], nxr.at[xf], sibling).wait_recv()
    routed = jnp.zeros((HALF, 256), F32)
    for xf in range(XS):
        routed = routed + jnp.where(nxb[xf, :, 255:256] == here, nxb[xf], 0.0)
    for i in range(HALF):
        nzs[i] = routed[i : i + 1]
    for d in FAR_FIRST:
        zt = (z + d) % ZS
        copy = remote(nzs.at[head_of(zt)], nzr_b.at[z], nzsm.at[d], nzr.at[z], dev(x, y, zt, c))
        copy.start()
        sends.append(copy)
    nzr_b[z] = nzs[mine]

    d_copies, e_copies = [], []
    for n in range(PARTS):
        part = slice(n * PART, (n + 1) * PART)
        for d in (2, 1, 3):
            yf = (y + YS - d) % YS
            remote(tsend.at[part], ty.at[yf, part], ys.at[n, d], yr.at[n, yf], sibling).wait_recv()
        before = jnp.zeros((PART, LANES), F32)
        whole = jnp.zeros((PART, LANES), F32)
        for yf in range(YS):
            piece = ty[yf, part].astype(F32)
            whole = whole + piece
            before = before + piece * (yf < y).astype(F32)
        wholeb[part] = jnp.where(lane == LANES - 1, slot, whole)
        for zz in range(ZS):
            psend[zz, part] = before.astype(BF16)
            before = before + gat[zz, part].astype(F32)
        d_part = [
            remote(wholeb.at[part], dbuf.at[x, part], dsm.at[n, d], dr.at[n, x], dev((x + d) % XS, y, z, c))
            for d in (2, 1, 3)
        ]

        @pl.when(leads)
        def _():
            for copy in d_part:
                copy.start()
            dbuf[x, part] = wholeb[part]

        d_copies += d_part
        for d in FAR_FIRST:
            zt = (z + d) % ZS
            copy = remote(psend.at[zt, part], pbuf.at[mine, part], ps.at[n, d], pr.at[n, mine], dev(x, y, zt, c))
            copy.start()
            sends.append(copy)
        pbuf[mine, part] = psend[z, part]

    for d in FAR_FIRST:
        zf = (z + ZS - d) % ZS
        remote(nzs.at[0], nzr_b.at[zf], nzsm.at[d], nzr.at[zf], sibling).wait_recv()
    whole_norm = nzr_b[0]
    for zz in range(1, ZS):
        whole_norm = whole_norm + nzr_b[zz]
    nzo[0] = whole_norm
    nzb[mine] = whole_norm
    for d in FAR_FIRST:
        copy = remote(nzo.at[0], nzb.at[mine], nbs.at[d], nbr.at[mine], dev(x, y, (z + d) % ZS, c))
        copy.start()
        sends.append(copy)

    for n in range(PARTS - 1):
        part = slice(n * PART, (n + 1) * PART)
        numb[mine] = numb[mine] + jnp.dot(phiq[n, mine], pbuf[mine, part], preferred_element_type=F32)
        for d in FAR_FIRST:
            i = head_of((z + ZS - d) % ZS)
            remote(pbuf.at[i, part], pbuf.at[i, part], ps.at[n, d], pr.at[n, i], sibling).wait_recv()
            numb[i] = numb[i] + jnp.dot(phiq[n, i], pbuf[i, part], preferred_element_type=F32)

    for d in range(1, 4):
        member = (me4 + d) % 4
        e_copies.append(
            remote(drt.at[member], dfin, des.at[d], der.at[0], dev(x, y, pair + member // 2, member % 2))
        )

    @pl.when(leads)
    def _():
        for n in range(PARTS):
            part = slice(n * PART, (n + 1) * PART)
            for d in range(1, XS):
                xf = (x + d) % XS
                remote(wholeb.at[part], dbuf.at[xf, part], dsm.at[n, d], dr.at[n, xf], sibling).wait_recv()
        state = jnp.zeros((ROWS, LANES), F32)
        for xf in range(XS):
            state = state + jnp.where(dbuf[xf, :, LANES - 1 :] == here, dbuf[xf], 0.0)
        dt[...] = jnp.concatenate([state, jnp.zeros((256 - ROWS, LANES), F32)], 0).T
        for sub in range(4):
            drt[sub] = dt[28 * sub : 28 * sub + 32, :]
        for copy in e_copies:
            copy.start()
        dfin[...] = drt[me4]

    last = slice((PARTS - 1) * PART, ROWS)

    for d in FAR_FIRST:
        i = head_of((z + ZS - d) % ZS)
        remote(nzo.at[0], nzb.at[i], nbs.at[d], nbr.at[i], sibling).wait_recv()
    nss[...] = jnp.concatenate([nzb[i, :, 0:ROWS] for i in range(HALF)], 0)
    nfull[c] = nss[...]
    to_sib_n = remote(nss, nfull.at[c], nps.at[0], npr.at[0], sibling)
    to_sib_n.start()
    sends.append(to_sib_n)

    for d in FAR_FIRST:
        i = head_of((z + ZS - d) % ZS)
        remote(pbuf.at[i, last], pbuf.at[i, last], ps.at[PARTS - 1, d], pr.at[PARTS - 1, i], sibling).wait_recv()
    for i in range(HALF):
        num = numb[i] + jnp.dot(phiq[PARTS - 1, i], pbuf[i, last], preferred_element_type=F32)
        den = num[:, HV : HV + 1] + (1.0 - live_col)
        numb[i] = num * (live_col / den)
        osend[i] = numb[i, pl.ds(theirs, TOK), :].astype(BF16)
    out_send = remote(osend, orecv, osm.at[0], orm.at[0], sibling)
    out_send.start()
    sends.append(out_send)

    def side_by_side(get, at):
        for j in range(7):
            left = get(j)
            if j:
                left = pltpu.roll(left, 128 - 16 * j, 1)
            right = pltpu.roll(get(j + 1), HV - 16 * j, 1)
            tile = jnp.where(lane < HV - 16 * j, left, right).astype(BF16)
            mixed[:, pl.ds(pl.multiple_of(at + 128 * j, 128), 128)] = tile

    side_by_side(lambda i: numb[i, pl.ds(ours, TOK), :], half)

    loads[8].wait()

    @pl.when(jnp.logical_not(leads))
    def _():
        remote(dfin, dfin, des.at[0], der.at[0], sibling).wait_recv()

    full = jnp.dot(dfin[:, 0:ROWS], sel_v[...], precision=lax.Precision.HIGHEST, preferred_element_type=F32)
    dstate[...] = full[0:28, None, 0:EXPAND]
    to_sib_n.wait_recv()
    norms = nfull[...].reshape(HEADS, ROWS)
    full = jnp.dot(norms, sel_v[...], precision=lax.Precision.HIGHEST, preferred_element_type=F32)
    dnorm[...] = full[:, 0:EXPAND]

    out_send.wait_recv()
    side_by_side(lambda i: orecv[i].astype(F32), pl.multiple_of(COLS * (1 - c), 128))

    for copy in sends:
        copy.wait_send()

    @pl.when(sends_halo)
    def _():
        halo0.wait_send()
        halo1.wait_send()

    @pl.when(leads)
    def _():
        for copy in d_copies + e_copies:
            copy.wait_send()


def on_device(tokens_in, query_weight, key_weight, value_weight, conv_weight, prompt_lengths, decode_map):
    sel = jnp.asarray(selection())
    hbm = pl.BlockSpec(memory_space=pltpu.HBM)
    vmem = pl.BlockSpec(memory_space=pltpu.VMEM)
    smem = pl.BlockSpec(memory_space=pltpu.SMEM)
    dma = pltpu.SemaphoreType.DMA
    mixed, dstate, dnorm = pl.pallas_call(
        kernel,
        out_shape=(
            jax.ShapeDtypeStruct((TOK, D), BF16),
            jax.ShapeDtypeStruct((28, 1, EXPAND), F32),
            jax.ShapeDtypeStruct((HEADS, EXPAND), F32),
        ),
        in_specs=[hbm] * 5 + [smem] * 2 + [hbm],
        out_specs=(vmem, vmem, vmem),
        scratch_shapes=[
            pltpu.VMEM((CHIP + HALO, D), BF16),
            pltpu.VMEM((D, 256), BF16),
            pltpu.VMEM((D, COLS), BF16),
            pltpu.VMEM((CONV, COLS), F32),
            pltpu.VMEM((ROWS, 384), F32),
            pltpu.VMEM((CHIP, 256), F32),
            pltpu.VMEM((HALO + CHIP, COLS), F32),
            pltpu.VMEM((CHIP, COLS), F32),
            pltpu.VMEM((HALF, CHIP, LANES), BF16),
            pltpu.VMEM((HALF, 32, CHIP), F32),
            pltpu.VMEM((HALF, ROWS, CHIP), BF16),
            pltpu.VMEM((PARTS, HALF, CHIP, PART), BF16),
            pltpu.VMEM((LANES, CHIP), BF16),
            pltpu.VMEM((HALF, CHIP, LANES), F32),
            pltpu.VMEM((HALF, ROWS, LANES), BF16),
            pltpu.VMEM((ZS, ROWS, LANES), BF16),
            pltpu.VMEM((ROWS, LANES), BF16),
            pltpu.VMEM((YS, ROWS, LANES), BF16),
            pltpu.VMEM((ZS, ROWS, LANES), BF16),
            pltpu.VMEM((HALF, ROWS, LANES), BF16),
            pltpu.VMEM((ROWS, LANES), F32),
            pltpu.VMEM((LANES, 256), F32),
            pltpu.VMEM((XS, ROWS, LANES), F32),
            pltpu.VMEM((4, 32, 256), F32),
            pltpu.VMEM((32, 256), F32),
            pltpu.VMEM((HALF, ROWS), F32),
            pltpu.VMEM((YS, HALF, ROWS), F32),
            pltpu.VMEM((HALF, 256), F32),
            pltpu.VMEM((XS, HALF, 256), F32),
            pltpu.VMEM((HALF, 1, 256), F32),
            pltpu.VMEM((ZS, 1, 256), F32),
            pltpu.VMEM((1, 1, 256), F32),
            pltpu.VMEM((HALF, 1, 256), F32),
            pltpu.VMEM((HALF, ROWS), F32),
            pltpu.VMEM((2, HALF, ROWS), F32),
            pltpu.VMEM((HALF, TOK, LANES), BF16),
            pltpu.VMEM((HALF, TOK, LANES), BF16),
            dma((9,)),
            dma((3,)),
            dma((2,)),
            dma((PARTS, ZS)),
            dma((PARTS, ZS)),
            dma((PARTS, YS)),
            dma((PARTS, YS)),
            dma((PARTS, ZS)),
            dma((PARTS, ZS)),
            dma((PARTS, XS)),
            dma((PARTS, XS)),
            dma((4,)),
            dma((1,)),
            dma((YS,)),
            dma((YS,)),
            dma((XS,)),
            dma((XS,)),
            dma((ZS,)),
            dma((ZS,)),
            dma((ZS,)),
            dma((ZS,)),
            dma((1,)),
            dma((1,)),
            dma((1,)),
            dma((1,)),
        ],
        compiler_params=pltpu.CompilerParams(
            collective_id=0, has_side_effects=True, vmem_limit_bytes=40 * 1024 * 1024
        ),
        cost_estimate=pl.CostEstimate(flops=2_000_000_000, bytes_accessed=8_000_000, transcendentals=0),
        name="taylor_attention",
    )(*[pltpu.with_memory_space_constraint(a, pltpu.HBM) for a in (tokens_in[0], query_weight, key_weight, value_weight, conv_weight)], prompt_lengths, decode_map, pltpu.with_memory_space_constraint(sel, pltpu.HBM))
    return (mixed[None], jnp.transpose(dstate, (1, 2, 0)), jnp.transpose(dnorm)[None])


def solution(mesh):
    return jax.shard_map(
        on_device,
        mesh=mesh,
        in_specs=(P("req", "blk", None), P(), P(), P(), P(), P("req"), P("req")),
        out_specs=(P("req", "blk", None), P("req", None, "blk"), P("req", None, None)),
        check_vma=False,
    )
```

```python
import math

import jax
import jax.numpy as jnp
import numpy as np
from jax import lax
from jax.experimental import pallas as pl
from jax.experimental.pallas import tpu as pltpu
from jax.sharding import PartitionSpec as P

HEADS = 16
FEAT = 16
CONV = 3
D = 1792
HV = 112
EXPAND = 273
XS, YS, ZS = 4, 4, 8
HALF = HEADS // 2
COLS = HALF * HV
TOK = 128
CHIP = 2 * TOK
HALO = 8
ROWS = 160
LANES = 128
MESH = pl.DeviceIdType.MESH
VCHUNKS = ((0, 256), (256, 256), (512, 256), (768, 128))
FAR_FIRST = (4, 3, 5, 2, 6, 1, 7)
PARTS = 2
PART = ROWS // PARTS
F32 = jnp.float32
BF16 = jnp.bfloat16


def selection():
    sel = np.zeros((384, ROWS), np.float32)
    sel[0, 152] = 1.0
    for a in range(16):
        sel[1 + a, a] = 1.0
        for b in range(16):
            row = 17 + 16 * a + b
            r = (b - a) % 16
            if r == 0:
                sel[row, 16 + a] = 1.0
            elif r < 8:
                sel[row, 16 + 16 * r + a] = math.sqrt(0.5)
            elif r > 8:
                sel[row, 16 + 16 * (16 - r) + b] = math.sqrt(0.5)
            else:
                sel[row, 144 + min(a, b)] = math.sqrt(0.5)
    return sel.T.copy()


def features(heads_t, yy, extra):
    yy[:, 0:16, :] = heads_t
    yy[:, 16:32, :] = heads_t
    parts = [heads_t, heads_t * heads_t * math.sqrt(0.5)]
    for r in range(1, 8):
        parts.append(heads_t * yy[:, r : r + 16, :])
    parts.append(heads_t[:, 0:8] * heads_t[:, 8:16])
    row = lax.broadcasted_iota(jnp.int32, (HALF, 8, CHIP), 1)
    parts.append(jnp.where(row == 0, 1.0, 0.0).astype(F32))
    phi = jnp.concatenate(parts, 1)
    if extra is not None:
        phi = phi * extra
    return phi


def kernel(
    tok, wq, wk, wv, cw, plen, dmap, sel,
    mixed, dstate, dnorm,
    xs, wqk_v, wv_v, cw_v, sel_v,
    qkb, vbuf, cvb, vp, yy, phik, phiq, ktb, numb, gsend, gat, tsend, ty, psend, pbuf,
    wholeb, dt, dbuf, drt, dfin, nys, nyb, nxs, nxb, nzs, nzr_b, nzo, nzb, nss, nfull, osend, orecv,
    lsem, xsend, xrecv, gs, gr, ys, yr, ps, pr, dsm, dr, des, der,
    nysm, nyr, nxsm, nxr, nzsm, nzr, nbs, nbr, nps, npr, osm, orm,
):
    x = lax.axis_index("req")
    blk = lax.axis_index("blk")
    c = blk % 2
    chip = blk // 2
    z = chip % ZS
    y = chip // ZS

    def head_of(z_):
        return (z_ % 2) * 4 + z_ // 2

    mine = head_of(z)

    def dev(x_, y_, z_, c_):
        return ((y_ * ZS + z_) * 2 + c_, x_)

    nxt = (chip + 1) % (YS * ZS)
    prv = (chip + YS * ZS - 1) % (YS * ZS)
    sibling = dev(x, y, z, 1 - c)
    pair = z - z % 2
    lead = dev(x, y, pair + y % 2, y // 2)
    leads = (z % 2 == y % 2) & (c == y // 2)
    leads_int = leads.astype(jnp.int32)
    me4 = (z % 2) * 2 + c

    def remote(src, dst, send, recv, device):
        return pltpu.make_async_remote_copy(
            src_ref=src, dst_ref=dst, send_sem=send, recv_sem=recv, device_id=device, device_id_type=MESH
        )

    half = pl.multiple_of(COLS * c, 128)
    khalf = pl.multiple_of(128 * c, 128)
    loads = [
        pltpu.make_async_copy(tok, xs.at[0:TOK], lsem.at[0]),
        pltpu.make_async_copy(wk.at[:, pl.ds(khalf, 128)], wqk_v.at[:, 0:128], lsem.at[1]),
        pltpu.make_async_copy(wq.at[:, pl.ds(khalf, 128)], wqk_v.at[:, 128:256], lsem.at[2]),
        pltpu.make_async_copy(cw.at[:, pl.ds(half, COLS)], cw_v, lsem.at[3]),
    ]
    for n, (at, size) in enumerate(VCHUNKS):
        loads.append(
            pltpu.make_async_copy(
                wv.at[:, pl.ds(pl.multiple_of(half + at, 128), size)], wv_v.at[:, at : at + size], lsem.at[4 + n]
            )
        )
    loads.append(pltpu.make_async_copy(sel, sel_v, lsem.at[8]))
    for copy in loads:
        copy.start()

    barrier = pltpu.get_barrier_semaphore()

    def here_i_am(device):
        pl.semaphore_signal(barrier, inc=1, device_id=device, device_id_type=MESH)

    here_i_am(sibling)

    @pl.when(chip > 0)
    def _():
        here_i_am((prv * 2 + 1, x))

    for d in FAR_FIRST:
        here_i_am(dev(x, y, (z + d) % ZS, c))
    for d in range(1, YS):
        here_i_am(dev(x, (y + d) % YS, z, c))
    for d in range(1, XS):
        here_i_am(dev((x + d) % XS, y, z, c))

    @pl.when(jnp.logical_not(leads))
    def _():
        here_i_am(lead)

    last_not = (chip < YS * ZS - 1).astype(jnp.int32)
    pl.semaphore_wait(barrier, 1 + (ZS - 1) + (YS - 1) + (XS - 1) + 2 * c * last_not + 3 * leads_int)

    to_sib = remote(tok, xs.at[TOK:CHIP], xsend.at[0], xrecv.at[0], sibling)
    tail = tok.at[TOK - HALO : TOK]
    halo0 = remote(tail, xs.at[CHIP : CHIP + HALO], xsend.at[1], xrecv.at[1], (nxt * 2, x))
    halo1 = remote(tail, xs.at[CHIP : CHIP + HALO], xsend.at[2], xrecv.at[1], (nxt * 2 + 1, x))

    sends_halo = (c == 1) & (chip < YS * ZS - 1)

    @pl.when(sends_halo)
    def _():
        halo0.start()
        halo1.start()

    to_sib.start()

    @pl.when(chip == 0)
    def _():
        xs[CHIP:, :] = jnp.zeros((HALO, D), BF16)

    slot = dmap[0].astype(F32)
    length = plen[0]
    lane_tok = lax.broadcasted_iota(jnp.int32, (1, CHIP), 1) + chip * CHIP
    live_row = jnp.where(lane_tok < length, 1.0, 0.0).astype(F32)
    sub_tok = lax.broadcasted_iota(jnp.int32, (CHIP, 1), 0) + chip * CHIP
    live_col = jnp.where(sub_tok < length, 1.0, 0.0).astype(F32)
    lane = lax.broadcasted_iota(jnp.int32, (1, LANES), 1)

    ours = pl.multiple_of(TOK * c, TOK)
    theirs = pl.multiple_of(TOK * (1 - c), TOK)
    v_ours = pl.multiple_of(HALO + TOK * c, HALO)
    v_theirs = pl.multiple_of(HALO + TOK * (1 - c), HALO)
    for n in range(3):
        loads[n].wait()
    qkb[pl.ds(ours, TOK), :] = jnp.dot(xs[0:TOK, :], wqk_v[...], preferred_element_type=F32)
    for n, (at, size) in enumerate(VCHUNKS):
        loads[4 + n].wait()
        val = jnp.dot(xs[0:TOK, :], wv_v[:, at : at + size], preferred_element_type=F32)
        vbuf[pl.ds(v_ours, TOK), at : at + size] = val.astype(BF16).astype(F32)
    to_sib.wait_recv()
    qkb[pl.ds(theirs, TOK), :] = jnp.dot(xs[TOK:CHIP, :], wqk_v[...], preferred_element_type=F32)

    keys_t = qkb[:, 0:128].T
    ktb[...] = keys_t.astype(BF16)
    phi = features(keys_t.reshape(HALF, FEAT, CHIP) * 0.5, yy, live_row[None])
    phik[...] = phi.astype(BF16)

    @pl.when(chip > 0)
    def _():
        halo1.wait_recv()

    loads[3].wait()
    for n, (at, size) in enumerate(VCHUNKS):
        val = jnp.dot(xs[TOK:, :], wv_v[:, at : at + size], preferred_element_type=F32)
        val = val.astype(BF16).astype(F32)
        vbuf[pl.ds(v_theirs, TOK), at : at + size] = val[0:TOK]
        vbuf[0:HALO, at : at + size] = val[TOK:]
    for n, (at, size) in enumerate(VCHUNKS):
        conv = jnp.zeros((CHIP, size), F32)
        for tap in range(CONV):
            conv = conv + cw_v[tap : tap + 1, at : at + size] * vbuf[HALO - tap : HALO - tap + CHIP, at : at + size]
        cvb[:, at : at + size] = conv
    for i in range(HALF):
        tile, off = (HV * i) // 128, (HV * i) % 128
        width = 128 if off + HV <= 128 else 256
        wide = cvb[:, 128 * tile : 128 * tile + width]
        if off:
            wide = pltpu.roll(wide, width - off, 1)
        head = jnp.where(lane < HV, wide[:, 0:128], jnp.where(lane == HV, 1.0, 0.0))
        vp[i] = head.astype(BF16)

    sends = [to_sib]
    for n in range(PARTS):
        part = slice(n * PART, (n + 1) * PART)
        for d in FAR_FIRST:
            zt = (z + d) % ZS
            i = head_of(zt)
            gsend[i, part] = jnp.dot(phik[i, part], vp[i], preferred_element_type=F32).astype(BF16)
            copy = remote(gsend.at[i, part], gat.at[z, part], gs.at[n, d], gr.at[n, z], dev(x, y, zt, c))
            copy.start()
            sends.append(copy)
        gat[z, part] = jnp.dot(phik[mine, part], vp[mine], preferred_element_type=F32).astype(BF16)

    here = x.astype(F32)
    wide = lax.broadcasted_iota(jnp.int32, (1, 256), 1)
    row8 = lax.broadcasted_iota(jnp.int32, (HALF, 1), 0)
    ones = jnp.ones((HALF, CHIP), BF16)
    sums = jnp.zeros((HALF, ROWS), F32)
    for i in range(HALF):
        head_sum = lax.dot_general(ones, phik[i], (((1,), (1,)), ((), ())), preferred_element_type=F32)
        sums = jnp.where(row8 == i, head_sum, sums)
    nys[...] = sums
    nyb[y] = sums
    for d in (2, 1, 3):
        copy = remote(nys, nyb.at[y], nysm.at[d], nyr.at[y], dev(x, (y + d) % YS, z, c))
        copy.start()
        sends.append(copy)

    queries = qkb[:, 128:256]
    phi_q = features((queries.T).reshape(HALF, FEAT, CHIP) * 0.5, yy, None)
    for i in range(HALF):
        for n in range(PARTS):
            phiq[n, i] = phi_q[i, n * PART : (n + 1) * PART].T.astype(BF16)
    row_t = lax.broadcasted_iota(jnp.int32, (CHIP, CHIP), 0)
    col_s = lax.broadcasted_iota(jnp.int32, (CHIP, CHIP), 1)
    causal = jnp.where(row_t >= col_s, 1.0, 0.0).astype(F32) * live_row
    for i in range(HALF):
        one_head = jnp.where(lane // FEAT == i, queries, 0.0).astype(BF16)
        dots = jnp.dot(one_head, ktb[...], preferred_element_type=F32) * 0.25
        weights = (1.0 + dots + 0.5 * dots * dots) * causal
        numb[i] = jnp.dot(weights.astype(BF16), vp[i], preferred_element_type=F32)

    for d in range(1, YS):
        yf = (y + d) % YS
        remote(nys, nyb.at[yf], nysm.at[d], nyr.at[yf], sibling).wait_recv()
    nxs[:, 0:ROWS] = nyb[0] + nyb[1] + nyb[2] + nyb[3]
    nxs[:, ROWS:] = jnp.zeros((HALF, 256 - ROWS), F32) + slot
    nxb[x] = nxs[...]
    for d in (2, 1, 3):
        copy = remote(nxs, nxb.at[x], nxsm.at[d], nxr.at[x], dev((x + d) % XS, y, z, c))
        copy.start()
        sends.append(copy)

    for n in range(PARTS):
        part = slice(n * PART, (n + 1) * PART)
        for d in FAR_FIRST:
            zf = (z + ZS - d) % ZS
            remote(gat.at[zf, part], gat.at[zf, part], gs.at[n, d], gr.at[n, zf], sibling).wait_recv()
        total = gat[0, part].astype(F32)
        for zz in range(1, ZS):
            total = total + gat[zz, part].astype(F32)
        tsend[part] = total.astype(BF16)
        for d in (2, 1, 3):
            copy = remote(
                tsend.at[part], ty.at[y, part], ys.at[n, d], yr.at[n, y], dev(x, (y + d) % YS, z, c)
            )
            copy.start()
            sends.append(copy)
        ty[y, part] = total.astype(BF16)

    for d in range(1, XS):
        xf = (x + d) % XS
        remote(nxs, nxb.at[xf], nxsm.at[d], nxr.at[xf], sibling).wait_recv()
    routed = jnp.zeros((HALF, 256), F32)
    for xf in range(XS):
        routed = routed + jnp.where(nxb[xf, :, 255:256] == here, nxb[xf], 0.0)
    for i in range(HALF):
        nzs[i] = routed[i : i + 1]
    for d in FAR_FIRST:
        zt = (z + d) % ZS
        copy = remote(nzs.at[head_of(zt)], nzr_b.at[z], nzsm.at[d], nzr.at[z], dev(x, y, zt, c))
        copy.start()
        sends.append(copy)
    nzr_b[z] = nzs[mine]

    d_copies, e_copies = [], []
    for n in range(PARTS):
        part = slice(n * PART, (n + 1) * PART)
        for d in (2, 1, 3):
            yf = (y + YS - d) % YS
            remote(tsend.at[part], ty.at[yf, part], ys.at[n, d], yr.at[n, yf], sibling).wait_recv()
        before = jnp.zeros((PART, LANES), F32)
        whole = jnp.zeros((PART, LANES), F32)
        for yf in range(YS):
            piece = ty[yf, part].astype(F32)
            whole = whole + piece
            before = before + piece * (yf < y).astype(F32)
        wholeb[part] = jnp.where(lane == LANES - 1, slot, whole)
        for zz in range(ZS):
            psend[zz, part] = before.astype(BF16)
            before = before + gat[zz, part].astype(F32)
        d_part = [
            remote(wholeb.at[part], dbuf.at[x, part], dsm.at[n, d], dr.at[n, x], dev((x + d) % XS, y, z, c))
            for d in (2, 1, 3)
        ]

        @pl.when(leads)
        def _():
            for copy in d_part:
                copy.start()
            dbuf[x, part] = wholeb[part]

        d_copies += d_part
        for d in FAR_FIRST:
            zt = (z + d) % ZS
            copy = remote(psend.at[zt, part], pbuf.at[mine, part], ps.at[n, d], pr.at[n, mine], dev(x, y, zt, c))
            copy.start()
            sends.append(copy)
        pbuf[mine, part] = psend[z, part]

    for d in FAR_FIRST:
        zf = (z + ZS - d) % ZS
        remote(nzs.at[0], nzr_b.at[zf], nzsm.at[d], nzr.at[zf], sibling).wait_recv()
    whole_norm = nzr_b[0]
    for zz in range(1, ZS):
        whole_norm = whole_norm + nzr_b[zz]
    nzo[0] = whole_norm
    nzb[mine] = whole_norm
    for d in FAR_FIRST:
        copy = remote(nzo.at[0], nzb.at[mine], nbs.at[d], nbr.at[mine], dev(x, y, (z + d) % ZS, c))
        copy.start()
        sends.append(copy)

    for n in range(PARTS - 1):
        part = slice(n * PART, (n + 1) * PART)
        numb[mine] = numb[mine] + jnp.dot(phiq[n, mine], pbuf[mine, part], preferred_element_type=F32)
        for d in FAR_FIRST:
            i = head_of((z + ZS - d) % ZS)
            remote(pbuf.at[i, part], pbuf.at[i, part], ps.at[n, d], pr.at[n, i], sibling).wait_recv()
            numb[i] = numb[i] + jnp.dot(phiq[n, i], pbuf[i, part], preferred_element_type=F32)

    for d in range(1, 4):
        member = (me4 + d) % 4
        e_copies.append(
            remote(drt.at[member], dfin, des.at[d], der.at[0], dev(x, y, pair + member // 2, member % 2))
        )

    @pl.when(leads)
    def _():
        for n in range(PARTS):
            part = slice(n * PART, (n + 1) * PART)
            for d in range(1, XS):
                xf = (x + d) % XS
                remote(wholeb.at[part], dbuf.at[xf, part], dsm.at[n, d], dr.at[n, xf], sibling).wait_recv()
        state = jnp.zeros((ROWS, LANES), F32)
        for xf in range(XS):
            state = state + jnp.where(dbuf[xf, :, LANES - 1 :] == here, dbuf[xf], 0.0)
        dt[...] = jnp.concatenate([state, jnp.zeros((256 - ROWS, LANES), F32)], 0).T
        for sub in range(4):
            drt[sub] = dt[28 * sub : 28 * sub + 32, :]
        for copy in e_copies:
            copy.start()
        dfin[...] = drt[me4]

    last = slice((PARTS - 1) * PART, ROWS)

    for d in FAR_FIRST:
        i = head_of((z + ZS - d) % ZS)
        remote(nzo.at[0], nzb.at[i], nbs.at[d], nbr.at[i], sibling).wait_recv()
    nss[...] = jnp.concatenate([nzb[i, :, 0:ROWS] for i in range(HALF)], 0)
    nfull[c] = nss[...]
    to_sib_n = remote(nss, nfull.at[c], nps.at[0], npr.at[0], sibling)
    to_sib_n.start()
    sends.append(to_sib_n)

    for d in FAR_FIRST:
        i = head_of((z + ZS - d) % ZS)
        remote(pbuf.at[i, last], pbuf.at[i, last], ps.at[PARTS - 1, d], pr.at[PARTS - 1, i], sibling).wait_recv()
    for i in range(HALF):
        num = numb[i] + jnp.dot(phiq[PARTS - 1, i], pbuf[i, last], preferred_element_type=F32)
        den = num[:, HV : HV + 1] + (1.0 - live_col)
        numb[i] = num * (live_col / den)
        osend[i] = numb[i, pl.ds(theirs, TOK), :].astype(BF16)
    out_send = remote(osend, orecv, osm.at[0], orm.at[0], sibling)
    out_send.start()
    sends.append(out_send)

    def side_by_side(get, at):
        for j in range(7):
            left = get(j)
            if j:
                left = pltpu.roll(left, 128 - 16 * j, 1)
            right = pltpu.roll(get(j + 1), HV - 16 * j, 1)
            tile = jnp.where(lane < HV - 16 * j, left, right).astype(BF16)
            mixed[:, pl.ds(pl.multiple_of(at + 128 * j, 128), 128)] = tile

    side_by_side(lambda i: numb[i, pl.ds(ours, TOK), :], half)

    loads[8].wait()

    @pl.when(jnp.logical_not(leads))
    def _():
        remote(dfin, dfin, des.at[0], der.at[0], sibling).wait_recv()

    full = jnp.dot(dfin[:, 0:ROWS], sel_v[...], precision=lax.Precision.HIGHEST, preferred_element_type=F32)
    dstate[...] = full[0:28, None, 0:EXPAND]
    to_sib_n.wait_recv()
    norms = nfull[...].reshape(HEADS, ROWS)
    full = jnp.dot(norms, sel_v[...], precision=lax.Precision.HIGHEST, preferred_element_type=F32)
    dnorm[...] = full[:, 0:EXPAND]

    out_send.wait_recv()
    side_by_side(lambda i: orecv[i].astype(F32), pl.multiple_of(COLS * (1 - c), 128))

    for copy in sends:
        copy.wait_send()

    @pl.when(sends_halo)
    def _():
        halo0.wait_send()
        halo1.wait_send()

    @pl.when(leads)
    def _():
        for copy in d_copies + e_copies:
            copy.wait_send()


def on_device(tokens_in, query_weight, key_weight, value_weight, conv_weight, prompt_lengths, decode_map):
    sel = jnp.asarray(selection())
    hbm = pl.BlockSpec(memory_space=pltpu.HBM)
    vmem = pl.BlockSpec(memory_space=pltpu.VMEM)
    smem = pl.BlockSpec(memory_space=pltpu.SMEM)
    dma = pltpu.SemaphoreType.DMA
    mixed, dstate, dnorm = pl.pallas_call(
        kernel,
        out_shape=(
            jax.ShapeDtypeStruct((TOK, D), BF16),
            jax.ShapeDtypeStruct((28, 1, EXPAND), F32),
            jax.ShapeDtypeStruct((HEADS, EXPAND), F32),
        ),
        in_specs=[hbm] * 5 + [smem] * 2 + [hbm],
        out_specs=(vmem, vmem, vmem),
        scratch_shapes=[
            pltpu.VMEM((CHIP + HALO, D), BF16),
            pltpu.VMEM((D, 256), BF16),
            pltpu.VMEM((D, COLS), BF16),
            pltpu.VMEM((CONV, COLS), F32),
            pltpu.VMEM((ROWS, 384), F32),
            pltpu.VMEM((CHIP, 256), F32),
            pltpu.VMEM((HALO + CHIP, COLS), F32),
            pltpu.VMEM((CHIP, COLS), F32),
            pltpu.VMEM((HALF, CHIP, LANES), BF16),
            pltpu.VMEM((HALF, 32, CHIP), F32),
            pltpu.VMEM((HALF, ROWS, CHIP), BF16),
            pltpu.VMEM((PARTS, HALF, CHIP, PART), BF16),
            pltpu.VMEM((LANES, CHIP), BF16),
            pltpu.VMEM((HALF, CHIP, LANES), F32),
            pltpu.VMEM((HALF, ROWS, LANES), BF16),
            pltpu.VMEM((ZS, ROWS, LANES), BF16),
            pltpu.VMEM((ROWS, LANES), BF16),
            pltpu.VMEM((YS, ROWS, LANES), BF16),
            pltpu.VMEM((ZS, ROWS, LANES), BF16),
            pltpu.VMEM((HALF, ROWS, LANES), BF16),
            pltpu.VMEM((ROWS, LANES), F32),
            pltpu.VMEM((LANES, 256), F32),
            pltpu.VMEM((XS, ROWS, LANES), F32),
            pltpu.VMEM((4, 32, 256), F32),
            pltpu.VMEM((32, 256), F32),
            pltpu.VMEM((HALF, ROWS), F32),
            pltpu.VMEM((YS, HALF, ROWS), F32),
            pltpu.VMEM((HALF, 256), F32),
            pltpu.VMEM((XS, HALF, 256), F32),
            pltpu.VMEM((HALF, 1, 256), F32),
            pltpu.VMEM((ZS, 1, 256), F32),
            pltpu.VMEM((1, 1, 256), F32),
            pltpu.VMEM((HALF, 1, 256), F32),
            pltpu.VMEM((HALF, ROWS), F32),
            pltpu.VMEM((2, HALF, ROWS), F32),
            pltpu.VMEM((HALF, TOK, LANES), BF16),
            pltpu.VMEM((HALF, TOK, LANES), BF16),
            dma((9,)),
            dma((3,)),
            dma((2,)),
            dma((PARTS, ZS)),
            dma((PARTS, ZS)),
            dma((PARTS, YS)),
            dma((PARTS, YS)),
            dma((PARTS, ZS)),
            dma((PARTS, ZS)),
            dma((PARTS, XS)),
            dma((PARTS, XS)),
            dma((4,)),
            dma((1,)),
            dma((YS,)),
            dma((YS,)),
            dma((XS,)),
            dma((XS,)),
            dma((ZS,)),
            dma((ZS,)),
            dma((ZS,)),
            dma((ZS,)),
            dma((1,)),
            dma((1,)),
            dma((1,)),
            dma((1,)),
        ],
        compiler_params=pltpu.CompilerParams(
            collective_id=0, has_side_effects=True, vmem_limit_bytes=40 * 1024 * 1024
        ),
        cost_estimate=pl.CostEstimate(flops=2_000_000_000, bytes_accessed=8_000_000, transcendentals=0),
        name="taylor_attention",
    )(*[pltpu.with_memory_space_constraint(a, pltpu.HBM) for a in (tokens_in[0], query_weight, key_weight, value_weight, conv_weight)], prompt_lengths, decode_map, pltpu.with_memory_space_constraint(sel, pltpu.HBM))
    return (mixed[None], jnp.transpose(dstate, (1, 2, 0)), jnp.transpose(dnorm)[None])


def solution(mesh):
    return jax.shard_map(
        on_device,
        mesh=mesh,
        in_specs=(P("req", "blk", None), P(), P(), P(), P(), P("req"), P("req")),
        out_specs=(P("req", "blk", None), P("req", None, "blk"), P("req", None, None)),
        check_vma=False,
    )
```

```python
import math

import jax
import jax.numpy as jnp
import numpy as np
from jax import lax
from jax.experimental import pallas as pl
from jax.experimental.pallas import tpu as pltpu
from jax.sharding import PartitionSpec as P

HEADS = 16
FEAT = 16
CONV = 3
D = 1792
HV = 112
EXPAND = 273
XS, YS, ZS = 4, 4, 8
HALF = HEADS // 2
COLS = HALF * HV
TOK = 128
CHIP = 2 * TOK
HALO = 8
ROWS = 160
LANES = 128
MESH = pl.DeviceIdType.MESH
VCHUNKS = ((0, 256), (256, 256), (512, 256), (768, 128))
FAR_FIRST = (4, 3, 5, 2, 6, 1, 7)
PARTS = 2
PART = ROWS // PARTS
F32 = jnp.float32
BF16 = jnp.bfloat16


def selection():
    sel = np.zeros((384, ROWS), np.float32)
    sel[0, 152] = 1.0
    for a in range(16):
        sel[1 + a, a] = 1.0
        for b in range(16):
            row = 17 + 16 * a + b
            r = (b - a) % 16
            if r == 0:
                sel[row, 16 + a] = 1.0
            elif r < 8:
                sel[row, 16 + 16 * r + a] = math.sqrt(0.5)
            elif r > 8:
                sel[row, 16 + 16 * (16 - r) + b] = math.sqrt(0.5)
            else:
                sel[row, 144 + min(a, b)] = math.sqrt(0.5)
    return sel.T.copy()


def features(heads_t, yy, extra):
    yy[:, 0:16, :] = heads_t
    yy[:, 16:32, :] = heads_t
    parts = [heads_t, heads_t * heads_t * math.sqrt(0.5)]
    for r in range(1, 8):
        parts.append(heads_t * yy[:, r : r + 16, :])
    parts.append(heads_t[:, 0:8] * heads_t[:, 8:16])
    row = lax.broadcasted_iota(jnp.int32, (HALF, 8, CHIP), 1)
    parts.append(jnp.where(row == 0, 1.0, 0.0).astype(F32))
    phi = jnp.concatenate(parts, 1)
    if extra is not None:
        phi = phi * extra
    return phi


def kernel(
    tok, wq, wk, wv, cw, plen, dmap, sel,
    mixed, dstate, dnorm,
    xs, wqk_v, wv_v, cw_v, sel_v,
    qkb, vbuf, cvb, vp, yy, phik, phiq, ktb, numb, gsend, gat, tsend, ty, psend, pbuf,
    wholeb, dt, dbuf, drt, dfin, nys, nyb, nxs, nxb, nzs, nzr_b, nzo, nzb, nss, nfull, osend, orecv,
    lsem, xsend, xrecv, gs, gr, ys, yr, ps, pr, dsm, dr, des, der,
    nysm, nyr, nxsm, nxr, nzsm, nzr, nbs, nbr, nps, npr, osm, orm,
):
    x = lax.axis_index("req")
    blk = lax.axis_index("blk")
    c = blk % 2
    chip = blk // 2
    z = chip % ZS
    y = chip // ZS

    def head_of(z_):
        return (z_ % 2) * 4 + z_ // 2

    mine = head_of(z)

    def dev(x_, y_, z_, c_):
        return ((y_ * ZS + z_) * 2 + c_, x_)

    nxt = (chip + 1) % (YS * ZS)
    prv = (chip + YS * ZS - 1) % (YS * ZS)
    sibling = dev(x, y, z, 1 - c)
    pair = z - z % 2
    lead = dev(x, y, pair + y % 2, y // 2)
    leads = (z % 2 == y % 2) & (c == y // 2)
    leads_int = leads.astype(jnp.int32)
    me4 = (z % 2) * 2 + c

    def remote(src, dst, send, recv, device):
        return pltpu.make_async_remote_copy(
            src_ref=src, dst_ref=dst, send_sem=send, recv_sem=recv, device_id=device, device_id_type=MESH
        )

    half = pl.multiple_of(COLS * c, 128)
    khalf = pl.multiple_of(128 * c, 128)
    loads = [
        pltpu.make_async_copy(tok, xs.at[0:TOK], lsem.at[0]),
        pltpu.make_async_copy(wk.at[:, pl.ds(khalf, 128)], wqk_v.at[:, 0:128], lsem.at[1]),
        pltpu.make_async_copy(wq.at[:, pl.ds(khalf, 128)], wqk_v.at[:, 128:256], lsem.at[2]),
        pltpu.make_async_copy(cw.at[:, pl.ds(half, COLS)], cw_v, lsem.at[3]),
    ]
    for n, (at, size) in enumerate(VCHUNKS):
        loads.append(
            pltpu.make_async_copy(
                wv.at[:, pl.ds(pl.multiple_of(half + at, 128), size)], wv_v.at[:, at : at + size], lsem.at[4 + n]
            )
        )
    loads.append(pltpu.make_async_copy(sel, sel_v, lsem.at[8]))
    for copy in loads:
        copy.start()

    barrier = pltpu.get_barrier_semaphore()

    def here_i_am(device):
        pl.semaphore_signal(barrier, inc=1, device_id=device, device_id_type=MESH)

    here_i_am(sibling)

    @pl.when(chip > 0)
    def _():
        here_i_am((prv * 2 + 1, x))

    for d in FAR_FIRST:
        here_i_am(dev(x, y, (z + d) % ZS, c))
    for d in range(1, YS):
        here_i_am(dev(x, (y + d) % YS, z, c))
    for d in range(1, XS):
        here_i_am(dev((x + d) % XS, y, z, c))

    @pl.when(jnp.logical_not(leads))
    def _():
        here_i_am(lead)

    last_not = (chip < YS * ZS - 1).astype(jnp.int32)
    pl.semaphore_wait(barrier, 1 + (ZS - 1) + (YS - 1) + (XS - 1) + 2 * c * last_not + 3 * leads_int)

    to_sib = remote(tok, xs.at[TOK:CHIP], xsend.at[0], xrecv.at[0], sibling)
    tail = tok.at[TOK - HALO : TOK]
    halo0 = remote(tail, xs.at[CHIP : CHIP + HALO], xsend.at[1], xrecv.at[1], (nxt * 2, x))
    halo1 = remote(tail, xs.at[CHIP : CHIP + HALO], xsend.at[2], xrecv.at[1], (nxt * 2 + 1, x))

    sends_halo = (c == 1) & (chip < YS * ZS - 1)

    @pl.when(sends_halo)
    def _():
        halo0.start()
        halo1.start()

    to_sib.start()

    @pl.when(chip == 0)
    def _():
        xs[CHIP:, :] = jnp.zeros((HALO, D), BF16)

    slot = dmap[0].astype(F32)
    length = plen[0]
    lane_tok = lax.broadcasted_iota(jnp.int32, (1, CHIP), 1) + chip * CHIP
    live_row = jnp.where(lane_tok < length, 1.0, 0.0).astype(F32)
    sub_tok = lax.broadcasted_iota(jnp.int32, (CHIP, 1), 0) + chip * CHIP
    live_col = jnp.where(sub_tok < length, 1.0, 0.0).astype(F32)
    lane = lax.broadcasted_iota(jnp.int32, (1, LANES), 1)

    ours = pl.multiple_of(TOK * c, TOK)
    theirs = pl.multiple_of(TOK * (1 - c), TOK)
    v_ours = pl.multiple_of(HALO + TOK * c, HALO)
    v_theirs = pl.multiple_of(HALO + TOK * (1 - c), HALO)
    for n in range(3):
        loads[n].wait()
    qkb[pl.ds(ours, TOK), :] = jnp.dot(xs[0:TOK, :], wqk_v[...], preferred_element_type=F32)
    for n, (at, size) in enumerate(VCHUNKS):
        loads[4 + n].wait()
        val = jnp.dot(xs[0:TOK, :], wv_v[:, at : at + size], preferred_element_type=F32)
        vbuf[pl.ds(v_ours, TOK), at : at + size] = val.astype(BF16).astype(F32)
    to_sib.wait_recv()
    qkb[pl.ds(theirs, TOK), :] = jnp.dot(xs[TOK:CHIP, :], wqk_v[...], preferred_element_type=F32)

    keys_t = qkb[:, 0:128].T
    ktb[...] = keys_t.astype(BF16)
    phi = features(keys_t.reshape(HALF, FEAT, CHIP) * 0.5, yy, live_row[None])
    phik[...] = phi.astype(BF16)

    @pl.when(chip > 0)
    def _():
        halo1.wait_recv()

    loads[3].wait()
    for n, (at, size) in enumerate(VCHUNKS):
        val = jnp.dot(xs[TOK:, :], wv_v[:, at : at + size], preferred_element_type=F32)
        val = val.astype(BF16).astype(F32)
        vbuf[pl.ds(v_theirs, TOK), at : at + size] = val[0:TOK]
        vbuf[0:HALO, at : at + size] = val[TOK:]
    for n, (at, size) in enumerate(VCHUNKS):
        conv = jnp.zeros((CHIP, size), F32)
        for tap in range(CONV):
            conv = conv + cw_v[tap : tap + 1, at : at + size] * vbuf[HALO - tap : HALO - tap + CHIP, at : at + size]
        cvb[:, at : at + size] = conv
    for i in range(HALF):
        tile, off = (HV * i) // 128, (HV * i) % 128
        width = 128 if off + HV <= 128 else 256
        wide = cvb[:, 128 * tile : 128 * tile + width]
        if off:
            wide = pltpu.roll(wide, width - off, 1)
        head = jnp.where(lane < HV, wide[:, 0:128], jnp.where(lane == HV, 1.0, 0.0))
        vp[i] = head.astype(BF16)

    sends = [to_sib]
    for n in range(PARTS):
        part = slice(n * PART, (n + 1) * PART)
        for i in range(HALF):
            gsend[i, part] = jnp.dot(phik[i, part], vp[i], preferred_element_type=F32).astype(BF16)
        for d in FAR_FIRST:
            zt = (z + d) % ZS
            i = head_of(zt)
            copy = remote(gsend.at[i, part], gat.at[z, part], gs.at[n, d], gr.at[n, z], dev(x, y, zt, c))
            copy.start()
            sends.append(copy)
        gat[z, part] = gsend[mine, part]

    here = x.astype(F32)
    wide = lax.broadcasted_iota(jnp.int32, (1, 256), 1)
    row8 = lax.broadcasted_iota(jnp.int32, (HALF, 1), 0)
    ones = jnp.ones((HALF, CHIP), BF16)
    sums = jnp.zeros((HALF, ROWS), F32)
    for i in range(HALF):
        head_sum = lax.dot_general(ones, phik[i], (((1,), (1,)), ((), ())), preferred_element_type=F32)
        sums = jnp.where(row8 == i, head_sum, sums)
    nys[...] = sums
    nyb[y] = sums
    for d in (2, 1, 3):
        copy = remote(nys, nyb.at[y], nysm.at[d], nyr.at[y], dev(x, (y + d) % YS, z, c))
        copy.start()
        sends.append(copy)

    queries = qkb[:, 128:256]
    phi_q = features((queries.T).reshape(HALF, FEAT, CHIP) * 0.5, yy, None)
    for i in range(HALF):
        for n in range(PARTS):
            phiq[n, i] = phi_q[i, n * PART : (n + 1) * PART].T.astype(BF16)
    row_t = lax.broadcasted_iota(jnp.int32, (CHIP, CHIP), 0)
    col_s = lax.broadcasted_iota(jnp.int32, (CHIP, CHIP), 1)
    causal = jnp.where(row_t >= col_s, 1.0, 0.0).astype(F32) * live_row
    for i in range(HALF):
        one_head = jnp.where(lane // FEAT == i, queries, 0.0).astype(BF16)
        dots = jnp.dot(one_head, ktb[...], preferred_element_type=F32) * 0.25
        weights = (1.0 + dots + 0.5 * dots * dots) * causal
        numb[i] = jnp.dot(weights.astype(BF16), vp[i], preferred_element_type=F32)

    for d in range(1, YS):
        yf = (y + d) % YS
        remote(nys, nyb.at[yf], nysm.at[d], nyr.at[yf], sibling).wait_recv()
    nxs[:, 0:ROWS] = nyb[0] + nyb[1] + nyb[2] + nyb[3]
    nxs[:, ROWS:] = jnp.zeros((HALF, 256 - ROWS), F32) + slot
    nxb[x] = nxs[...]
    for d in (2, 1, 3):
        copy = remote(nxs, nxb.at[x], nxsm.at[d], nxr.at[x], dev((x + d) % XS, y, z, c))
        copy.start()
        sends.append(copy)

    for n in range(PARTS):
        part = slice(n * PART, (n + 1) * PART)
        for d in FAR_FIRST:
            zf = (z + ZS - d) % ZS
            remote(gat.at[zf, part], gat.at[zf, part], gs.at[n, d], gr.at[n, zf], sibling).wait_recv()
        total = gat[0, part].astype(F32)
        for zz in range(1, ZS):
            total = total + gat[zz, part].astype(F32)
        tsend[part] = total.astype(BF16)
        for d in (2, 1, 3):
            copy = remote(
                tsend.at[part], ty.at[y, part], ys.at[n, d], yr.at[n, y], dev(x, (y + d) % YS, z, c)
            )
            copy.start()
            sends.append(copy)
        ty[y, part] = total.astype(BF16)

    for d in range(1, XS):
        xf = (x + d) % XS
        remote(nxs, nxb.at[xf], nxsm.at[d], nxr.at[xf], sibling).wait_recv()
    routed = jnp.zeros((HALF, 256), F32)
    for xf in range(XS):
        routed = routed + jnp.where(nxb[xf, :, 255:256] == here, nxb[xf], 0.0)
    for i in range(HALF):
        nzs[i] = routed[i : i + 1]
    for d in FAR_FIRST:
        zt = (z + d) % ZS
        copy = remote(nzs.at[head_of(zt)], nzr_b.at[z], nzsm.at[d], nzr.at[z], dev(x, y, zt, c))
        copy.start()
        sends.append(copy)
    nzr_b[z] = nzs[mine]

    d_copies, e_copies = [], []
    for n in range(PARTS):
        part = slice(n * PART, (n + 1) * PART)
        for d in (2, 1, 3):
            yf = (y + YS - d) % YS
            remote(tsend.at[part], ty.at[yf, part], ys.at[n, d], yr.at[n, yf], sibling).wait_recv()
        before = jnp.zeros((PART, LANES), F32)
        whole = jnp.zeros((PART, LANES), F32)
        for yf in range(YS):
            piece = ty[yf, part].astype(F32)
            whole = whole + piece
            before = before + piece * (yf < y).astype(F32)
        wholeb[part] = jnp.where(lane == LANES - 1, slot, whole)
        for zz in range(ZS):
            psend[zz, part] = before.astype(BF16)
            before = before + gat[zz, part].astype(F32)
        d_part = [
            remote(wholeb.at[part], dbuf.at[x, part], dsm.at[n, d], dr.at[n, x], dev((x + d) % XS, y, z, c))
            for d in (2, 1, 3)
        ]

        @pl.when(leads)
        def _():
            for copy in d_part:
                copy.start()
            dbuf[x, part] = wholeb[part]

        d_copies += d_part
        for d in FAR_FIRST:
            zt = (z + d) % ZS
            copy = remote(psend.at[zt, part], pbuf.at[mine, part], ps.at[n, d], pr.at[n, mine], dev(x, y, zt, c))
            copy.start()
            sends.append(copy)
        pbuf[mine, part] = psend[z, part]

    for d in FAR_FIRST:
        zf = (z + ZS - d) % ZS
        remote(nzs.at[0], nzr_b.at[zf], nzsm.at[d], nzr.at[zf], sibling).wait_recv()
    whole_norm = nzr_b[0]
    for zz in range(1, ZS):
        whole_norm = whole_norm + nzr_b[zz]
    nzo[0] = whole_norm
    nzb[mine] = whole_norm
    for d in FAR_FIRST:
        copy = remote(nzo.at[0], nzb.at[mine], nbs.at[d], nbr.at[mine], dev(x, y, (z + d) % ZS, c))
        copy.start()
        sends.append(copy)

    for n in range(PARTS - 1):
        part = slice(n * PART, (n + 1) * PART)
        numb[mine] = numb[mine] + jnp.dot(phiq[n, mine], pbuf[mine, part], preferred_element_type=F32)
        for d in FAR_FIRST:
            i = head_of((z + ZS - d) % ZS)
            remote(pbuf.at[i, part], pbuf.at[i, part], ps.at[n, d], pr.at[n, i], sibling).wait_recv()
            numb[i] = numb[i] + jnp.dot(phiq[n, i], pbuf[i, part], preferred_element_type=F32)

    for d in range(1, 4):
        member = (me4 + d) % 4
        e_copies.append(
            remote(drt.at[member], dfin, des.at[d], der.at[0], dev(x, y, pair + member // 2, member % 2))
        )

    @pl.when(leads)
    def _():
        for n in range(PARTS):
            part = slice(n * PART, (n + 1) * PART)
            for d in range(1, XS):
                xf = (x + d) % XS
                remote(wholeb.at[part], dbuf.at[xf, part], dsm.at[n, d], dr.at[n, xf], sibling).wait_recv()
        state = jnp.zeros((ROWS, LANES), F32)
        for xf in range(XS):
            state = state + jnp.where(dbuf[xf, :, LANES - 1 :] == here, dbuf[xf], 0.0)
        dt[...] = jnp.concatenate([state, jnp.zeros((256 - ROWS, LANES), F32)], 0).T
        for sub in range(4):
            drt[sub] = dt[28 * sub : 28 * sub + 32, :]
        for copy in e_copies:
            copy.start()
        dfin[...] = drt[me4]

    last = slice((PARTS - 1) * PART, ROWS)

    for d in FAR_FIRST:
        i = head_of((z + ZS - d) % ZS)
        remote(nzo.at[0], nzb.at[i], nbs.at[d], nbr.at[i], sibling).wait_recv()
    nss[...] = jnp.concatenate([nzb[i, :, 0:ROWS] for i in range(HALF)], 0)
    nfull[c] = nss[...]
    to_sib_n = remote(nss, nfull.at[c], nps.at[0], npr.at[0], sibling)
    to_sib_n.start()
    sends.append(to_sib_n)

    for d in FAR_FIRST:
        i = head_of((z + ZS - d) % ZS)
        remote(pbuf.at[i, last], pbuf.at[i, last], ps.at[PARTS - 1, d], pr.at[PARTS - 1, i], sibling).wait_recv()
    for i in range(HALF):
        num = numb[i] + jnp.dot(phiq[PARTS - 1, i], pbuf[i, last], preferred_element_type=F32)
        den = num[:, HV : HV + 1] + (1.0 - live_col)
        numb[i] = num * (live_col / den)
        osend[i] = numb[i, pl.ds(theirs, TOK), :].astype(BF16)
    out_send = remote(osend, orecv, osm.at[0], orm.at[0], sibling)
    out_send.start()
    sends.append(out_send)

    def side_by_side(get, at):
        for j in range(7):
            left = get(j)
            if j:
                left = pltpu.roll(left, 128 - 16 * j, 1)
            right = pltpu.roll(get(j + 1), HV - 16 * j, 1)
            tile = jnp.where(lane < HV - 16 * j, left, right).astype(BF16)
            mixed[:, pl.ds(pl.multiple_of(at + 128 * j, 128), 128)] = tile

    side_by_side(lambda i: numb[i, pl.ds(ours, TOK), :], half)

    loads[8].wait()

    @pl.when(jnp.logical_not(leads))
    def _():
        remote(dfin, dfin, des.at[0], der.at[0], sibling).wait_recv()

    full = jnp.dot(dfin[:, 0:ROWS], sel_v[...], precision=lax.Precision.HIGHEST, preferred_element_type=F32)
    dstate[...] = full[0:28, None, 0:EXPAND]
    to_sib_n.wait_recv()
    norms = nfull[...].reshape(HEADS, ROWS)
    full = jnp.dot(norms, sel_v[...], precision=lax.Precision.HIGHEST, preferred_element_type=F32)
    dnorm[...] = full[:, 0:EXPAND]

    out_send.wait_recv()
    side_by_side(lambda i: orecv[i].astype(F32), pl.multiple_of(COLS * (1 - c), 128))

    for copy in sends:
        copy.wait_send()

    @pl.when(sends_halo)
    def _():
        halo0.wait_send()
        halo1.wait_send()

    @pl.when(leads)
    def _():
        for copy in d_copies + e_copies:
            copy.wait_send()


def on_device(tokens_in, query_weight, key_weight, value_weight, conv_weight, prompt_lengths, decode_map):
    sel = jnp.asarray(selection())
    hbm = pl.BlockSpec(memory_space=pltpu.HBM)
    vmem = pl.BlockSpec(memory_space=pltpu.VMEM)
    smem = pl.BlockSpec(memory_space=pltpu.SMEM)
    dma = pltpu.SemaphoreType.DMA
    mixed, dstate, dnorm = pl.pallas_call(
        kernel,
        out_shape=(
            jax.ShapeDtypeStruct((TOK, D), BF16),
            jax.ShapeDtypeStruct((28, 1, EXPAND), F32),
            jax.ShapeDtypeStruct((HEADS, EXPAND), F32),
        ),
        in_specs=[hbm] * 5 + [smem] * 2 + [hbm],
        out_specs=(vmem, vmem, vmem),
        scratch_shapes=[
            pltpu.VMEM((CHIP + HALO, D), BF16),
            pltpu.VMEM((D, 256), BF16),
            pltpu.VMEM((D, COLS), BF16),
            pltpu.VMEM((CONV, COLS), F32),
            pltpu.VMEM((ROWS, 384), F32),
            pltpu.VMEM((CHIP, 256), F32),
            pltpu.VMEM((HALO + CHIP, COLS), F32),
            pltpu.VMEM((CHIP, COLS), F32),
            pltpu.VMEM((HALF, CHIP, LANES), BF16),
            pltpu.VMEM((HALF, 32, CHIP), F32),
            pltpu.VMEM((HALF, ROWS, CHIP), BF16),
            pltpu.VMEM((PARTS, HALF, CHIP, PART), BF16),
            pltpu.VMEM((LANES, CHIP), BF16),
            pltpu.VMEM((HALF, CHIP, LANES), F32),
            pltpu.VMEM((HALF, ROWS, LANES), BF16),
            pltpu.VMEM((ZS, ROWS, LANES), BF16),
            pltpu.VMEM((ROWS, LANES), BF16),
            pltpu.VMEM((YS, ROWS, LANES), BF16),
            pltpu.VMEM((ZS, ROWS, LANES), BF16),
            pltpu.VMEM((HALF, ROWS, LANES), BF16),
            pltpu.VMEM((ROWS, LANES), F32),
            pltpu.VMEM((LANES, 256), F32),
            pltpu.VMEM((XS, ROWS, LANES), F32),
            pltpu.VMEM((4, 32, 256), F32),
            pltpu.VMEM((32, 256), F32),
            pltpu.VMEM((HALF, ROWS), F32),
            pltpu.VMEM((YS, HALF, ROWS), F32),
            pltpu.VMEM((HALF, 256), F32),
            pltpu.VMEM((XS, HALF, 256), F32),
            pltpu.VMEM((HALF, 1, 256), F32),
            pltpu.VMEM((ZS, 1, 256), F32),
            pltpu.VMEM((1, 1, 256), F32),
            pltpu.VMEM((HALF, 1, 256), F32),
            pltpu.VMEM((HALF, ROWS), F32),
            pltpu.VMEM((2, HALF, ROWS), F32),
            pltpu.VMEM((HALF, TOK, LANES), BF16),
            pltpu.VMEM((HALF, TOK, LANES), BF16),
            dma((9,)),
            dma((3,)),
            dma((2,)),
            dma((PARTS, ZS)),
            dma((PARTS, ZS)),
            dma((PARTS, YS)),
            dma((PARTS, YS)),
            dma((PARTS, ZS)),
            dma((PARTS, ZS)),
            dma((PARTS, XS)),
            dma((PARTS, XS)),
            dma((4,)),
            dma((1,)),
            dma((YS,)),
            dma((YS,)),
            dma((XS,)),
            dma((XS,)),
            dma((ZS,)),
            dma((ZS,)),
            dma((ZS,)),
            dma((ZS,)),
            dma((1,)),
            dma((1,)),
            dma((1,)),
            dma((1,)),
        ],
        compiler_params=pltpu.CompilerParams(
            collective_id=0, has_side_effects=True, vmem_limit_bytes=40 * 1024 * 1024
        ),
        cost_estimate=pl.CostEstimate(flops=2_000_000_000, bytes_accessed=8_000_000, transcendentals=0),
        name="taylor_attention",
    )(*[pltpu.with_memory_space_constraint(a, pltpu.HBM) for a in (tokens_in[0], query_weight, key_weight, value_weight, conv_weight)], prompt_lengths, decode_map, pltpu.with_memory_space_constraint(sel, pltpu.HBM))
    return (mixed[None], jnp.transpose(dstate, (1, 2, 0)), jnp.transpose(dnorm)[None])


def solution(mesh):
    return jax.shard_map(
        on_device,
        mesh=mesh,
        in_specs=(P("req", "blk", None), P(), P(), P(), P(), P("req"), P("req")),
        out_specs=(P("req", "blk", None), P("req", None, "blk"), P("req", None, None)),
        check_vma=False,
    )
```

```python
import math

import jax
import jax.numpy as jnp
import numpy as np
from jax import lax
from jax.experimental import pallas as pl
from jax.experimental.pallas import tpu as pltpu
from jax.sharding import PartitionSpec as P

HEADS = 16
FEAT = 16
CONV = 3
D = 1792
HV = 112
EXPAND = 273
XS, YS, ZS = 4, 4, 8
HALF = HEADS // 2
COLS = HALF * HV
TOK = 128
CHIP = 2 * TOK
HALO = 8
ROWS = 160
LANES = 128
MESH = pl.DeviceIdType.MESH
VCHUNKS = ((0, 256), (256, 256), (512, 256), (768, 128))
FAR_FIRST = (4, 3, 5, 2, 6, 1, 7)
PARTS = 2
TILE = 144
PART_ROWS = (slice(0, 80), slice(80, TILE))
PART_SIZE = (80, TILE - 80)
F32 = jnp.float32
BF16 = jnp.bfloat16


def selection():
    sel = np.zeros((384, ROWS), np.float32)
    sel[0, 136] = 1.0
    for a in range(16):
        sel[1 + a, 144 + a if a < 15 else 137] = 1.0
        for b in range(16):
            row = 17 + 16 * a + b
            r = (b - a) % 16
            if r == 0:
                sel[row, a] = 1.0
            elif r < 8:
                sel[row, 16 * r + a] = math.sqrt(0.5)
            elif r > 8:
                sel[row, 16 * (16 - r) + b] = math.sqrt(0.5)
            else:
                sel[row, 128 + min(a, b)] = math.sqrt(0.5)
    return sel.T.copy()


def features(heads_t, yy, extra):
    yy[:, 0:16, :] = heads_t
    yy[:, 16:32, :] = heads_t
    parts = [heads_t * heads_t * math.sqrt(0.5)]
    for r in range(1, 8):
        parts.append(heads_t * yy[:, r : r + 16, :])
    parts.append(heads_t[:, 0:8] * heads_t[:, 8:16])
    row = lax.broadcasted_iota(jnp.int32, (HALF, 8, CHIP), 1)
    parts.append(jnp.where(row == 0, 1.0, jnp.where(row == 1, heads_t[:, 15:16], 0.0)).astype(F32))
    parts.append(heads_t)
    phi = jnp.concatenate(parts, 1)
    if extra is not None:
        phi = phi * extra
    return phi


def kernel(
    tok, wq, wk, wv, cw, plen, dmap, sel,
    mixed, dstate, dnorm,
    xs, wqk_v, wv_v, cw_v, sel_v,
    qkb, vbuf, cvb, vp, yy, phik, phiq, yqs, ktb, numb, stb, gsend, gat, tsend, ty, psend, pbuf,
    wholeb, dt, dbuf, drt, dfin, nys, nyb, nxs, nxb, nzs, nzr_b, nzo, nzb, nss, nfull, osend, orecv,
    lsem, xsend, xrecv, gs, gr, ys, yr, ps, pr, dsm, dr, des, der,
    nysm, nyr, nxsm, nxr, nzsm, nzr, nbs, nbr, nps, npr, osm, orm,
):
    x = lax.axis_index("req")
    blk = lax.axis_index("blk")
    c = blk % 2
    chip = blk // 2
    z = chip % ZS
    y = chip // ZS

    def head_of(z_):
        return (z_ % 2) * 4 + z_ // 2

    mine = head_of(z)

    def dev(x_, y_, z_, c_):
        return ((y_ * ZS + z_) * 2 + c_, x_)

    nxt = (chip + 1) % (YS * ZS)
    prv = (chip + YS * ZS - 1) % (YS * ZS)
    sibling = dev(x, y, z, 1 - c)
    pair = z - z % 2
    lead = dev(x, y, pair + y % 2, y // 2)
    leads = (z % 2 == y % 2) & (c == y // 2)
    leads_int = leads.astype(jnp.int32)
    me4 = (z % 2) * 2 + c

    def remote(src, dst, send, recv, device):
        return pltpu.make_async_remote_copy(
            src_ref=src, dst_ref=dst, send_sem=send, recv_sem=recv, device_id=device, device_id_type=MESH
        )

    half = pl.multiple_of(COLS * c, 128)
    khalf = pl.multiple_of(128 * c, 128)
    loads = [
        pltpu.make_async_copy(tok, xs.at[0:TOK], lsem.at[0]),
        pltpu.make_async_copy(wk.at[:, pl.ds(khalf, 128)], wqk_v.at[:, 0:128], lsem.at[1]),
        pltpu.make_async_copy(wq.at[:, pl.ds(khalf, 128)], wqk_v.at[:, 128:256], lsem.at[2]),
        pltpu.make_async_copy(cw.at[:, pl.ds(half, COLS)], cw_v, lsem.at[3]),
    ]
    for n, (at, size) in enumerate(VCHUNKS):
        loads.append(
            pltpu.make_async_copy(
                wv.at[:, pl.ds(pl.multiple_of(half + at, 128), size)], wv_v.at[:, at : at + size], lsem.at[4 + n]
            )
        )
    loads.append(pltpu.make_async_copy(sel, sel_v, lsem.at[8]))
    for copy in loads:
        copy.start()

    barrier = pltpu.get_barrier_semaphore()

    def here_i_am(device):
        pl.semaphore_signal(barrier, inc=1, device_id=device, device_id_type=MESH)

    here_i_am(sibling)

    @pl.when(chip > 0)
    def _():
        here_i_am((prv * 2 + 1, x))

    for d in FAR_FIRST:
        here_i_am(dev(x, y, (z + d) % ZS, c))
    for d in range(1, YS):
        here_i_am(dev(x, (y + d) % YS, z, c))
    for d in range(1, XS):
        here_i_am(dev((x + d) % XS, y, z, c))

    @pl.when(jnp.logical_not(leads))
    def _():
        here_i_am(lead)

    last_not = (chip < YS * ZS - 1).astype(jnp.int32)
    pl.semaphore_wait(barrier, 1 + (ZS - 1) + (YS - 1) + (XS - 1) + 2 * c * last_not + 3 * leads_int)

    to_sib = remote(tok, xs.at[TOK:CHIP], xsend.at[0], xrecv.at[0], sibling)
    tail = tok.at[TOK - HALO : TOK]
    halo0 = remote(tail, xs.at[CHIP : CHIP + HALO], xsend.at[1], xrecv.at[1], (nxt * 2, x))
    halo1 = remote(tail, xs.at[CHIP : CHIP + HALO], xsend.at[2], xrecv.at[1], (nxt * 2 + 1, x))

    sends_halo = (c == 1) & (chip < YS * ZS - 1)

    @pl.when(sends_halo)
    def _():
        halo0.start()
        halo1.start()

    to_sib.start()

    @pl.when(chip == 0)
    def _():
        xs[CHIP:, :] = jnp.zeros((HALO, D), BF16)

    slot = dmap[0].astype(F32)
    length = plen[0]
    lane_tok = lax.broadcasted_iota(jnp.int32, (1, CHIP), 1) + chip * CHIP
    live_row = jnp.where(lane_tok < length, 1.0, 0.0).astype(F32)
    sub_tok = lax.broadcasted_iota(jnp.int32, (CHIP, 1), 0) + chip * CHIP
    live_col = jnp.where(sub_tok < length, 1.0, 0.0).astype(F32)
    lane = lax.broadcasted_iota(jnp.int32, (1, LANES), 1)

    ours = pl.multiple_of(TOK * c, TOK)
    theirs = pl.multiple_of(TOK * (1 - c), TOK)
    v_ours = pl.multiple_of(HALO + TOK * c, HALO)
    v_theirs = pl.multiple_of(HALO + TOK * (1 - c), HALO)
    for n in range(3):
        loads[n].wait()
    qkb[pl.ds(ours, TOK), :] = jnp.dot(xs[0:TOK, :], wqk_v[...], preferred_element_type=F32)
    for n, (at, size) in enumerate(VCHUNKS):
        loads[4 + n].wait()
        val = jnp.dot(xs[0:TOK, :], wv_v[:, at : at + size], preferred_element_type=F32)
        vbuf[pl.ds(v_ours, TOK), at : at + size] = val.astype(BF16).astype(F32)
    to_sib.wait_recv()
    qkb[pl.ds(theirs, TOK), :] = jnp.dot(xs[TOK:CHIP, :], wqk_v[...], preferred_element_type=F32)

    keys_t = qkb[:, 0:128].T
    ktb[...] = keys_t.astype(BF16)
    phi = features(keys_t.reshape(HALF, FEAT, CHIP) * 0.5, yy, live_row[None])
    phik[...] = phi.astype(BF16)

    @pl.when(chip > 0)
    def _():
        halo1.wait_recv()

    loads[3].wait()
    for n, (at, size) in enumerate(VCHUNKS):
        val = jnp.dot(xs[TOK:, :], wv_v[:, at : at + size], preferred_element_type=F32)
        val = val.astype(BF16).astype(F32)
        vbuf[pl.ds(v_theirs, TOK), at : at + size] = val[0:TOK]
        vbuf[0:HALO, at : at + size] = val[TOK:]
    for n, (at, size) in enumerate(VCHUNKS):
        conv = jnp.zeros((CHIP, size), F32)
        for tap in range(CONV):
            conv = conv + cw_v[tap : tap + 1, at : at + size] * vbuf[HALO - tap : HALO - tap + CHIP, at : at + size]
        cvb[:, at : at + size] = conv
    for i in range(HALF):
        tile, off = (HV * i) // 128, (HV * i) % 128
        width = 128 if off + HV <= 128 else 256
        wide = cvb[:, 128 * tile : 128 * tile + width]
        if off:
            wide = pltpu.roll(wide, width - off, 1)
        head = jnp.where(lane < HV, wide[:, 0:128], jnp.where(lane == HV, 1.0, 0.0))
        vp[i] = head.astype(BF16)

    sends = [to_sib]
    linear = []
    for i in range(HALF):
        state = jnp.dot(phik[i], vp[i], preferred_element_type=F32)
        stb[i] = state[0:TILE]
        linear.append(state[TILE:])
    linear_t = jnp.concatenate(linear, 0).T
    for i in range(HALF):
        moved = pltpu.roll(linear_t, (HV + 1 - FEAT * i) % LANES, 1)
        gsend[i, 0:LANES] = jnp.where(lane > HV, moved, stb[i, 0:LANES]).astype(BF16)
        gsend[i, LANES:] = stb[i, LANES:].astype(BF16)
    for n in range(PARTS):
        part = PART_ROWS[n]
        for d in FAR_FIRST:
            zt = (z + d) % ZS
            i = head_of(zt)
            copy = remote(gsend.at[i, part], gat.at[z, part], gs.at[n, d], gr.at[n, z], dev(x, y, zt, c))
            copy.start()
            sends.append(copy)
        gat[z, part] = gsend[mine, part]

    here = x.astype(F32)
    wide = lax.broadcasted_iota(jnp.int32, (1, 256), 1)
    row8 = lax.broadcasted_iota(jnp.int32, (HALF, 1), 0)
    ones = jnp.ones((HALF, CHIP), BF16)
    sums = jnp.zeros((HALF, ROWS), F32)
    for i in range(HALF):
        head_sum = lax.dot_general(ones, phik[i], (((1,), (1,)), ((), ())), preferred_element_type=F32)
        sums = jnp.where(row8 == i, head_sum, sums)
    nys[...] = sums
    nyb[y] = sums
    for d in (2, 1, 3):
        copy = remote(nys, nyb.at[y], nysm.at[d], nyr.at[y], dev(x, (y + d) % YS, z, c))
        copy.start()
        sends.append(copy)

    queries = qkb[:, 128:256]
    phi_q = features((queries.T).reshape(HALF, FEAT, CHIP) * 0.5, yy, None)
    for i in range(HALF):
        for n in range(PARTS):
            phiq[n, i, :, 0 : PART_SIZE[n]] = phi_q[i, PART_ROWS[n]].T.astype(BF16)
        spread = pltpu.roll(queries, (HV + 1 - FEAT * i) % LANES, 1)
        yqs[i] = jnp.where(lane > HV, spread * 0.5, 0.0).astype(BF16)
    row_t = lax.broadcasted_iota(jnp.int32, (CHIP, CHIP), 0)
    col_s = lax.broadcasted_iota(jnp.int32, (CHIP, CHIP), 1)
    causal = jnp.where(row_t >= col_s, 1.0, 0.0).astype(F32) * live_row
    for i in range(HALF):
        one_head = jnp.where(lane // FEAT == i, queries, 0.0).astype(BF16)
        dots = jnp.dot(one_head, ktb[...], preferred_element_type=F32) * 0.25
        weights = (1.0 + dots + 0.5 * dots * dots) * causal
        numb[i] = jnp.dot(weights.astype(BF16), vp[i], preferred_element_type=F32)

    for d in range(1, YS):
        yf = (y + d) % YS
        remote(nys, nyb.at[yf], nysm.at[d], nyr.at[yf], sibling).wait_recv()
    nxs[:, 0:ROWS] = nyb[0] + nyb[1] + nyb[2] + nyb[3]
    nxs[:, ROWS:] = jnp.zeros((HALF, 256 - ROWS), F32) + slot
    nxb[x] = nxs[...]
    for d in (2, 1, 3):
        copy = remote(nxs, nxb.at[x], nxsm.at[d], nxr.at[x], dev((x + d) % XS, y, z, c))
        copy.start()
        sends.append(copy)

    for n in range(PARTS):
        part = PART_ROWS[n]
        for d in FAR_FIRST:
            zf = (z + ZS - d) % ZS
            remote(gat.at[zf, part], gat.at[zf, part], gs.at[n, d], gr.at[n, zf], sibling).wait_recv()
        total = gat[0, part].astype(F32)
        for zz in range(1, ZS):
            total = total + gat[zz, part].astype(F32)
        tsend[part] = total.astype(BF16)
        for d in (2, 1, 3):
            copy = remote(
                tsend.at[part], ty.at[y, part], ys.at[n, d], yr.at[n, y], dev(x, (y + d) % YS, z, c)
            )
            copy.start()
            sends.append(copy)
        ty[y, part] = total.astype(BF16)

    for d in range(1, XS):
        xf = (x + d) % XS
        remote(nxs, nxb.at[xf], nxsm.at[d], nxr.at[xf], sibling).wait_recv()
    routed = jnp.zeros((HALF, 256), F32)
    for xf in range(XS):
        routed = routed + jnp.where(nxb[xf, :, 255:256] == here, nxb[xf], 0.0)
    for i in range(HALF):
        nzs[i] = routed[i : i + 1]
    for d in FAR_FIRST:
        zt = (z + d) % ZS
        copy = remote(nzs.at[head_of(zt)], nzr_b.at[z], nzsm.at[d], nzr.at[z], dev(x, y, zt, c))
        copy.start()
        sends.append(copy)
    nzr_b[z] = nzs[mine]

    d_copies, e_copies = [], []
    for n in range(PARTS):
        part = PART_ROWS[n]
        for d in (2, 1, 3):
            yf = (y + YS - d) % YS
            remote(tsend.at[part], ty.at[yf, part], ys.at[n, d], yr.at[n, yf], sibling).wait_recv()
        before = jnp.zeros((PART_SIZE[n], LANES), F32)
        whole = jnp.zeros((PART_SIZE[n], LANES), F32)
        row_at = lax.broadcasted_iota(jnp.int32, (PART_SIZE[n], 1), 0) + part.start
        for yf in range(YS):
            piece = ty[yf, part].astype(F32)
            whole = whole + piece
            before = before + piece * (yf < y).astype(F32)
        wholeb[part] = jnp.where(row_at == TILE - 1, slot, whole)
        for zz in range(ZS):
            psend[zz, part] = before.astype(BF16)
            before = before + gat[zz, part].astype(F32)
        d_part = [
            remote(wholeb.at[part], dbuf.at[x, part], dsm.at[n, d], dr.at[n, x], dev((x + d) % XS, y, z, c))
            for d in (2, 1, 3)
        ]

        @pl.when(leads)
        def _():
            for copy in d_part:
                copy.start()
            dbuf[x, part] = wholeb[part]

        d_copies += d_part
        for d in FAR_FIRST:
            zt = (z + d) % ZS
            copy = remote(psend.at[zt, part], pbuf.at[mine, part], ps.at[n, d], pr.at[n, mine], dev(x, y, zt, c))
            copy.start()
            sends.append(copy)
        pbuf[mine, part] = psend[z, part]

    for d in FAR_FIRST:
        zf = (z + ZS - d) % ZS
        remote(nzs.at[0], nzr_b.at[zf], nzsm.at[d], nzr.at[zf], sibling).wait_recv()
    whole_norm = nzr_b[0]
    for zz in range(1, ZS):
        whole_norm = whole_norm + nzr_b[zz]
    nzo[0] = whole_norm
    nzb[mine] = whole_norm
    for d in FAR_FIRST:
        copy = remote(nzo.at[0], nzb.at[mine], nbs.at[d], nbr.at[mine], dev(x, y, (z + d) % ZS, c))
        copy.start()
        sends.append(copy)

    for n in range(PARTS - 1):
        part = PART_ROWS[n]
        size = PART_SIZE[n]
        numb[mine] = numb[mine] + jnp.dot(phiq[n, mine, :, 0:size], pbuf[mine, part], preferred_element_type=F32)
        for d in FAR_FIRST:
            i = head_of((z + ZS - d) % ZS)
            remote(pbuf.at[i, part], pbuf.at[i, part], ps.at[n, d], pr.at[n, i], sibling).wait_recv()
            numb[i] = numb[i] + jnp.dot(phiq[n, i, :, 0:size], pbuf[i, part], preferred_element_type=F32)

    for d in range(1, 4):
        member = (me4 + d) % 4
        e_copies.append(
            remote(drt.at[member], dfin, des.at[d], der.at[0], dev(x, y, pair + member // 2, member % 2))
        )

    @pl.when(leads)
    def _():
        for n in range(PARTS):
            part = PART_ROWS[n]
            for d in range(1, XS):
                xf = (x + d) % XS
                remote(wholeb.at[part], dbuf.at[xf, part], dsm.at[n, d], dr.at[n, xf], sibling).wait_recv()
        state = jnp.zeros((TILE, LANES), F32)
        for xf in range(XS):
            state = state + jnp.where(dbuf[xf, TILE - 1 :, :] == here, dbuf[xf], 0.0)
        turned = jnp.concatenate([state, jnp.zeros((256 - TILE, LANES), F32)], 0).T
        moved = pltpu.roll(state[0:LANES], 256 - LANES + TILE - LANES - HV - 1, 1)
        dt[:, 0:LANES] = turned[:, 0:LANES]
        spare = (lane >= TILE - LANES) & (lane < TILE - LANES + FEAT - 1)
        dt[:, LANES:] = jnp.where(spare, moved, turned[:, LANES:])
        for sub in range(4):
            drt[sub] = dt[28 * sub : 28 * sub + 32, :]
        for copy in e_copies:
            copy.start()
        dfin[...] = drt[me4]

    last = PART_ROWS[PARTS - 1]

    for d in FAR_FIRST:
        i = head_of((z + ZS - d) % ZS)
        remote(nzo.at[0], nzb.at[i], nbs.at[d], nbr.at[i], sibling).wait_recv()
    nss[...] = jnp.concatenate([nzb[i, :, 0:ROWS] for i in range(HALF)], 0)
    nfull[c] = nss[...]
    to_sib_n = remote(nss, nfull.at[c], nps.at[0], npr.at[0], sibling)
    to_sib_n.start()
    sends.append(to_sib_n)

    for d in FAR_FIRST:
        i = head_of((z + ZS - d) % ZS)
        remote(pbuf.at[i, last], pbuf.at[i, last], ps.at[PARTS - 1, d], pr.at[PARTS - 1, i], sibling).wait_recv()
    for i in range(HALF):
        num = numb[i] + jnp.dot(phiq[PARTS - 1, i, :, 0 : PART_SIZE[-1]], pbuf[i, last], preferred_element_type=F32)
        num = num + lax.dot_general(
            yqs[i], pbuf[i, 0:LANES], (((1,), (1,)), ((), ())), preferred_element_type=F32
        )
        den = num[:, HV : HV + 1] + (1.0 - live_col)
        numb[i] = num * (live_col / den)
        osend[i] = numb[i, pl.ds(theirs, TOK), :].astype(BF16)
    out_send = remote(osend, orecv, osm.at[0], orm.at[0], sibling)
    out_send.start()
    sends.append(out_send)

    def side_by_side(get, at):
        for j in range(7):
            left = get(j)
            if j:
                left = pltpu.roll(left, 128 - 16 * j, 1)
            right = pltpu.roll(get(j + 1), HV - 16 * j, 1)
            tile = jnp.where(lane < HV - 16 * j, left, right).astype(BF16)
            mixed[:, pl.ds(pl.multiple_of(at + 128 * j, 128), 128)] = tile

    side_by_side(lambda i: numb[i, pl.ds(ours, TOK), :], half)

    loads[8].wait()

    @pl.when(jnp.logical_not(leads))
    def _():
        remote(dfin, dfin, des.at[0], der.at[0], sibling).wait_recv()

    full = jnp.dot(dfin[:, 0:ROWS], sel_v[...], precision=lax.Precision.HIGHEST, preferred_element_type=F32)
    dstate[...] = full[0:28, None, 0:EXPAND]
    to_sib_n.wait_recv()
    norms = nfull[...].reshape(HEADS, ROWS)
    full = jnp.dot(norms, sel_v[...], precision=lax.Precision.HIGHEST, preferred_element_type=F32)
    dnorm[...] = full[:, 0:EXPAND]

    out_send.wait_recv()
    side_by_side(lambda i: orecv[i].astype(F32), pl.multiple_of(COLS * (1 - c), 128))

    for copy in sends:
        copy.wait_send()

    @pl.when(sends_halo)
    def _():
        halo0.wait_send()
        halo1.wait_send()

    @pl.when(leads)
    def _():
        for copy in d_copies + e_copies:
            copy.wait_send()


def on_device(tokens_in, query_weight, key_weight, value_weight, conv_weight, prompt_lengths, decode_map):
    sel = jnp.asarray(selection())
    hbm = pl.BlockSpec(memory_space=pltpu.HBM)
    vmem = pl.BlockSpec(memory_space=pltpu.VMEM)
    smem = pl.BlockSpec(memory_space=pltpu.SMEM)
    dma = pltpu.SemaphoreType.DMA
    mixed, dstate, dnorm = pl.pallas_call(
        kernel,
        out_shape=(
            jax.ShapeDtypeStruct((TOK, D), BF16),
            jax.ShapeDtypeStruct((28, 1, EXPAND), F32),
            jax.ShapeDtypeStruct((HEADS, EXPAND), F32),
        ),
        in_specs=[hbm] * 5 + [smem] * 2 + [hbm],
        out_specs=(vmem, vmem, vmem),
        scratch_shapes=[
            pltpu.VMEM((CHIP + HALO, D), BF16),
            pltpu.VMEM((D, 256), BF16),
            pltpu.VMEM((D, COLS), BF16),
            pltpu.VMEM((CONV, COLS), F32),
            pltpu.VMEM((ROWS, 384), F32),
            pltpu.VMEM((CHIP, 256), F32),
            pltpu.VMEM((HALO + CHIP, COLS), F32),
            pltpu.VMEM((CHIP, COLS), F32),
            pltpu.VMEM((HALF, CHIP, LANES), BF16),
            pltpu.VMEM((HALF, 32, CHIP), F32),
            pltpu.VMEM((HALF, ROWS, CHIP), BF16),
            pltpu.VMEM((PARTS, HALF, CHIP, PART_SIZE[0]), BF16),
            pltpu.VMEM((HALF, CHIP, LANES), BF16),
            pltpu.VMEM((LANES, CHIP), BF16),
            pltpu.VMEM((HALF, CHIP, LANES), F32),
            pltpu.VMEM((HALF, TILE, LANES), F32),
            pltpu.VMEM((HALF, TILE, LANES), BF16),
            pltpu.VMEM((ZS, TILE, LANES), BF16),
            pltpu.VMEM((TILE, LANES), BF16),
            pltpu.VMEM((YS, TILE, LANES), BF16),
            pltpu.VMEM((ZS, TILE, LANES), BF16),
            pltpu.VMEM((HALF, TILE, LANES), BF16),
            pltpu.VMEM((TILE, LANES), F32),
            pltpu.VMEM((LANES, 256), F32),
            pltpu.VMEM((XS, TILE, LANES), F32),
            pltpu.VMEM((4, 32, 256), F32),
            pltpu.VMEM((32, 256), F32),
            pltpu.VMEM((HALF, ROWS), F32),
            pltpu.VMEM((YS, HALF, ROWS), F32),
            pltpu.VMEM((HALF, 256), F32),
            pltpu.VMEM((XS, HALF, 256), F32),
            pltpu.VMEM((HALF, 1, 256), F32),
            pltpu.VMEM((ZS, 1, 256), F32),
            pltpu.VMEM((1, 1, 256), F32),
            pltpu.VMEM((HALF, 1, 256), F32),
            pltpu.VMEM((HALF, ROWS), F32),
            pltpu.VMEM((2, HALF, ROWS), F32),
            pltpu.VMEM((HALF, TOK, LANES), BF16),
            pltpu.VMEM((HALF, TOK, LANES), BF16),
            dma((9,)),
            dma((3,)),
            dma((2,)),
            dma((PARTS, ZS)),
            dma((PARTS, ZS)),
            dma((PARTS, YS)),
            dma((PARTS, YS)),
            dma((PARTS, ZS)),
            dma((PARTS, ZS)),
            dma((PARTS, XS)),
            dma((PARTS, XS)),
            dma((4,)),
            dma((1,)),
            dma((YS,)),
            dma((YS,)),
            dma((XS,)),
            dma((XS,)),
            dma((ZS,)),
            dma((ZS,)),
            dma((ZS,)),
            dma((ZS,)),
            dma((1,)),
            dma((1,)),
            dma((1,)),
            dma((1,)),
        ],
        compiler_params=pltpu.CompilerParams(
            collective_id=0, has_side_effects=True, vmem_limit_bytes=40 * 1024 * 1024
        ),
        cost_estimate=pl.CostEstimate(flops=2_000_000_000, bytes_accessed=8_000_000, transcendentals=0),
        name="taylor_attention",
    )(*[pltpu.with_memory_space_constraint(a, pltpu.HBM) for a in (tokens_in[0], query_weight, key_weight, value_weight, conv_weight)], prompt_lengths, decode_map, pltpu.with_memory_space_constraint(sel, pltpu.HBM))
    return (mixed[None], jnp.transpose(dstate, (1, 2, 0)), jnp.transpose(dnorm)[None])


def solution(mesh):
    return jax.shard_map(
        on_device,
        mesh=mesh,
        in_specs=(P("req", "blk", None), P(), P(), P(), P(), P("req"), P("req")),
        out_specs=(P("req", "blk", None), P("req", None, "blk"), P("req", None, None)),
        check_vma=False,
    )
```

```python
import math

import jax
import jax.numpy as jnp
import numpy as np
from jax import lax
from jax.experimental import pallas as pl
from jax.experimental.pallas import tpu as pltpu
from jax.sharding import PartitionSpec as P

HEADS = 16
FEAT = 16
CONV = 3
D = 1792
HV = 112
EXPAND = 273
XS, YS, ZS = 4, 4, 8
HALF = HEADS // 2
COLS = HALF * HV
TOK = 128
CHIP = 2 * TOK
HALO = 8
ROWS = 160
LANES = 128
MESH = pl.DeviceIdType.MESH
VCHUNKS = ((0, 256), (256, 256), (512, 256), (768, 128))
FAR_FIRST = (4, 3, 5, 2, 6, 1, 7)
PARTS = 2
TILE = 144
PART_ROWS = (slice(0, 80), slice(80, TILE))
PART_SIZE = (80, TILE - 80)
F32 = jnp.float32
BF16 = jnp.bfloat16


def selection():
    sel = np.zeros((384, ROWS), np.float32)
    sel[0, 136] = 1.0
    for a in range(16):
        sel[1 + a, 144 + a if a < 15 else 137] = 1.0
        for b in range(16):
            row = 17 + 16 * a + b
            r = (b - a) % 16
            if r == 0:
                sel[row, a] = 1.0
            elif r < 8:
                sel[row, 16 * r + a] = math.sqrt(0.5)
            elif r > 8:
                sel[row, 16 * (16 - r) + b] = math.sqrt(0.5)
            else:
                sel[row, 128 + min(a, b)] = math.sqrt(0.5)
    return sel.T.copy()


def features(heads_t, yy, extra):
    yy[:, 0:16, :] = heads_t
    yy[:, 16:32, :] = heads_t
    parts = [heads_t * heads_t * math.sqrt(0.5)]
    for r in range(1, 8):
        parts.append(heads_t * yy[:, r : r + 16, :])
    parts.append(heads_t[:, 0:8] * heads_t[:, 8:16])
    row = lax.broadcasted_iota(jnp.int32, (HALF, 8, CHIP), 1)
    parts.append(jnp.where(row == 0, 1.0, jnp.where(row == 1, heads_t[:, 15:16], 0.0)).astype(F32))
    parts.append(heads_t)
    phi = jnp.concatenate(parts, 1)
    if extra is not None:
        phi = phi * extra
    return phi


def kernel(
    tok, wq, wk, wv, cw, plen, dmap, sel,
    mixed, dstate, dnorm,
    xs, wqk_v, wv_v, cw_v, sel_v,
    qkb, vbuf, cvb, vp, yy, phik, phiq, yqs, ktb, numb, stb, gsend, gat, tsend, ty, psend, pbuf,
    wholeb, dt, dbuf, drt, dfin, nys, nyb, nxs, nxb, nzs, nzr_b, nzo, nzb, nss, nfull, osend, orecv,
    lsem, xsend, xrecv, gs, gr, ys, yr, ps, pr, dsm, dr, des, der,
    nysm, nyr, nxsm, nxr, nzsm, nzr, nbs, nbr, nps, npr, osm, orm,
):
    x = lax.axis_index("req")
    blk = lax.axis_index("blk")
    c = blk % 2
    chip = blk // 2
    z = chip % ZS
    y = chip // ZS

    def head_of(z_):
        return (z_ % 2) * 4 + z_ // 2

    mine = head_of(z)

    def dev(x_, y_, z_, c_):
        return ((y_ * ZS + z_) * 2 + c_, x_)

    nxt = (chip + 1) % (YS * ZS)
    prv = (chip + YS * ZS - 1) % (YS * ZS)
    sibling = dev(x, y, z, 1 - c)
    pair = z - z % 2
    lead = dev(x, y, pair + y % 2, y // 2)
    leads = (z % 2 == y % 2) & (c == y // 2)
    leads_int = leads.astype(jnp.int32)
    me4 = (z % 2) * 2 + c

    def remote(src, dst, send, recv, device):
        return pltpu.make_async_remote_copy(
            src_ref=src, dst_ref=dst, send_sem=send, recv_sem=recv, device_id=device, device_id_type=MESH
        )

    half = pl.multiple_of(COLS * c, 128)
    khalf = pl.multiple_of(128 * c, 128)
    loads = [
        pltpu.make_async_copy(tok, xs.at[0:TOK], lsem.at[0]),
        pltpu.make_async_copy(wk.at[:, pl.ds(khalf, 128)], wqk_v.at[:, 0:128], lsem.at[1]),
        pltpu.make_async_copy(wq.at[:, pl.ds(khalf, 128)], wqk_v.at[:, 128:256], lsem.at[2]),
        pltpu.make_async_copy(cw.at[:, pl.ds(half, COLS)], cw_v, lsem.at[3]),
    ]
    for n, (at, size) in enumerate(VCHUNKS):
        loads.append(
            pltpu.make_async_copy(
                wv.at[:, pl.ds(pl.multiple_of(half + at, 128), size)], wv_v.at[:, at : at + size], lsem.at[4 + n]
            )
        )
    loads.append(pltpu.make_async_copy(sel, sel_v, lsem.at[8]))
    for copy in loads:
        copy.start()

    barrier = pltpu.get_barrier_semaphore()

    def here_i_am(device):
        pl.semaphore_signal(barrier, inc=1, device_id=device, device_id_type=MESH)

    here_i_am(sibling)

    @pl.when(chip > 0)
    def _():
        here_i_am((prv * 2 + 1, x))

    for d in FAR_FIRST:
        here_i_am(dev(x, y, (z + d) % ZS, c))
    for d in range(1, YS):
        here_i_am(dev(x, (y + d) % YS, z, c))
    for d in range(1, XS):
        here_i_am(dev((x + d) % XS, y, z, c))

    @pl.when(jnp.logical_not(leads))
    def _():
        here_i_am(lead)

    last_not = (chip < YS * ZS - 1).astype(jnp.int32)
    pl.semaphore_wait(barrier, 1 + (ZS - 1) + (YS - 1) + (XS - 1) + 2 * c * last_not + 3 * leads_int)

    to_sib = remote(tok, xs.at[TOK:CHIP], xsend.at[0], xrecv.at[0], sibling)
    tail = tok.at[TOK - HALO : TOK]
    halo0 = remote(tail, xs.at[CHIP : CHIP + HALO], xsend.at[1], xrecv.at[1], (nxt * 2, x))
    halo1 = remote(tail, xs.at[CHIP : CHIP + HALO], xsend.at[2], xrecv.at[1], (nxt * 2 + 1, x))

    sends_halo = (c == 1) & (chip < YS * ZS - 1)

    @pl.when(sends_halo)
    def _():
        halo0.start()
        halo1.start()

    to_sib.start()

    @pl.when(chip == 0)
    def _():
        xs[CHIP:, :] = jnp.zeros((HALO, D), BF16)

    slot = dmap[0].astype(F32)
    length = plen[0]
    lane_tok = lax.broadcasted_iota(jnp.int32, (1, CHIP), 1) + chip * CHIP
    live_row = jnp.where(lane_tok < length, 1.0, 0.0).astype(F32)
    lane = lax.broadcasted_iota(jnp.int32, (1, LANES), 1)

    ours = pl.multiple_of(TOK * c, TOK)
    theirs = pl.multiple_of(TOK * (1 - c), TOK)
    v_ours = pl.multiple_of(HALO + TOK * c, HALO)
    v_theirs = pl.multiple_of(HALO + TOK * (1 - c), HALO)
    for n in range(3):
        loads[n].wait()
    qkb[pl.ds(ours, TOK), :] = jnp.dot(xs[0:TOK, :], wqk_v[...], preferred_element_type=F32)
    for n, (at, size) in enumerate(VCHUNKS):
        loads[4 + n].wait()
        val = jnp.dot(xs[0:TOK, :], wv_v[:, at : at + size], preferred_element_type=F32)
        vbuf[pl.ds(v_ours, TOK), at : at + size] = val.astype(BF16).astype(F32)
    to_sib.wait_recv()
    qkb[pl.ds(theirs, TOK), :] = jnp.dot(xs[TOK:CHIP, :], wqk_v[...], preferred_element_type=F32)

    keys_t = qkb[:, 0:128].T
    ktb[...] = keys_t.astype(BF16)
    phi = features(keys_t.reshape(HALF, FEAT, CHIP) * 0.5, yy, live_row[None])
    phik[...] = phi.astype(BF16)

    @pl.when(chip > 0)
    def _():
        halo1.wait_recv()

    loads[3].wait()
    for n, (at, size) in enumerate(VCHUNKS):
        val = jnp.dot(xs[TOK:, :], wv_v[:, at : at + size], preferred_element_type=F32)
        val = val.astype(BF16).astype(F32)
        vbuf[pl.ds(v_theirs, TOK), at : at + size] = val[0:TOK]
        vbuf[0:HALO, at : at + size] = val[TOK:]
    for n, (at, size) in enumerate(VCHUNKS):
        conv = jnp.zeros((CHIP, size), F32)
        for tap in range(CONV):
            conv = conv + cw_v[tap : tap + 1, at : at + size] * vbuf[HALO - tap : HALO - tap + CHIP, at : at + size]
        cvb[:, at : at + size] = conv
    for i in range(HALF):
        tile, off = (HV * i) // 128, (HV * i) % 128
        width = 128 if off + HV <= 128 else 256
        wide = cvb[:, 128 * tile : 128 * tile + width]
        if off:
            wide = pltpu.roll(wide, width - off, 1)
        head = jnp.where(lane < HV, wide[:, 0:128], jnp.where(lane == HV, 1.0, 0.0))
        vp[i] = head.astype(BF16)

    sends = [to_sib]
    linear = []
    for i in range(HALF):
        state = jnp.dot(phik[i], vp[i], preferred_element_type=F32)
        stb[i] = state[0:TILE]
        linear.append(state[TILE:])
    linear_t = jnp.concatenate(linear, 0).T
    for i in range(HALF):
        moved = pltpu.roll(linear_t, (HV + 1 - FEAT * i) % LANES, 1)
        gsend[i, 0:LANES] = jnp.where(lane > HV, moved, stb[i, 0:LANES]).astype(BF16)
        gsend[i, LANES:] = stb[i, LANES:].astype(BF16)
    for n in range(PARTS):
        part = PART_ROWS[n]
        for d in FAR_FIRST:
            zt = (z + d) % ZS
            i = head_of(zt)
            copy = remote(gsend.at[i, part], gat.at[z, part], gs.at[n, d], gr.at[n, z], dev(x, y, zt, c))
            copy.start()
            sends.append(copy)
        gat[z, part] = gsend[mine, part]

    here = x.astype(F32)
    wide = lax.broadcasted_iota(jnp.int32, (1, 256), 1)
    row8 = lax.broadcasted_iota(jnp.int32, (HALF, 1), 0)
    ones = jnp.ones((HALF, CHIP), BF16)
    sums = jnp.zeros((HALF, ROWS), F32)
    for i in range(HALF):
        head_sum = lax.dot_general(ones, phik[i], (((1,), (1,)), ((), ())), preferred_element_type=F32)
        sums = jnp.where(row8 == i, head_sum, sums)
    nys[...] = sums
    nyb[y] = sums
    for d in (2, 1, 3):
        copy = remote(nys, nyb.at[y], nysm.at[d], nyr.at[y], dev(x, (y + d) % YS, z, c))
        copy.start()
        sends.append(copy)

    queries = qkb[:, 128:256]
    phi_q = features((queries.T).reshape(HALF, FEAT, CHIP) * 0.5, yy, None)
    for i in range(HALF):
        for n in range(PARTS):
            phiq[n, i, :, 0 : PART_SIZE[n]] = phi_q[i, PART_ROWS[n]].T.astype(BF16)
        spread = pltpu.roll(queries, (HV + 1 - FEAT * i) % LANES, 1)
        yqs[i] = jnp.where(lane > HV, spread * 0.5, 0.0).astype(BF16)
    row_t = lax.broadcasted_iota(jnp.int32, (CHIP, CHIP), 0)
    col_s = lax.broadcasted_iota(jnp.int32, (CHIP, CHIP), 1)
    causal = jnp.where(row_t >= col_s, 1.0, 0.0).astype(F32) * live_row
    for i in range(HALF):
        one_head = jnp.where(lane // FEAT == i, queries, 0.0).astype(BF16)
        dots = jnp.dot(one_head, ktb[...], preferred_element_type=F32) * 0.25
        weights = (1.0 + dots + 0.5 * dots * dots) * causal
        numb[i] = jnp.dot(weights.astype(BF16), vp[i], preferred_element_type=F32)

    for d in range(1, YS):
        yf = (y + d) % YS
        remote(nys, nyb.at[yf], nysm.at[d], nyr.at[yf], sibling).wait_recv()
    nxs[:, 0:ROWS] = nyb[0] + nyb[1] + nyb[2] + nyb[3]
    nxs[:, ROWS:] = jnp.zeros((HALF, 256 - ROWS), F32) + slot
    nxb[x] = nxs[...]
    for d in (2, 1, 3):
        copy = remote(nxs, nxb.at[x], nxsm.at[d], nxr.at[x], dev((x + d) % XS, y, z, c))
        copy.start()
        sends.append(copy)

    for n in range(PARTS):
        part = PART_ROWS[n]
        for d in FAR_FIRST:
            zf = (z + ZS - d) % ZS
            remote(gat.at[zf, part], gat.at[zf, part], gs.at[n, d], gr.at[n, zf], sibling).wait_recv()
        total = gat[0, part].astype(F32)
        for zz in range(1, ZS):
            total = total + gat[zz, part].astype(F32)
        tsend[part] = total.astype(BF16)
        for d in (2, 1, 3):
            copy = remote(
                tsend.at[part], ty.at[y, part], ys.at[n, d], yr.at[n, y], dev(x, (y + d) % YS, z, c)
            )
            copy.start()
            sends.append(copy)
        ty[y, part] = total.astype(BF16)

    for d in range(1, XS):
        xf = (x + d) % XS
        remote(nxs, nxb.at[xf], nxsm.at[d], nxr.at[xf], sibling).wait_recv()
    routed = jnp.zeros((HALF, 256), F32)
    for xf in range(XS):
        routed = routed + jnp.where(nxb[xf, :, 255:256] == here, nxb[xf], 0.0)
    for i in range(HALF):
        nzs[i] = routed[i : i + 1]
    for d in FAR_FIRST:
        zt = (z + d) % ZS
        copy = remote(nzs.at[head_of(zt)], nzr_b.at[z], nzsm.at[d], nzr.at[z], dev(x, y, zt, c))
        copy.start()
        sends.append(copy)
    nzr_b[z] = nzs[mine]

    d_copies, e_copies = [], []
    for n in range(PARTS):
        part = PART_ROWS[n]
        for d in (2, 1, 3):
            yf = (y + YS - d) % YS
            remote(tsend.at[part], ty.at[yf, part], ys.at[n, d], yr.at[n, yf], sibling).wait_recv()
        before = jnp.zeros((PART_SIZE[n], LANES), F32)
        whole = jnp.zeros((PART_SIZE[n], LANES), F32)
        row_at = lax.broadcasted_iota(jnp.int32, (PART_SIZE[n], 1), 0) + part.start
        for yf in range(YS):
            piece = ty[yf, part].astype(F32)
            whole = whole + piece
            before = before + piece * (yf < y).astype(F32)
        wholeb[part] = jnp.where(row_at == TILE - 1, slot, whole)
        for zz in range(ZS):
            psend[zz, part] = before.astype(BF16)
            before = before + gat[zz, part].astype(F32)
        d_part = [
            remote(wholeb.at[part], dbuf.at[x, part], dsm.at[n, d], dr.at[n, x], dev((x + d) % XS, y, z, c))
            for d in (2, 1, 3)
        ]

        @pl.when(leads)
        def _():
            for copy in d_part:
                copy.start()
            dbuf[x, part] = wholeb[part]

        d_copies += d_part
        for d in FAR_FIRST:
            zt = (z + d) % ZS
            copy = remote(psend.at[zt, part], pbuf.at[mine, part], ps.at[n, d], pr.at[n, mine], dev(x, y, zt, c))
            copy.start()
            sends.append(copy)
        pbuf[mine, part] = psend[z, part]

    for d in FAR_FIRST:
        zf = (z + ZS - d) % ZS
        remote(nzs.at[0], nzr_b.at[zf], nzsm.at[d], nzr.at[zf], sibling).wait_recv()
    whole_norm = nzr_b[0]
    for zz in range(1, ZS):
        whole_norm = whole_norm + nzr_b[zz]
    nzo[0] = whole_norm
    nzb[mine] = whole_norm
    for d in FAR_FIRST:
        copy = remote(nzo.at[0], nzb.at[mine], nbs.at[d], nbr.at[mine], dev(x, y, (z + d) % ZS, c))
        copy.start()
        sends.append(copy)

    for d in range(1, 4):
        member = (me4 + d) % 4
        e_copies.append(
            remote(drt.at[member], dfin, des.at[d], der.at[0], dev(x, y, pair + member // 2, member % 2))
        )

    @pl.when(leads)
    def _():
        for n in range(PARTS):
            part = PART_ROWS[n]
            for d in range(1, XS):
                xf = (x + d) % XS
                remote(wholeb.at[part], dbuf.at[xf, part], dsm.at[n, d], dr.at[n, xf], sibling).wait_recv()
        state = jnp.zeros((TILE, LANES), F32)
        for xf in range(XS):
            state = state + jnp.where(dbuf[xf, TILE - 1 :, :] == here, dbuf[xf], 0.0)
        turned = jnp.concatenate([state, jnp.zeros((256 - TILE, LANES), F32)], 0).T
        moved = pltpu.roll(state[0:LANES], 256 - LANES + TILE - LANES - HV - 1, 1)
        dt[:, 0:LANES] = turned[:, 0:LANES]
        spare = (lane >= TILE - LANES) & (lane < TILE - LANES + FEAT - 1)
        dt[:, LANES:] = jnp.where(spare, moved, turned[:, LANES:])
        for sub in range(4):
            drt[sub] = dt[28 * sub : 28 * sub + 32, :]
        for copy in e_copies:
            copy.start()
        dfin[...] = drt[me4]

    for n in range(PARTS - 1):
        part = PART_ROWS[n]
        size = PART_SIZE[n]
        numb[mine] = numb[mine] + jnp.dot(phiq[n, mine, :, 0:size], pbuf[mine, part], preferred_element_type=F32)
        for d in FAR_FIRST:
            i = head_of((z + ZS - d) % ZS)
            remote(pbuf.at[i, part], pbuf.at[i, part], ps.at[n, d], pr.at[n, i], sibling).wait_recv()
            numb[i] = numb[i] + jnp.dot(phiq[n, i, :, 0:size], pbuf[i, part], preferred_element_type=F32)

    last = PART_ROWS[PARTS - 1]

    for d in FAR_FIRST:
        i = head_of((z + ZS - d) % ZS)
        remote(nzo.at[0], nzb.at[i], nbs.at[d], nbr.at[i], sibling).wait_recv()
    nss[...] = jnp.concatenate([nzb[i, :, 0:ROWS] for i in range(HALF)], 0)
    nfull[c] = nss[...]
    to_sib_n = remote(nss, nfull.at[c], nps.at[0], npr.at[0], sibling)
    to_sib_n.start()
    sends.append(to_sib_n)

    for d in FAR_FIRST:
        i = head_of((z + ZS - d) % ZS)
        remote(pbuf.at[i, last], pbuf.at[i, last], ps.at[PARTS - 1, d], pr.at[PARTS - 1, i], sibling).wait_recv()
    def finish(i, start):
        rows = pl.ds(start, TOK)
        at = lax.broadcasted_iota(jnp.int32, (TOK, 1), 0) + chip * CHIP + start
        alive = jnp.where(at < length, 1.0, 0.0).astype(F32)
        num = numb[i, rows, :] + jnp.dot(
            phiq[PARTS - 1, i, rows, 0 : PART_SIZE[-1]], pbuf[i, last], preferred_element_type=F32
        )
        num = num + lax.dot_general(
            yqs[i, rows, :], pbuf[i, 0:LANES], (((1,), (1,)), ((), ())), preferred_element_type=F32
        )
        den = num[:, HV : HV + 1] + (1.0 - alive)
        return num * (alive / den)

    for i in range(HALF):
        osend[i] = finish(i, theirs).astype(BF16)
    out_send = remote(osend, orecv, osm.at[0], orm.at[0], sibling)
    out_send.start()
    sends.append(out_send)
    for i in range(HALF):
        numb[i, pl.ds(ours, TOK), :] = finish(i, ours)

    def side_by_side(get, at):
        for j in range(7):
            left = get(j)
            if j:
                left = pltpu.roll(left, 128 - 16 * j, 1)
            right = pltpu.roll(get(j + 1), HV - 16 * j, 1)
            tile = jnp.where(lane < HV - 16 * j, left, right).astype(BF16)
            mixed[:, pl.ds(pl.multiple_of(at + 128 * j, 128), 128)] = tile

    side_by_side(lambda i: numb[i, pl.ds(ours, TOK), :], half)

    loads[8].wait()

    @pl.when(jnp.logical_not(leads))
    def _():
        remote(dfin, dfin, des.at[0], der.at[0], sibling).wait_recv()

    full = jnp.dot(dfin[:, 0:ROWS], sel_v[...], precision=lax.Precision.HIGHEST, preferred_element_type=F32)
    dstate[...] = full[0:28, None, 0:EXPAND]
    to_sib_n.wait_recv()
    norms = nfull[...].reshape(HEADS, ROWS)
    full = jnp.dot(norms, sel_v[...], precision=lax.Precision.HIGHEST, preferred_element_type=F32)
    dnorm[...] = full[:, 0:EXPAND]

    out_send.wait_recv()
    side_by_side(lambda i: orecv[i].astype(F32), pl.multiple_of(COLS * (1 - c), 128))

    for copy in sends:
        copy.wait_send()

    @pl.when(sends_halo)
    def _():
        halo0.wait_send()
        halo1.wait_send()

    @pl.when(leads)
    def _():
        for copy in d_copies + e_copies:
            copy.wait_send()


def on_device(tokens_in, query_weight, key_weight, value_weight, conv_weight, prompt_lengths, decode_map):
    sel = jnp.asarray(selection())
    hbm = pl.BlockSpec(memory_space=pltpu.HBM)
    vmem = pl.BlockSpec(memory_space=pltpu.VMEM)
    smem = pl.BlockSpec(memory_space=pltpu.SMEM)
    dma = pltpu.SemaphoreType.DMA
    mixed, dstate, dnorm = pl.pallas_call(
        kernel,
        out_shape=(
            jax.ShapeDtypeStruct((TOK, D), BF16),
            jax.ShapeDtypeStruct((28, 1, EXPAND), F32),
            jax.ShapeDtypeStruct((HEADS, EXPAND), F32),
        ),
        in_specs=[hbm] * 5 + [smem] * 2 + [hbm],
        out_specs=(vmem, vmem, vmem),
        scratch_shapes=[
            pltpu.VMEM((CHIP + HALO, D), BF16),
            pltpu.VMEM((D, 256), BF16),
            pltpu.VMEM((D, COLS), BF16),
            pltpu.VMEM((CONV, COLS), F32),
            pltpu.VMEM((ROWS, 384), F32),
            pltpu.VMEM((CHIP, 256), F32),
            pltpu.VMEM((HALO + CHIP, COLS), F32),
            pltpu.VMEM((CHIP, COLS), F32),
            pltpu.VMEM((HALF, CHIP, LANES), BF16),
            pltpu.VMEM((HALF, 32, CHIP), F32),
            pltpu.VMEM((HALF, ROWS, CHIP), BF16),
            pltpu.VMEM((PARTS, HALF, CHIP, PART_SIZE[0]), BF16),
            pltpu.VMEM((HALF, CHIP, LANES), BF16),
            pltpu.VMEM((LANES, CHIP), BF16),
            pltpu.VMEM((HALF, CHIP, LANES), F32),
            pltpu.VMEM((HALF, TILE, LANES), F32),
            pltpu.VMEM((HALF, TILE, LANES), BF16),
            pltpu.VMEM((ZS, TILE, LANES), BF16),
            pltpu.VMEM((TILE, LANES), BF16),
            pltpu.VMEM((YS, TILE, LANES), BF16),
            pltpu.VMEM((ZS, TILE, LANES), BF16),
            pltpu.VMEM((HALF, TILE, LANES), BF16),
            pltpu.VMEM((TILE, LANES), F32),
            pltpu.VMEM((LANES, 256), F32),
            pltpu.VMEM((XS, TILE, LANES), F32),
            pltpu.VMEM((4, 32, 256), F32),
            pltpu.VMEM((32, 256), F32),
            pltpu.VMEM((HALF, ROWS), F32),
            pltpu.VMEM((YS, HALF, ROWS), F32),
            pltpu.VMEM((HALF, 256), F32),
            pltpu.VMEM((XS, HALF, 256), F32),
            pltpu.VMEM((HALF, 1, 256), F32),
            pltpu.VMEM((ZS, 1, 256), F32),
            pltpu.VMEM((1, 1, 256), F32),
            pltpu.VMEM((HALF, 1, 256), F32),
            pltpu.VMEM((HALF, ROWS), F32),
            pltpu.VMEM((2, HALF, ROWS), F32),
            pltpu.VMEM((HALF, TOK, LANES), BF16),
            pltpu.VMEM((HALF, TOK, LANES), BF16),
            dma((9,)),
            dma((3,)),
            dma((2,)),
            dma((PARTS, ZS)),
            dma((PARTS, ZS)),
            dma((PARTS, YS)),
            dma((PARTS, YS)),
            dma((PARTS, ZS)),
            dma((PARTS, ZS)),
            dma((PARTS, XS)),
            dma((PARTS, XS)),
            dma((4,)),
            dma((1,)),
            dma((YS,)),
            dma((YS,)),
            dma((XS,)),
            dma((XS,)),
            dma((ZS,)),
            dma((ZS,)),
            dma((ZS,)),
            dma((ZS,)),
            dma((1,)),
            dma((1,)),
            dma((1,)),
            dma((1,)),
        ],
        compiler_params=pltpu.CompilerParams(
            collective_id=0, has_side_effects=True, vmem_limit_bytes=40 * 1024 * 1024
        ),
        cost_estimate=pl.CostEstimate(flops=2_000_000_000, bytes_accessed=8_000_000, transcendentals=0),
        name="taylor_attention",
    )(*[pltpu.with_memory_space_constraint(a, pltpu.HBM) for a in (tokens_in[0], query_weight, key_weight, value_weight, conv_weight)], prompt_lengths, decode_map, pltpu.with_memory_space_constraint(sel, pltpu.HBM))
    return (mixed[None], jnp.transpose(dstate, (1, 2, 0)), jnp.transpose(dnorm)[None])


def solution(mesh):
    return jax.shard_map(
        on_device,
        mesh=mesh,
        in_specs=(P("req", "blk", None), P(), P(), P(), P(), P("req"), P("req")),
        out_specs=(P("req", "blk", None), P("req", None, "blk"), P("req", None, None)),
        check_vma=False,
    )
```

```python
import math

import jax
import jax.numpy as jnp
import numpy as np
from jax import lax
from jax.experimental import pallas as pl
from jax.experimental.pallas import tpu as pltpu
from jax.sharding import PartitionSpec as P

HEADS = 16
FEAT = 16
CONV = 3
D = 1792
HV = 112
EXPAND = 273
XS, YS, ZS = 4, 4, 8
HALF = HEADS // 2
COLS = HALF * HV
TOK = 128
CHIP = 2 * TOK
HALO = 8
ROWS = 160
LANES = 128
MESH = pl.DeviceIdType.MESH
VCHUNKS = ((0, 256), (256, 256), (512, 256), (768, 128))
FAR_FIRST = (4, 3, 5, 2, 6, 1, 7)
PARTS = 2
TILE = 144
PART_ROWS = (slice(0, 64), slice(64, TILE))
PART_SIZE = (64, TILE - 64)
F32 = jnp.float32
BF16 = jnp.bfloat16


def selection():
    sel = np.zeros((384, ROWS), np.float32)
    sel[0, 136] = 1.0
    for a in range(16):
        sel[1 + a, 144 + a if a < 15 else 137] = 1.0
        for b in range(16):
            row = 17 + 16 * a + b
            r = (b - a) % 16
            if r == 0:
                sel[row, a] = 1.0
            elif r < 8:
                sel[row, 16 * r + a] = math.sqrt(0.5)
            elif r > 8:
                sel[row, 16 * (16 - r) + b] = math.sqrt(0.5)
            else:
                sel[row, 128 + min(a, b)] = math.sqrt(0.5)
    return sel.T.copy()


def features(heads_t, yy, extra):
    yy[:, 0:16, :] = heads_t
    yy[:, 16:32, :] = heads_t
    parts = [heads_t * heads_t * math.sqrt(0.5)]
    for r in range(1, 8):
        parts.append(heads_t * yy[:, r : r + 16, :])
    parts.append(heads_t[:, 0:8] * heads_t[:, 8:16])
    row = lax.broadcasted_iota(jnp.int32, (HALF, 8, CHIP), 1)
    parts.append(jnp.where(row == 0, 1.0, jnp.where(row == 1, heads_t[:, 15:16], 0.0)).astype(F32))
    parts.append(heads_t)
    phi = jnp.concatenate(parts, 1)
    if extra is not None:
        phi = phi * extra
    return phi


def kernel(
    tok, wq, wk, wv, cw, plen, dmap, sel,
    mixed, dstate, dnorm,
    xs, wqk_v, wv_v, cw_v, sel_v,
    qkb, vbuf, cvb, vp, yy, phik, phiq, yqs, ktb, numb, stb, gsend, gat, tsend, ty, psend, pbuf,
    wholeb, dt, dbuf, drt, dfin, nys, nyb, nxs, nxb, nzs, nzr_b, nzo, nzb, nss, nfull, osend, orecv,
    lsem, xsend, xrecv, gs, gr, ys, yr, ps, pr, dsm, dr, des, der,
    nysm, nyr, nxsm, nxr, nzsm, nzr, nbs, nbr, nps, npr, osm, orm,
):
    x = lax.axis_index("req")
    blk = lax.axis_index("blk")
    c = blk % 2
    chip = blk // 2
    z = chip % ZS
    y = chip // ZS

    def head_of(z_):
        return (z_ % 2) * 4 + z_ // 2

    mine = head_of(z)

    def dev(x_, y_, z_, c_):
        return ((y_ * ZS + z_) * 2 + c_, x_)

    nxt = (chip + 1) % (YS * ZS)
    prv = (chip + YS * ZS - 1) % (YS * ZS)
    sibling = dev(x, y, z, 1 - c)
    pair = z - z % 2
    lead = dev(x, y, pair + y % 2, y // 2)
    leads = (z % 2 == y % 2) & (c == y // 2)
    leads_int = leads.astype(jnp.int32)
    me4 = (z % 2) * 2 + c

    def remote(src, dst, send, recv, device):
        return pltpu.make_async_remote_copy(
            src_ref=src, dst_ref=dst, send_sem=send, recv_sem=recv, device_id=device, device_id_type=MESH
        )

    half = pl.multiple_of(COLS * c, 128)
    khalf = pl.multiple_of(128 * c, 128)
    loads = [
        pltpu.make_async_copy(tok, xs.at[0:TOK], lsem.at[0]),
        pltpu.make_async_copy(wk.at[:, pl.ds(khalf, 128)], wqk_v.at[:, 0:128], lsem.at[1]),
        pltpu.make_async_copy(wq.at[:, pl.ds(khalf, 128)], wqk_v.at[:, 128:256], lsem.at[2]),
        pltpu.make_async_copy(cw.at[:, pl.ds(half, COLS)], cw_v, lsem.at[3]),
    ]
    for n, (at, size) in enumerate(VCHUNKS):
        loads.append(
            pltpu.make_async_copy(
                wv.at[:, pl.ds(pl.multiple_of(half + at, 128), size)], wv_v.at[:, at : at + size], lsem.at[4 + n]
            )
        )
    loads.append(pltpu.make_async_copy(sel, sel_v, lsem.at[8]))
    for copy in loads:
        copy.start()

    barrier = pltpu.get_barrier_semaphore()

    def here_i_am(device):
        pl.semaphore_signal(barrier, inc=1, device_id=device, device_id_type=MESH)

    here_i_am(sibling)

    @pl.when(chip > 0)
    def _():
        here_i_am((prv * 2 + 1, x))

    for d in FAR_FIRST:
        here_i_am(dev(x, y, (z + d) % ZS, c))
    for d in range(1, YS):
        here_i_am(dev(x, (y + d) % YS, z, c))
    for d in range(1, XS):
        here_i_am(dev((x + d) % XS, y, z, c))

    @pl.when(jnp.logical_not(leads))
    def _():
        here_i_am(lead)

    last_not = (chip < YS * ZS - 1).astype(jnp.int32)
    pl.semaphore_wait(barrier, 1 + (ZS - 1) + (YS - 1) + (XS - 1) + 2 * c * last_not + 3 * leads_int)

    to_sib = remote(tok, xs.at[TOK:CHIP], xsend.at[0], xrecv.at[0], sibling)
    tail = tok.at[TOK - HALO : TOK]
    halo0 = remote(tail, xs.at[CHIP : CHIP + HALO], xsend.at[1], xrecv.at[1], (nxt * 2, x))
    halo1 = remote(tail, xs.at[CHIP : CHIP + HALO], xsend.at[2], xrecv.at[1], (nxt * 2 + 1, x))

    sends_halo = (c == 1) & (chip < YS * ZS - 1)

    @pl.when(sends_halo)
    def _():
        halo0.start()
        halo1.start()

    to_sib.start()

    @pl.when(chip == 0)
    def _():
        xs[CHIP:, :] = jnp.zeros((HALO, D), BF16)

    slot = dmap[0].astype(F32)
    length = plen[0]
    lane_tok = lax.broadcasted_iota(jnp.int32, (1, CHIP), 1) + chip * CHIP
    live_row = jnp.where(lane_tok < length, 1.0, 0.0).astype(F32)
    lane = lax.broadcasted_iota(jnp.int32, (1, LANES), 1)

    ours = pl.multiple_of(TOK * c, TOK)
    theirs = pl.multiple_of(TOK * (1 - c), TOK)
    v_ours = pl.multiple_of(HALO + TOK * c, HALO)
    v_theirs = pl.multiple_of(HALO + TOK * (1 - c), HALO)
    for n in range(3):
        loads[n].wait()
    qkb[pl.ds(ours, TOK), :] = jnp.dot(xs[0:TOK, :], wqk_v[...], preferred_element_type=F32)
    for n, (at, size) in enumerate(VCHUNKS):
        loads[4 + n].wait()
        val = jnp.dot(xs[0:TOK, :], wv_v[:, at : at + size], preferred_element_type=F32)
        vbuf[pl.ds(v_ours, TOK), at : at + size] = val.astype(BF16).astype(F32)
    to_sib.wait_recv()
    qkb[pl.ds(theirs, TOK), :] = jnp.dot(xs[TOK:CHIP, :], wqk_v[...], preferred_element_type=F32)

    keys_t = qkb[:, 0:128].T
    ktb[...] = keys_t.astype(BF16)
    phi = features(keys_t.reshape(HALF, FEAT, CHIP) * 0.5, yy, live_row[None])
    phik[...] = phi.astype(BF16)

    @pl.when(chip > 0)
    def _():
        halo1.wait_recv()

    loads[3].wait()
    for n, (at, size) in enumerate(VCHUNKS):
        val = jnp.dot(xs[TOK:, :], wv_v[:, at : at + size], preferred_element_type=F32)
        val = val.astype(BF16).astype(F32)
        vbuf[pl.ds(v_theirs, TOK), at : at + size] = val[0:TOK]
        vbuf[0:HALO, at : at + size] = val[TOK:]
    for n, (at, size) in enumerate(VCHUNKS):
        conv = jnp.zeros((CHIP, size), F32)
        for tap in range(CONV):
            conv = conv + cw_v[tap : tap + 1, at : at + size] * vbuf[HALO - tap : HALO - tap + CHIP, at : at + size]
        cvb[:, at : at + size] = conv
    for i in range(HALF):
        tile, off = (HV * i) // 128, (HV * i) % 128
        width = 128 if off + HV <= 128 else 256
        wide = cvb[:, 128 * tile : 128 * tile + width]
        if off:
            wide = pltpu.roll(wide, width - off, 1)
        head = jnp.where(lane < HV, wide[:, 0:128], jnp.where(lane == HV, 1.0, 0.0))
        vp[i] = head.astype(BF16)

    sends = [to_sib]
    linear = []
    for i in range(HALF):
        state = jnp.dot(phik[i], vp[i], preferred_element_type=F32)
        stb[i] = state[0:TILE]
        linear.append(state[TILE:])
    linear_t = jnp.concatenate(linear, 0).T
    for i in range(HALF):
        moved = pltpu.roll(linear_t, (HV + 1 - FEAT * i) % LANES, 1)
        gsend[i, 0:LANES] = jnp.where(lane > HV, moved, stb[i, 0:LANES]).astype(BF16)
        gsend[i, LANES:] = stb[i, LANES:].astype(BF16)
    for n in range(PARTS):
        part = PART_ROWS[n]
        for d in FAR_FIRST:
            zt = (z + d) % ZS
            i = head_of(zt)
            copy = remote(gsend.at[i, part], gat.at[z, part], gs.at[n, d], gr.at[n, z], dev(x, y, zt, c))
            copy.start()
            sends.append(copy)
        gat[z, part] = gsend[mine, part]

    here = x.astype(F32)
    wide = lax.broadcasted_iota(jnp.int32, (1, 256), 1)
    row8 = lax.broadcasted_iota(jnp.int32, (HALF, 1), 0)
    ones = jnp.ones((HALF, CHIP), BF16)
    sums = jnp.zeros((HALF, ROWS), F32)
    for i in range(HALF):
        head_sum = lax.dot_general(ones, phik[i], (((1,), (1,)), ((), ())), preferred_element_type=F32)
        sums = jnp.where(row8 == i, head_sum, sums)
    nys[...] = sums
    nyb[y] = sums
    for d in (2, 1, 3):
        copy = remote(nys, nyb.at[y], nysm.at[d], nyr.at[y], dev(x, (y + d) % YS, z, c))
        copy.start()
        sends.append(copy)

    queries = qkb[:, 128:256]
    phi_q = features((queries.T).reshape(HALF, FEAT, CHIP) * 0.5, yy, None)
    for i in range(HALF):
        for n in range(PARTS):
            phiq[n, i, :, 0 : PART_SIZE[n]] = phi_q[i, PART_ROWS[n]].T.astype(BF16)
        spread = pltpu.roll(queries, (HV + 1 - FEAT * i) % LANES, 1)
        yqs[i] = jnp.where(lane > HV, spread * 0.5, 0.0).astype(BF16)
    row_t = lax.broadcasted_iota(jnp.int32, (CHIP, CHIP), 0)
    col_s = lax.broadcasted_iota(jnp.int32, (CHIP, CHIP), 1)
    causal = jnp.where(row_t >= col_s, 1.0, 0.0).astype(F32) * live_row
    for i in range(HALF):
        one_head = jnp.where(lane // FEAT == i, queries, 0.0).astype(BF16)
        dots = jnp.dot(one_head, ktb[...], preferred_element_type=F32) * 0.25
        weights = (1.0 + dots + 0.5 * dots * dots) * causal
        numb[i] = jnp.dot(weights.astype(BF16), vp[i], preferred_element_type=F32)

    for d in range(1, YS):
        yf = (y + d) % YS
        remote(nys, nyb.at[yf], nysm.at[d], nyr.at[yf], sibling).wait_recv()
    nxs[:, 0:ROWS] = nyb[0] + nyb[1] + nyb[2] + nyb[3]
    nxs[:, ROWS:] = jnp.zeros((HALF, 256 - ROWS), F32) + slot
    nxb[x] = nxs[...]
    for d in (2, 1, 3):
        copy = remote(nxs, nxb.at[x], nxsm.at[d], nxr.at[x], dev((x + d) % XS, y, z, c))
        copy.start()
        sends.append(copy)

    for n in range(PARTS):
        part = PART_ROWS[n]
        for d in FAR_FIRST:
            zf = (z + ZS - d) % ZS
            remote(gat.at[zf, part], gat.at[zf, part], gs.at[n, d], gr.at[n, zf], sibling).wait_recv()
        total = gat[0, part].astype(F32)
        for zz in range(1, ZS):
            total = total + gat[zz, part].astype(F32)
        tsend[part] = total.astype(BF16)
        for d in (2, 1, 3):
            copy = remote(
                tsend.at[part], ty.at[y, part], ys.at[n, d], yr.at[n, y], dev(x, (y + d) % YS, z, c)
            )
            copy.start()
            sends.append(copy)
        ty[y, part] = total.astype(BF16)

    for d in range(1, XS):
        xf = (x + d) % XS
        remote(nxs, nxb.at[xf], nxsm.at[d], nxr.at[xf], sibling).wait_recv()
    routed = jnp.zeros((HALF, 256), F32)
    for xf in range(XS):
        routed = routed + jnp.where(nxb[xf, :, 255:256] == here, nxb[xf], 0.0)
    for i in range(HALF):
        nzs[i] = routed[i : i + 1]
    for d in FAR_FIRST:
        zt = (z + d) % ZS
        copy = remote(nzs.at[head_of(zt)], nzr_b.at[z], nzsm.at[d], nzr.at[z], dev(x, y, zt, c))
        copy.start()
        sends.append(copy)
    nzr_b[z] = nzs[mine]

    d_copies, e_copies = [], []
    for n in range(PARTS):
        part = PART_ROWS[n]
        for d in (2, 1, 3):
            yf = (y + YS - d) % YS
            remote(tsend.at[part], ty.at[yf, part], ys.at[n, d], yr.at[n, yf], sibling).wait_recv()
        before = jnp.zeros((PART_SIZE[n], LANES), F32)
        whole = jnp.zeros((PART_SIZE[n], LANES), F32)
        row_at = lax.broadcasted_iota(jnp.int32, (PART_SIZE[n], 1), 0) + part.start
        for yf in range(YS):
            piece = ty[yf, part].astype(F32)
            whole = whole + piece
            before = before + piece * (yf < y).astype(F32)
        wholeb[part] = jnp.where(row_at == TILE - 1, slot, whole)
        for zz in range(ZS):
            psend[zz, part] = before.astype(BF16)
            before = before + gat[zz, part].astype(F32)
        d_part = [
            remote(wholeb.at[part], dbuf.at[x, part], dsm.at[n, d], dr.at[n, x], dev((x + d) % XS, y, z, c))
            for d in (2, 1, 3)
        ]

        @pl.when(leads)
        def _():
            for copy in d_part:
                copy.start()
            dbuf[x, part] = wholeb[part]

        d_copies += d_part
        for d in FAR_FIRST:
            zt = (z + d) % ZS
            copy = remote(psend.at[zt, part], pbuf.at[mine, part], ps.at[n, d], pr.at[n, mine], dev(x, y, zt, c))
            copy.start()
            sends.append(copy)
        pbuf[mine, part] = psend[z, part]

    for d in FAR_FIRST:
        zf = (z + ZS - d) % ZS
        remote(nzs.at[0], nzr_b.at[zf], nzsm.at[d], nzr.at[zf], sibling).wait_recv()
    whole_norm = nzr_b[0]
    for zz in range(1, ZS):
        whole_norm = whole_norm + nzr_b[zz]
    nzo[0] = whole_norm
    nzb[mine] = whole_norm
    for d in FAR_FIRST:
        copy = remote(nzo.at[0], nzb.at[mine], nbs.at[d], nbr.at[mine], dev(x, y, (z + d) % ZS, c))
        copy.start()
        sends.append(copy)

    for d in range(1, 4):
        member = (me4 + d) % 4
        e_copies.append(
            remote(drt.at[member], dfin, des.at[d], der.at[0], dev(x, y, pair + member // 2, member % 2))
        )

    @pl.when(leads)
    def _():
        for n in range(PARTS):
            part = PART_ROWS[n]
            for d in range(1, XS):
                xf = (x + d) % XS
                remote(wholeb.at[part], dbuf.at[xf, part], dsm.at[n, d], dr.at[n, xf], sibling).wait_recv()
        state = jnp.zeros((TILE, LANES), F32)
        for xf in range(XS):
            state = state + jnp.where(dbuf[xf, TILE - 1 :, :] == here, dbuf[xf], 0.0)
        turned = jnp.concatenate([state, jnp.zeros((256 - TILE, LANES), F32)], 0).T
        moved = pltpu.roll(state[0:LANES], 256 - LANES + TILE - LANES - HV - 1, 1)
        dt[:, 0:LANES] = turned[:, 0:LANES]
        spare = (lane >= TILE - LANES) & (lane < TILE - LANES + FEAT - 1)
        dt[:, LANES:] = jnp.where(spare, moved, turned[:, LANES:])
        for sub in range(4):
            drt[sub] = dt[28 * sub : 28 * sub + 32, :]
        for copy in e_copies:
            copy.start()
        dfin[...] = drt[me4]

    for n in range(PARTS - 1):
        part = PART_ROWS[n]
        size = PART_SIZE[n]
        numb[mine] = numb[mine] + jnp.dot(phiq[n, mine, :, 0:size], pbuf[mine, part], preferred_element_type=F32)
        for d in FAR_FIRST:
            i = head_of((z + ZS - d) % ZS)
            remote(pbuf.at[i, part], pbuf.at[i, part], ps.at[n, d], pr.at[n, i], sibling).wait_recv()
            numb[i] = numb[i] + jnp.dot(phiq[n, i, :, 0:size], pbuf[i, part], preferred_element_type=F32)

    last = PART_ROWS[PARTS - 1]

    for d in FAR_FIRST:
        i = head_of((z + ZS - d) % ZS)
        remote(nzo.at[0], nzb.at[i], nbs.at[d], nbr.at[i], sibling).wait_recv()
    nss[...] = jnp.concatenate([nzb[i, :, 0:ROWS] for i in range(HALF)], 0)
    nfull[c] = nss[...]
    to_sib_n = remote(nss, nfull.at[c], nps.at[0], npr.at[0], sibling)
    to_sib_n.start()
    sends.append(to_sib_n)

    for d in FAR_FIRST:
        i = head_of((z + ZS - d) % ZS)
        remote(pbuf.at[i, last], pbuf.at[i, last], ps.at[PARTS - 1, d], pr.at[PARTS - 1, i], sibling).wait_recv()
    def finish(i, start):
        rows = pl.ds(start, TOK)
        at = lax.broadcasted_iota(jnp.int32, (TOK, 1), 0) + chip * CHIP + start
        alive = jnp.where(at < length, 1.0, 0.0).astype(F32)
        num = numb[i, rows, :] + jnp.dot(
            phiq[PARTS - 1, i, rows, 0 : PART_SIZE[-1]], pbuf[i, last], preferred_element_type=F32
        )
        num = num + lax.dot_general(
            yqs[i, rows, :], pbuf[i, 0:LANES], (((1,), (1,)), ((), ())), preferred_element_type=F32
        )
        den = num[:, HV : HV + 1] + (1.0 - alive)
        return num * (alive / den)

    for i in range(HALF):
        osend[i] = finish(i, theirs).astype(BF16)
    out_send = remote(osend, orecv, osm.at[0], orm.at[0], sibling)
    out_send.start()
    sends.append(out_send)
    for i in range(HALF):
        numb[i, pl.ds(ours, TOK), :] = finish(i, ours)

    def side_by_side(get, at):
        for j in range(7):
            left = get(j)
            if j:
                left = pltpu.roll(left, 128 - 16 * j, 1)
            right = pltpu.roll(get(j + 1), HV - 16 * j, 1)
            tile = jnp.where(lane < HV - 16 * j, left, right).astype(BF16)
            mixed[:, pl.ds(pl.multiple_of(at + 128 * j, 128), 128)] = tile

    side_by_side(lambda i: numb[i, pl.ds(ours, TOK), :], half)

    loads[8].wait()
    to_sib_n.wait_recv()
    norms = nfull[...].reshape(HEADS, ROWS)
    full = jnp.dot(norms, sel_v[...], precision=lax.Precision.HIGHEST, preferred_element_type=F32)
    dnorm[...] = full[:, 0:EXPAND]

    @pl.when(jnp.logical_not(leads))
    def _():
        remote(dfin, dfin, des.at[0], der.at[0], sibling).wait_recv()

    full = jnp.dot(dfin[:, 0:ROWS], sel_v[...], precision=lax.Precision.HIGHEST, preferred_element_type=F32)
    dstate[...] = full[0:28, None, 0:EXPAND]
    out_send.wait_recv()
    side_by_side(lambda i: orecv[i].astype(F32), pl.multiple_of(COLS * (1 - c), 128))

    for copy in sends:
        copy.wait_send()

    @pl.when(sends_halo)
    def _():
        halo0.wait_send()
        halo1.wait_send()

    @pl.when(leads)
    def _():
        for copy in d_copies + e_copies:
            copy.wait_send()


def on_device(tokens_in, query_weight, key_weight, value_weight, conv_weight, prompt_lengths, decode_map):
    sel = jnp.asarray(selection())
    hbm = pl.BlockSpec(memory_space=pltpu.HBM)
    vmem = pl.BlockSpec(memory_space=pltpu.VMEM)
    smem = pl.BlockSpec(memory_space=pltpu.SMEM)
    dma = pltpu.SemaphoreType.DMA
    mixed, dstate, dnorm = pl.pallas_call(
        kernel,
        out_shape=(
            jax.ShapeDtypeStruct((TOK, D), BF16),
            jax.ShapeDtypeStruct((28, 1, EXPAND), F32),
            jax.ShapeDtypeStruct((HEADS, EXPAND), F32),
        ),
        in_specs=[hbm] * 5 + [smem] * 2 + [hbm],
        out_specs=(vmem, vmem, vmem),
        scratch_shapes=[
            pltpu.VMEM((CHIP + HALO, D), BF16),
            pltpu.VMEM((D, 256), BF16),
            pltpu.VMEM((D, COLS), BF16),
            pltpu.VMEM((CONV, COLS), F32),
            pltpu.VMEM((ROWS, 384), F32),
            pltpu.VMEM((CHIP, 256), F32),
            pltpu.VMEM((HALO + CHIP, COLS), F32),
            pltpu.VMEM((CHIP, COLS), F32),
            pltpu.VMEM((HALF, CHIP, LANES), BF16),
            pltpu.VMEM((HALF, 32, CHIP), F32),
            pltpu.VMEM((HALF, ROWS, CHIP), BF16),
            pltpu.VMEM((PARTS, HALF, CHIP, PART_SIZE[1]), BF16),
            pltpu.VMEM((HALF, CHIP, LANES), BF16),
            pltpu.VMEM((LANES, CHIP), BF16),
            pltpu.VMEM((HALF, CHIP, LANES), F32),
            pltpu.VMEM((HALF, TILE, LANES), F32),
            pltpu.VMEM((HALF, TILE, LANES), BF16),
            pltpu.VMEM((ZS, TILE, LANES), BF16),
            pltpu.VMEM((TILE, LANES), BF16),
            pltpu.VMEM((YS, TILE, LANES), BF16),
            pltpu.VMEM((ZS, TILE, LANES), BF16),
            pltpu.VMEM((HALF, TILE, LANES), BF16),
            pltpu.VMEM((TILE, LANES), F32),
            pltpu.VMEM((LANES, 256), F32),
            pltpu.VMEM((XS, TILE, LANES), F32),
            pltpu.VMEM((4, 32, 256), F32),
            pltpu.VMEM((32, 256), F32),
            pltpu.VMEM((HALF, ROWS), F32),
            pltpu.VMEM((YS, HALF, ROWS), F32),
            pltpu.VMEM((HALF, 256), F32),
            pltpu.VMEM((XS, HALF, 256), F32),
            pltpu.VMEM((HALF, 1, 256), F32),
            pltpu.VMEM((ZS, 1, 256), F32),
            pltpu.VMEM((1, 1, 256), F32),
            pltpu.VMEM((HALF, 1, 256), F32),
            pltpu.VMEM((HALF, ROWS), F32),
            pltpu.VMEM((2, HALF, ROWS), F32),
            pltpu.VMEM((HALF, TOK, LANES), BF16),
            pltpu.VMEM((HALF, TOK, LANES), BF16),
            dma((9,)),
            dma((3,)),
            dma((2,)),
            dma((PARTS, ZS)),
            dma((PARTS, ZS)),
            dma((PARTS, YS)),
            dma((PARTS, YS)),
            dma((PARTS, ZS)),
            dma((PARTS, ZS)),
            dma((PARTS, XS)),
            dma((PARTS, XS)),
            dma((4,)),
            dma((1,)),
            dma((YS,)),
            dma((YS,)),
            dma((XS,)),
            dma((XS,)),
            dma((ZS,)),
            dma((ZS,)),
            dma((ZS,)),
            dma((ZS,)),
            dma((1,)),
            dma((1,)),
            dma((1,)),
            dma((1,)),
        ],
        compiler_params=pltpu.CompilerParams(
            collective_id=0, has_side_effects=True, vmem_limit_bytes=40 * 1024 * 1024
        ),
        cost_estimate=pl.CostEstimate(flops=2_000_000_000, bytes_accessed=8_000_000, transcendentals=0),
        name="taylor_attention",
    )(*[pltpu.with_memory_space_constraint(a, pltpu.HBM) for a in (tokens_in[0], query_weight, key_weight, value_weight, conv_weight)], prompt_lengths, decode_map, pltpu.with_memory_space_constraint(sel, pltpu.HBM))
    return (mixed[None], jnp.transpose(dstate, (1, 2, 0)), jnp.transpose(dnorm)[None])


def solution(mesh):
    return jax.shard_map(
        on_device,
        mesh=mesh,
        in_specs=(P("req", "blk", None), P(), P(), P(), P(), P("req"), P("req")),
        out_specs=(P("req", "blk", None), P("req", None, "blk"), P("req", None, None)),
        check_vma=False,
    )
```
